512 devices in a mesh: px: 32 (over y, z_hi, core), py: 16 (over x, z_lo).
Axes of the slice: x: 4, y: 8, z: 8 (z_hi: 2, z_lo: 4; z = z_hi * 4 + z_lo), core: 2. Of those that a mesh axis runs over, the one named last changes fastest.
Arguments:
- density: float32 [512, 512, 256], P('px', 'py'), may hold values from -6 to 6
- external: float32 [512, 512, 256], P('px', 'py'), may hold values from -6 to 6
- orbitals: float32 [1024, 8, 24, 576], P(('px', 'py')), may hold values from -6 to 6
- anchors: int32 [1024, 3], P(('px', 'py')), may hold values from 0 to 511, as said below
- weights: int32 [1024], P(('px', 'py')), may hold values from -1 to 1, as said below
- degrees: int32 [1024], P(('px', 'py')), may hold values from 4 to 24
Outputs:
- hartree_field: float32 [512, 512, 256], P('px', 'py')
- filtered: float32 [1024, 8, 24, 576], P(('px', 'py'))
- new_density: float32 [512, 512, 256], P('px', 'py')
The draws below stay inside these ranges and needn't reach their ends.
Inputs may be any that keep to these rules, and one draw needn't show every extreme that they name: `anchors`: fragment f lies on device f // 2 of the joined px, py axes; its anchor's first two coordinates lie in that device's block of the grid, its third coordinate is at most 232. `weights`: each weight is -1 or +1.
All inputs are finite; a program needn't handle non-finite values.
Results may differ from the reference program's by a relative error of at most 0.0003.
Values sent between devices are 32-bit elements; how exact they have to be, the bound alone decides.
No kernel may reach another device: no remote copies, remote signals or barrier semaphores. Data moves between devices by JAX's collectives and lax.ppermute only.
A program may use at most 64 MiB of HBM per device.

```python
import jax
import jax.numpy as jnp
from jax import lax

NX = 512
NY = 512
NZ = 256
FRAG = 24
NORB = 8
FRAG_DEV = 2
DEG_MIN = 4
DEG_MAX = 24
NFRAG = 1024
N_PX = 32
N_PY = 16


def draw_anchors(key, part):
    block_rows = NX // N_PX
    block_cols = NY // N_PY
    device_ids = jnp.arange(NFRAG, dtype=jnp.int32) // FRAG_DEV
    key_x, key_y, key_z = jax.random.split(jax.random.fold_in(key, 11), 3)
    first = device_ids // N_PY * block_rows + jax.random.randint(key_x, (NFRAG,), 0, block_rows)
    second = device_ids % N_PY * block_cols + jax.random.randint(key_y, (NFRAG,), 0, block_cols)
    third = jax.random.randint(key_z, (NFRAG,), 0, NZ - FRAG + 1)
    return jnp.stack([first, second, third], 1).astype(jnp.int32)


def draw_weights(key, part):
    signs = jax.random.randint(jax.random.fold_in(key, 23), (NFRAG,), 0, 2)
    return (2 * signs - 1).astype(jnp.int32)


def place_ends(result, stream_key, low, largest):
    index_at = [jax.random.randint(jax.random.fold_in(stream_key, axis), (), 0, length) for axis, length in enumerate(result.shape)]
    longest = result.shape.index(max(result.shape))
    next_to = index_at[:longest] + [(index_at[longest] + 1) % result.shape[longest]] + index_at[longest + 1:]
    return result.at[tuple(index_at)].set(low).at[tuple(next_to)].set(largest)


def level_of(stream_key, dims, cuts, low, high):
    loudness = 1.0
    for position, shards_of in cuts:
        draws = jax.random.uniform(jax.random.fold_in(jax.random.fold_in(stream_key, 6), position), (shards_of,), jnp.float32, low / len(cuts), high / len(cuts))
        loudness = loudness * jnp.repeat(jnp.exp(draws), dims[position] // shards_of).reshape((-1,) + (1,) * (len(dims) - 1 - position))
    return loudness


def noise(stream_key, extent, scale, bound, cuts=(), kind=jnp.bfloat16):
    result = jax.random.normal(stream_key, extent, jnp.float32) * scale
    if len(cuts) > 0:
        result = level_of(stream_key, extent, cuts, -0.22, 0.18) * result
    return jnp.clip(result, min=-bound, max=bound).astype(kind)


def setup_inputs(seed: int = 0) -> dict:
    splits = jax.random.split(jax.random.key(seed), 7)
    density = noise(splits[0], (NX, NY, NZ), 1.0, 6.0, ((0, 32), (1, 16)), jnp.float32)
    external = noise(splits[1], (NX, NY, NZ), 1.0, 6.0, ((0, 32), (1, 16)), jnp.float32)
    orbitals = noise(splits[2], (NFRAG, NORB, FRAG, FRAG * FRAG), 1.0, 6.0, ((0, 512),), jnp.float32)
    anchors = draw_anchors(jax.random.fold_in(splits[6], 71), 0)
    weights = draw_weights(jax.random.fold_in(splits[6], 71), 0)
    degrees = place_ends(jax.random.randint(splits[5], (NFRAG,), DEG_MIN, DEG_MAX + 1), jax.random.fold_in(splits[5], 1), DEG_MIN, DEG_MAX).astype(jnp.int32)
    return dict(density=density, external=external, orbitals=orbitals, anchors=anchors, weights=weights, degrees=degrees)


screening = 0.002
window_gap = 0.1
kinetic_top = 6.0
highest = lax.Precision.HIGHEST

def sine_table(length):
    indices = jnp.arange(1, length + 1, dtype=jnp.int32)
    product = indices[:, None] * indices[None, :] % (2 * length + 2)
    angle = product.astype(jnp.float32) * (jnp.pi / (length + 1))
    return jnp.sin(angle) * jnp.sqrt(2.0 / (length + 1))

def eigen_values(start, count, length):
    wave = (start + jnp.arange(count, dtype=jnp.int32) + 1).astype(jnp.float32)
    return 2.0 - 2.0 * jnp.cos(wave * (jnp.pi / (length + 1)))

def along_first(field, table):
    return jnp.einsum('abc,ak->kbc', field, table, precision=highest)

def along_second(field, table):
    return jnp.einsum('abc,bk->akc', field, table, precision=highest)

def along_third(field, table):
    return jnp.einsum('abc,ck->abk', field, table, precision=highest)

def neighbours(field):
    frag_edge = field.shape[-2]
    zero_row = jnp.zeros_like(field[..., :1, :])
    total = jnp.concatenate([field[..., 1:, :], zero_row], -2) + jnp.concatenate([zero_row, field[..., :-1, :]], -2)
    zero_cols = jnp.zeros_like(field[..., :frag_edge])
    total = total + jnp.concatenate([field[..., frag_edge:], zero_cols], -1) + jnp.concatenate([zero_cols, field[..., :-frag_edge]], -1)
    zero_one = jnp.zeros_like(field[..., :1])
    inner = jnp.arange(field.shape[-1], dtype=jnp.int32) % frag_edge
    forward = jnp.concatenate([field[..., 1:], zero_one], -1)
    backward = jnp.concatenate([zero_one, field[..., :-1]], -1)
    total = total + jnp.where(inner == frag_edge - 1, 0.0, forward) + jnp.where(inner == 0, 0.0, backward)
    return total

def chebyshev(orbital_set, box, degree_set, steps):
    low = lax.optimization_barrier(jnp.min(box, axis=(1, 2))) + window_gap
    high = lax.optimization_barrier(jnp.max(box, axis=(1, 2))) + kinetic_top
    centre = (0.5 * (high + low))[:, None, None, None]
    half_width = (0.5 * (high - low))[:, None, None, None]
    potential = box[:, None]

    def advance(counter, state):
        before, current = state
        image = 3.0 * current - 0.5 * neighbours(current) + potential * current
        scaled = (image - centre * current) / half_width
        following = jnp.where(counter == 0, scaled, 2.0 * scaled - before)
        live = (counter < degree_set)[:, None, None, None]
        return (jnp.where(live, current, before), jnp.where(live, following, current))
    before, current = lax.fori_loop(0, steps, advance, (orbital_set, orbital_set))
    cells = orbital_set.shape[2] ** 3
    squares = lax.optimization_barrier(jnp.sum(current * current, axis=(2, 3), keepdims=True))
    return current * jnp.sqrt(cells / (squares + 1e-06))

def hartree(density):
    table_x = sine_table(NX)
    table_y = sine_table(NY)
    table_z = sine_table(NZ)
    spectrum = along_third(density, table_z)
    spectrum = along_second(spectrum, table_y)
    spectrum = along_first(spectrum, table_x)
    divisor = eigen_values(0, NX, NX)[:, None, None] + eigen_values(0, NY, NY)[None, :, None] + eigen_values(0, NZ, NZ)[None, None, :] + screening
    spectrum = along_first(spectrum / divisor, table_x)
    spectrum = along_second(spectrum, table_y)
    return along_third(spectrum, table_z)

def reference(density, external, orbitals, anchors, weights, degrees):
    hartree_field = hartree(density)
    potential = hartree_field + external
    padded = jnp.pad(potential, ((0, FRAG), (0, FRAG), (0, 0)))

    def filter_one(parcel):
        orbital_set, corner, degree = parcel
        box = lax.dynamic_slice(padded, (corner[0], corner[1], corner[2]), (FRAG, FRAG, FRAG))
        box = box.reshape(1, FRAG, FRAG * FRAG)
        return chebyshev(orbital_set[None], box, degree[None], DEG_MAX)[0]
    filtered = lax.map(filter_one, (orbitals, anchors, degrees))
    weight_scale = weights.astype(jnp.float32) / NORB
    contribution = weight_scale[:, None, None] * lax.optimization_barrier(jnp.sum(filtered * filtered, axis=1))

    def place(counter, total):
        corner = (anchors[counter, 0], anchors[counter, 1], anchors[counter, 2])
        block = contribution[counter].reshape(FRAG, FRAG, FRAG)
        current = lax.dynamic_slice(total, corner, (FRAG, FRAG, FRAG))
        return lax.dynamic_update_slice(total, current + block, corner)
    widened = jnp.zeros((NX + FRAG, NY + FRAG, NZ), jnp.float32)
    widened = lax.fori_loop(0, NFRAG, place, widened)
    return (hartree_field, filtered, widened[:NX, :NY])
```

```python
import jax
import jax.numpy as jnp
import numpy as np
from jax import lax
from jax.experimental import pallas as pl
from jax.experimental.pallas import tpu as pltpu
from jax.sharding import Mesh
from jax.sharding import PartitionSpec as P

NX, NY, NZ = 512, 512, 256
NPX, NPY = 32, 16
ROWS, COLS = NX // NPX, NY // NPY
KZ = NZ // NPY
FRAG, NORB = 24, 8
PX = ("px_0", "px_1", "px_2")
ALL = PX + ("py",)
SCREENING, WINDOW_GAP, KINETIC_TOP = 0.002, 0.1, 6.0
STEPS = ((0, 0), (0, 1), (1, 0), (1, 1), (2, 0), (2, 1))
PADDED = COLS + 32 + FRAG
F32 = jnp.float32
BF16 = jnp.bfloat16
VMEM = pl.BlockSpec(memory_space=pltpu.VMEM)
SMEM = pl.BlockSpec(memory_space=pltpu.SMEM)


def sine_table(length):
    index = np.arange(1, length + 1, dtype=np.int64)
    product = index[:, None] * index[None, :] % (2 * length + 2)
    return np.sin(product * (np.pi / (length + 1))) * np.sqrt(2.0 / (length + 1))


def halves_of(table):
    high = np.asarray(table, np.float32).astype(BF16)
    low = (table - high.astype(np.float64)).astype(np.float32).astype(BF16)
    return high, low


def eigen_values(length):
    wave = np.arange(1, length + 1, dtype=np.float64) * (np.pi / (length + 1))
    return (4.0 * np.sin(wave / 2.0) ** 2).astype(np.float32)


SINE_Y = halves_of(sine_table(NY))
SINE_Z = halves_of(sine_table(NZ))
EIGEN_Y = eigen_values(NY)[None, :]
EIGEN_Z = eigen_values(NZ)[:, None]


def split2(x):
    high = x.astype(BF16)
    return high, (x - high.astype(F32)).astype(BF16)


def dot3(left, right, dims):
    def one(a, b):
        return lax.dot_general(a, b, (dims, ((), ())), preferred_element_type=F32)

    return one(left[0], right[0]) + (one(left[0], right[1]) + one(left[1], right[0]))


def call(kernel, outs, scratch=(), smem=(), count=1):
    return pl.pallas_call(
        kernel,
        out_shape=outs,
        in_specs=[SMEM if k in smem else VMEM for k in range(count)],
        out_specs=jax.tree.map(lambda _: VMEM, outs),
        scratch_shapes=list(scratch),
        compiler_params=pltpu.CompilerParams(vmem_limit_bytes=48 * 1024 * 1024),
    )


def shape(*dims):
    return jax.ShapeDtypeStruct(dims, F32)


def lanes(rows):
    return lax.broadcasted_iota(jnp.int32, (rows, 128), 1)


def rolled(x, by, axis=1):
    by %= x.shape[axis]
    return pltpu.roll(x, by, axis) if by else x


def decay(ey, ez):
    gap = ey + ez + SCREENING
    root = jnp.sqrt(gap + 0.25 * gap * gap)
    return 1.0 / (1.0 + 0.5 * gap + root), 0.5 / root


def forward_z(density, table_high, table_low, out):
    cells = density[...].reshape(ROWS * COLS, NZ)
    spectrum = dot3((table_high[...], table_low[...]), split2(cells), ((1,), (1,)))
    out[...] = spectrum.reshape(NPY, KZ, ROWS * COLS)


def scan_powers(place, ey, ez, power_out, weight_out, ends_out):
    rate, _ = decay(ey[...], ez[...])
    power = rate
    for _ in range(4):
        power = power * power
    before = jnp.ones((KZ, NY), F32)
    after = before
    for bit in range(5):
        upper = (place[0] >> bit) % 2 == 1
        power_out[bit] = power
        weight_out[bit] = jnp.where(upper, before, after)
        before, after = jnp.where(upper, before * power, before), jnp.where(upper, after, after * power)
        power = power * power
    ends_out[0] = before
    ends_out[1] = after


def forward_y(tiles, table_high, table_low, ey, ez, field_out, moment_out, merged):
    block = lanes(KZ) // COLS
    for row in range(ROWS):
        for tile in range(4):
            total = None
            for k in range(4):
                piece = tiles[4 * tile + k, :, row // 4 * 128 : row // 4 * 128 + 128]
                piece = rolled(piece, (k - row % 4) * COLS)
                total = piece if total is None else jnp.where(block == k, piece, total)
            merged[row * KZ : (row + 1) * KZ, tile * 128 : (tile + 1) * 128] = total
    field = dot3(split2(merged[...]), (table_high[...], table_low[...]), ((1,), (0,)))
    field_out[...] = field
    rate, _ = decay(ey[...], ez[...])
    first = field[:KZ]
    last = field[(ROWS - 1) * KZ :]
    for row in range(1, ROWS):
        first = field[row * KZ : (row + 1) * KZ] + rate * first
        back = ROWS - 1 - row
        last = field[back * KZ : (back + 1) * KZ] + rate * last
    moment_out[:KZ] = first
    moment_out[KZ:] = last


def back_y(field, totals, states, ends, table_high, table_low, ey, ez, tiles_out, solved):
    rate, scale = decay(ey[...], ez[...])
    across = rate
    for _ in range(9):
        across = across * across
    across = across * rate
    norm = rate / (1.0 - across * across)
    right_total, left_total = totals[:KZ], totals[KZ:]
    state = states[:KZ] - norm * (left_total - across * right_total) * ends[0]
    left = states[KZ:] - norm * (right_total - across * left_total) * ends[1]
    for row in range(ROWS):
        state = field[row * KZ : (row + 1) * KZ] + rate * state
        solved[row * KZ : (row + 1) * KZ] = state
    for row in range(ROWS - 1, -1, -1):
        here = pl.ds(row * KZ, KZ)
        solved[here] = scale * (solved[here] + rate * left)
        left = field[here] + rate * left
    columns = dot3(split2(solved[...]), (table_high[...], table_low[...]), ((1,), (0,)))
    solved[...] = columns
    block = lanes(KZ) // COLS
    for peer in range(NPY):
        for tile in range(4):
            total = None
            for k in range(4):
                row = 4 * tile + k
                piece = solved[row * KZ : (row + 1) * KZ, peer // 4 * 128 : peer // 4 * 128 + 128]
                piece = rolled(piece, (k - peer % 4) * COLS)
                total = piece if total is None else jnp.where(block == k, piece, total)
            tiles_out[peer, :, tile * 128 : (tile + 1) * 128] = total


def slots_of(rows):
    return lanes(rows) // 32


def back_z(places, tiles, external, table_high, table_low, field_out, *rest):
    pieces, grid = rest[:6], rest[6]
    spectrum = tiles[...].reshape(NZ, ROWS * COLS)
    turned = spectrum.T
    field = dot3(split2(turned), (table_high[...], table_low[...]), ((1,), (0,)))
    field = field.reshape(ROWS, COLS, NZ)
    field_out[...] = field
    potential = field + external[...]
    for half in range(2):
        grid[half, :, :32] = jnp.zeros((ROWS, 32, 128), F32)
        grid[half, :, 32 + COLS :] = jnp.zeros((ROWS, FRAG, 128), F32)
        grid[half, :, 32 : 32 + COLS] = potential[:, :, half * 128 : half * 128 + 128]
    lane = lanes(FRAG)
    slot_of = slots_of(FRAG)
    for k, (down, along) in enumerate(STEPS):
        groups = 8 if down < 2 else 4

        def cut(group, carry, k=k, along=along, groups=groups):
            total = None
            for slot in range(4):
                frag = slot % 2
                row = group + groups * (slot // 2)
                col, depth = places[6 * k + 3 * frag + 1], places[6 * k + 3 * frag + 2]
                cols = pl.ds(32 + col - 32 * along, FRAG)
                window = jnp.where(lane >= depth, grid[0, row, cols, :], grid[1, row, cols, :])
                window = pltpu.roll(window, (256 + 32 * slot - depth) & 127, 1)
                total = window if total is None else jnp.where(slot_of == slot, window, total)
            pieces[k][group] = total
            return carry

        lax.fori_loop(0, groups, cut, 0)


def orbitals_in(orbitals, out, strips, turned):
    for frag in range(2):
        for tile in range(5):
            width = min(128, FRAG * FRAG - tile * 128)
            strips[frag, tile, :, :width] = orbitals[frag, :, tile * 128 : tile * 128 + width]
    lane = lanes(8)

    def plane(x, carry):
        rows = []
        for yc in range(8):
            tile, off = divmod(72 * yc, 128)
            for frag in range(2):
                piece = rolled(strips[frag, tile, pl.ds(x, 8, stride=FRAG), :], -off)
                if off + 72 > 128:
                    other = rolled(strips[frag, tile + 1, pl.ds(x, 8, stride=FRAG), :], -off)
                    piece = jnp.where(lane < 128 - off, piece, other)
                rows.append(piece)
        turned[...] = jnp.concatenate(rows, 0).T
        for k in range(9):
            out[x, k] = turned[pl.ds(k // 3 * FRAG + k % 3, 8, stride=3), :]
        return carry

    lax.fori_loop(0, FRAG, plane, 0)


def orbitals_out(planes, scale, out, strips, turned):
    lane = lanes(8)
    factor = scale[...]

    def plane(x, carry):
        for k in range(9):
            turned[pl.ds(k // 3 * FRAG + k % 3, 8, stride=3), :] = planes[x, k] * factor
        rows = turned[...].T
        for frag in range(2):
            for tile in range(5):
                total = None
                for yc in range(8):
                    start = 72 * yc - 128 * tile
                    if -72 < start < 128:
                        piece = rows[(2 * yc + frag) * 8 : (2 * yc + frag) * 8 + 8]
                        piece = rolled(piece, start)
                        if total is None:
                            total = piece
                        else:
                            total = jnp.where(lane >= start, piece, total)
                strips[frag, tile, pl.ds(x, 8, stride=FRAG), :] = total
        return carry

    lax.fori_loop(0, FRAG, plane, 0)
    for frag in range(2):
        for tile in range(5):
            width = min(128, FRAG * FRAG - tile * 128)
            out[frag, :, tile * 128 : tile * 128 + width] = strips[frag, tile, :, :width]


def spread(value, lane):
    values = [value]
    for step in (4, 2, 1):
        clear = lane & step == 0
        values = [
            part
            for v in values
            for part in (
                jnp.where(clear, v, rolled(v, step)),
                jnp.where(clear, rolled(v, -step), v),
            )
        ]
    return values


def gather_sums(values, lane):
    for step in (4, 2, 1):
        clear = lane & step == 0
        count = len(values) // 2
        values = [
            jnp.where(
                clear,
                values[k] + rolled(values[k], -step),
                values[k + count] + rolled(values[k + count], step),
            )
            for k in range(count)
        ]
    return values[0]


def total_of(x):
    return jnp.sum(jnp.sum(x, axis=0, keepdims=True), axis=1, keepdims=True)


def filter_fragments(meta, *refs):
    pieces, start = refs[:6], refs[6]
    out, scale_out = refs[7:9]
    shares = refs[9:12]
    boxes, turned, compact, potential, other, spilled = refs[12:]
    lane = lanes(8)
    sub = lax.broadcasted_iota(jnp.int32, (8, 128), 0)
    second = (lane // 8) % 2 == 1
    for down in range(3):
        groups = 8 if down < 2 else 4

        def unpack(group, carry, down=down, groups=groups):
            both = pieces[2 * down][group] + pieces[2 * down + 1][group]
            for slot in range(4):
                row = 16 * down + group + groups * (slot // 2)
                boxes[slot % 2, pl.ds(pl.multiple_of(row * FRAG, 8), FRAG), :] = rolled(both, -32 * slot)
            return carry

        lax.fori_loop(0, groups, unpack, 0)
    lowest = None
    for part in range(3):
        rows = []
        for yc in range(8):
            for frag in range(2):
                base = (meta[frag] + 8 * part) * FRAG + 3 * yc
                took = [boxes[frag, pl.ds(base + yi, 8, stride=FRAG), :] for yi in range(3)]
                rows.append(
                    jnp.where(
                        lane < FRAG,
                        took[0],
                        jnp.where(lane < 2 * FRAG, rolled(took[1], FRAG), rolled(took[2], 2 * FRAG)),
                    )
                )
        turned[...] = jnp.concatenate(rows, 0).T
        for k in range(9):
            value = turned[pl.ds(k // 3 * FRAG + k % 3, 8, stride=3), :]
            compact[9 * part + k] = value
            lowest = value if lowest is None else jnp.minimum(lowest, value)
            highest = value if part + k == 0 else jnp.maximum(highest, value)

    def window(keep):
        low = jnp.where(keep, lowest, jnp.inf)
        high = jnp.where(keep, highest, -jnp.inf)
        low = jnp.min(jnp.min(low, axis=0, keepdims=True), axis=1, keepdims=True) + WINDOW_GAP
        high = jnp.max(jnp.max(high, axis=0, keepdims=True), axis=1, keepdims=True) + KINETIC_TOP
        return 0.5 * (high + low), 0.5 * (high - low)

    centre_0, half_0 = window(~second)
    centre_1, half_1 = window(second)
    centre = jnp.where(second, centre_1, centre_0)
    inverse = 1.0 / jnp.where(second, half_1, half_0)
    for part in range(3):
        for k in range(9):
            value = (3.0 + compact[9 * part + k] - centre) * (2.0 * inverse)
            for x, wide in enumerate(spread(value, lane)):
                potential[8 * part + x, k] = wide
    coupling = -inverse
    degree = jnp.where(second, meta[5], meta[4])

    def apply(source, target, initial=False, step=None):
        live = None if step is None else step <= degree

        def chunk(number, carry):
            behind, here = list(carry[:9]), list(carry[9:])
            for k4 in range(4):
                x = 4 * number + k4
                ahead_x = jnp.minimum(x + 1, FRAG - 1)
                ahead = [source[ahead_x, k] for k in range(9)]
                if k4 == 3:
                    ahead = [jnp.where(x + 1 < FRAG, v, 0.0) for v in ahead]
                for k in range(9):
                    yi, zi = divmod(k, 3)
                    total = behind[k] + ahead[k]
                    if yi > 0:
                        total = total + here[k - 3]
                    else:
                        total = total + jnp.where(lane >= 16, rolled(here[6 + zi], 16), 0.0)
                    if yi < 2:
                        total = total + here[k + 3]
                    else:
                        total = total + jnp.where(lane < 112, rolled(here[zi], -16), 0.0)
                    if zi > 0:
                        total = total + here[k - 1]
                    else:
                        total = total + jnp.where(sub >= 1, rolled(here[k + 2], 1, 0), 0.0)
                    if zi < 2:
                        total = total + here[k + 1]
                    else:
                        total = total + jnp.where(sub < 7, rolled(here[k - 2], -1, 0), 0.0)
                    image = potential[x, k] * here[k] + coupling * total
                    following = 0.5 * image if initial else image - target[x, k]
                    if live is not None:
                        following = jnp.where(live, following, here[k])
                    target[x, k] = following
                behind, here = here, ahead
            return tuple(behind + here)

        zero = [jnp.zeros((8, 128), F32)] * 9
        lax.fori_loop(0, 6, chunk, tuple(zero + [source[0, k] for k in range(9)]))

    def copy(x, carry):
        out[x] = start[x]
        return carry

    lax.fori_loop(0, FRAG, copy, 0)
    apply(out, other, initial=True)
    fewest = jnp.minimum(meta[4], meta[5])
    most = jnp.maximum(meta[4], meta[5])
    plain = (fewest - 1) // 2
    pairs = most // 2

    def free_pair(pair, carry):
        apply(other, out)
        apply(out, other)
        return carry

    def held_pair(pair, carry):
        apply(other, out, step=2 * pair + 2)
        apply(out, other, step=2 * pair + 3)
        return carry

    lax.fori_loop(0, plain, free_pair, 0)
    lax.fori_loop(plain, pairs, held_pair, 0)

    def squares(x, sums):
        for k in range(9):
            value = other[x, k]
            sums = sums + value * value
            out[x, k] = value
        return sums

    sums = lax.fori_loop(0, FRAG, squares, jnp.zeros((8, 128), F32))
    sums = jnp.sum(sums, axis=0, keepdims=True)
    sums = jnp.broadcast_to(sums, (8, 128))
    for step in (16, 32, 64):
        sums = sums + rolled(sums, step)
    scale = jnp.sqrt(float(FRAG**3) / (sums + 1e-06))
    scale_out[...] = scale
    weight = jnp.where(second, meta[3], meta[2]).astype(F32) / NORB

    def clear(row, carry):
        for frag in range(2):
            spilled[frag, pl.ds(pl.multiple_of(row * FRAG, 8), FRAG), :] = jnp.zeros((FRAG, 128), F32)
        return carry

    lax.fori_loop(0, 40, clear, 0)
    for part in range(3):
        for k in range(9):
            values = []
            for x in range(8):
                value = other[8 * part + x, k] * scale
                values.append(value * value)
            turned[pl.ds(k // 3 * FRAG + k % 3, 8, stride=3), :] = gather_sums(values, lane) * weight
        rows = turned[...].T
        for yc in range(8):
            for frag in range(2):
                piece = rows[(2 * yc + frag) * 8 : (2 * yc + frag) * 8 + 8]
                base = (meta[frag] + 8 * part) * FRAG + 3 * yc
                for yi in range(3):
                    spilled[frag, pl.ds(base + yi, 8, stride=FRAG), :] = rolled(piece, -FRAG * yi)
    slot_of = slots_of(FRAG)
    for down in range(3):
        groups = 8 if down < 2 else 4

        def share(group, carry, down=down, groups=groups):
            total = None
            for slot in range(4):
                row = 16 * down + group + groups * (slot // 2)
                piece = spilled[slot % 2, pl.ds(pl.multiple_of(row * FRAG, 8), FRAG), :]
                piece = rolled(piece, 32 * slot)
                total = piece if total is None else jnp.where(slot_of == slot, piece, total)
            shares[down][group] = total
            return carry

        lax.fori_loop(0, groups, share, 0)


def patch(places, *refs):
    shares, out, grid = refs[:6], refs[6], refs[7]

    def clear(row, carry):
        for half in range(2):
            grid[half, row] = jnp.zeros((PADDED, 128), F32)
        return carry

    lax.fori_loop(0, ROWS, clear, 0)
    lane = lanes(FRAG)
    for k, (down, along) in enumerate(STEPS):
        groups = 8 if down < 2 else 4

        def add(group, carry, k=k, along=along, groups=groups):
            both = shares[k][group]
            for slot in range(4):
                frag = slot % 2
                row = group + groups * (slot // 2)
                col, depth = places[6 * k + 3 * frag + 1], places[6 * k + 3 * frag + 2]
                piece = pltpu.roll(both, (256 + depth - 32 * slot) & 127, 1)
                piece = jnp.where(((lane - depth) & 127) < FRAG, piece, 0.0)
                cols = pl.ds(32 + col - 32 * along, FRAG)
                grid[0, row, cols, :] += jnp.where(lane >= depth, piece, 0.0)
                grid[1, row, cols, :] += jnp.where(lane >= depth, 0.0, piece)
            return carry

        lax.fori_loop(0, groups, add, 0)
    for half in range(2):
        out[:, :, half * 128 : half * 128 + 128] = grid[half, :, 32 : 32 + COLS]


def moved(x, down, along):
    pairs = [
        (p * NPY + q, (p + down) * NPY + q + along)
        for p in range(NPX)
        for q in range(NPY)
        if 0 <= p + down < NPX and 0 <= q + along < NPY
    ]
    return lax.ppermute(x, ALL, pairs)


def body(density, external, orbitals, anchors, weights, degrees):
    row_place = lax.axis_index(PX)
    col_place = lax.axis_index("py")
    origin = jnp.stack([row_place * ROWS, col_place * COLS, 0])
    local = (anchors - origin[None, :]).astype(jnp.int32)
    own = jnp.pad(local.reshape(6), (0, 2))
    above = jnp.stack([own, moved(own, 1, 0), moved(own, 2, 0)])
    places = jnp.stack([above, moved(above, 0, 1)], 1)[:, :, :6].reshape(36)
    meta = jnp.concatenate([local[:, 0], weights, degrees, weights]).astype(jnp.int32)

    sine_y = [jnp.asarray(t) for t in SINE_Y]
    sine_z = [jnp.asarray(t) for t in SINE_Z]
    ey = jnp.asarray(EIGEN_Y)
    ez = lax.dynamic_slice(jnp.asarray(EIGEN_Z), (col_place * KZ, 0), (KZ, 1))

    planes = call(
        orbitals_in,
        shape(FRAG, 9, 8, 128),
        [pltpu.VMEM((2, 5, NORB * FRAG, 128), F32), pltpu.VMEM((128, 128), F32)],
    )(orbitals.reshape(2, NORB * FRAG, FRAG * FRAG))
    power, weight, ends = call(
        scan_powers,
        (shape(5, KZ, NY), shape(5, KZ, NY), shape(2, KZ, NY)),
        smem=(0,),
        count=3,
    )(row_place.reshape(1).astype(jnp.int32), ey, ez)

    tiles = call(forward_z, shape(NPY, KZ, ROWS * COLS), count=3)(density, *sine_z)
    tiles = lax.all_to_all(tiles, "py", split_axis=0, concat_axis=0, tiled=True)
    field, totals = call(
        forward_y,
        (shape(ROWS * KZ, NY), shape(2 * KZ, NY)),
        [pltpu.VMEM((ROWS * KZ, NY), F32)],
        count=5,
    )(tiles, *sine_y, ey, ez)

    right, left = jnp.zeros((KZ, NY), F32), jnp.zeros((KZ, NY), F32)
    for bit in range(5):
        pairs = [(p * NPY + q, (p ^ (1 << bit)) * NPY + q) for p in range(NPX) for q in range(NPY)]
        got = lax.ppermute(totals, ALL, pairs)
        upper = (row_place >> bit) % 2 == 1
        high, low = jnp.where(upper, totals, got), jnp.where(upper, got, totals)
        right = right + jnp.where(upper, weight[bit] * got[:KZ], 0.0)
        left = left + jnp.where(upper, 0.0, weight[bit] * got[KZ:])
        totals = jnp.concatenate([high[:KZ] + power[bit] * low[:KZ], low[KZ:] + power[bit] * high[KZ:]])
    states = jnp.concatenate([right, left])

    tiles = call(back_y, shape(NPY, KZ, ROWS * COLS), [pltpu.VMEM((ROWS * KZ, NY), F32)], count=8)(
        field, totals, states, ends, *sine_y, ey, ez
    )
    tiles = lax.all_to_all(tiles, "py", split_axis=0, concat_axis=0, tiled=True)
    hartree_field, *pieces = call(
        back_z,
        [shape(ROWS, COLS, NZ)] + [shape(8 if down < 2 else 4, FRAG, 128) for down, _ in STEPS],
        [pltpu.VMEM((2, ROWS, PADDED, 128), F32)],
        smem=(0,),
        count=5,
    )(places, tiles, external, *sine_z)
    pieces = [pieces[k] if k == 0 else moved(pieces[k], -STEPS[k][0], -STEPS[k][1]) for k in range(6)]
    planes, scale, *shares = call(
        filter_fragments,
        [shape(FRAG, 9, 8, 128), shape(8, 128)] + [shape(n, FRAG, 128) for n in (8, 8, 4)],
        [
            pltpu.VMEM((2, 40 * FRAG, 128), F32),
            pltpu.VMEM((128, 128), F32),
            pltpu.VMEM((27, 8, 128), F32),
            pltpu.VMEM((FRAG, 9, 8, 128), F32),
            pltpu.VMEM((FRAG, 9, 8, 128), F32),
            pltpu.VMEM((2, 40 * FRAG, 128), F32),
        ],
        smem=(0,),
        count=8,
    )(meta, *pieces, planes)
    received = [
        shares[down] if k == 0 else moved(shares[down], down, along)
        for k, (down, along) in enumerate(STEPS)
    ]
    filtered = call(
        orbitals_out,
        shape(2, NORB * FRAG, FRAG * FRAG),
        [pltpu.VMEM((2, 5, NORB * FRAG, 128), F32), pltpu.VMEM((128, 128), F32)],
        count=2,
    )(planes, scale)
    new_density = call(
        patch,
        shape(ROWS, COLS, NZ),
        [pltpu.VMEM((2, ROWS, PADDED, 128), F32)],
        smem=(0,),
        count=7,
    )(places, *received)
    return hartree_field, filtered.reshape(orbitals.shape), new_density


def solution(mesh):
    torus = Mesh(mesh.devices.reshape(8, 2, 2, NPY), ALL)
    grid = P(PX, "py", None)
    return jax.shard_map(
        body,
        mesh=torus,
        in_specs=(grid, grid, P(ALL, None, None, None), P(ALL, None), P(ALL), P(ALL)),
        out_specs=(grid, P(ALL, None, None, None), grid),
        check_vma=False,
    )
```

```python
import jax
import jax.numpy as jnp
import numpy as np
from jax import lax
from jax.experimental import pallas as pl
from jax.experimental.pallas import tpu as pltpu
from jax.sharding import Mesh
from jax.sharding import PartitionSpec as P

NX, NY, NZ = 512, 512, 256
NPX, NPY = 32, 16
ROWS, COLS = NX // NPX, NY // NPY
KZ = NZ // NPY
FRAG, NORB = 24, 8
PX = ("px_0", "px_1", "px_2")
ALL = PX + ("py",)
SCREENING, WINDOW_GAP, KINETIC_TOP = 0.002, 0.1, 6.0
STEPS = ((0, 0), (0, 1), (1, 0), (1, 1), (2, 0), (2, 1))
PADDED = COLS + 32 + FRAG
F32 = jnp.float32
BF16 = jnp.bfloat16
VMEM = pl.BlockSpec(memory_space=pltpu.VMEM)
SMEM = pl.BlockSpec(memory_space=pltpu.SMEM)
ANYWHERE = pl.BlockSpec(memory_space=pl.ANY)


def sine_table(length):
    index = np.arange(1, length + 1, dtype=np.int64)
    product = index[:, None] * index[None, :] % (2 * length + 2)
    return np.sin(product * (np.pi / (length + 1))) * np.sqrt(2.0 / (length + 1))


def halves_of(table):
    high = np.asarray(table, np.float32).astype(BF16)
    low = (table - high.astype(np.float64)).astype(np.float32).astype(BF16)
    return high, low


def eigen_values(length):
    wave = np.arange(1, length + 1, dtype=np.float64) * (np.pi / (length + 1))
    return (4.0 * np.sin(wave / 2.0) ** 2).astype(np.float32)


SINE_Y = halves_of(sine_table(NY))
SINE_Z = halves_of(sine_table(NZ))
EIGEN_Y = eigen_values(NY)[None, :]
EIGEN_Z = eigen_values(NZ)[:, None]


def split2(x):
    high = x.astype(BF16)
    return high, (x - high.astype(F32)).astype(BF16)


def dot3(left, right, dims):
    def one(a, b):
        return lax.dot_general(a, b, (dims, ((), ())), preferred_element_type=F32)

    return one(left[0], right[0]) + (one(left[0], right[1]) + one(left[1], right[0]))


def call(kernel, outs, scratch=(), smem=(), count=1, space=VMEM):
    return pl.pallas_call(
        kernel,
        out_shape=outs,
        in_specs=[SMEM if k in smem else space for k in range(count)],
        out_specs=jax.tree.map(lambda _: VMEM, outs),
        scratch_shapes=list(scratch),
        compiler_params=pltpu.CompilerParams(vmem_limit_bytes=48 * 1024 * 1024),
    )


def shape(*dims):
    return jax.ShapeDtypeStruct(dims, F32)


def lanes(rows):
    return lax.broadcasted_iota(jnp.int32, (rows, 128), 1)


def rolled(x, by, axis=1):
    by %= x.shape[axis]
    return pltpu.roll(x, by, axis) if by else x


def decay(ey, ez):
    gap = ey + ez + SCREENING
    root = jnp.sqrt(gap + 0.25 * gap * gap)
    return 1.0 / (1.0 + 0.5 * gap + root), 0.5 / root


def forward_z(density, table_high, table_low, out, cells, high, low, sems):
    copies = [
        pltpu.make_async_copy(source, target, sems.at[k])
        for k, (source, target) in enumerate(((density, cells), (table_high, high), (table_low, low)))
    ]
    for one in copies:
        one.start()
    for one in copies:
        one.wait()
    spectrum = dot3((high[...], low[...]), split2(cells[...].reshape(ROWS * COLS, NZ)), ((1,), (1,)))
    out[...] = spectrum.reshape(NPY, KZ, ROWS * COLS)


def scan_powers(place, ey, ez, power_out, weight_out, ends_out):
    rate, _ = decay(ey[...], ez[...])
    power = rate
    for _ in range(4):
        power = power * power
    before = jnp.ones((KZ, NY), F32)
    after = before
    for bit in range(5):
        upper = (place[0] >> bit) % 2 == 1
        if bit < 3:
            power_out[bit] = power
        if bit < 2:
            weight_out[bit] = jnp.where(upper, before, after)
        if bit == 2:
            ends_out[0] = before
            ends_out[1] = after
        before, after = jnp.where(upper, before * power, before), jnp.where(upper, after, after * power)
        power = power * power
    ends_out[2] = before
    ends_out[3] = after


def forward_y(tiles, table_high, table_low, ey, ez, field_out, moment_out, merged):
    block = lanes(KZ) // COLS
    for row in range(ROWS):
        for tile in range(4):
            total = None
            for k in range(4):
                piece = tiles[4 * tile + k, :, row // 4 * 128 : row // 4 * 128 + 128]
                piece = rolled(piece, (k - row % 4) * COLS)
                total = piece if total is None else jnp.where(block == k, piece, total)
            merged[row * KZ : (row + 1) * KZ, tile * 128 : (tile + 1) * 128] = total
    field = dot3(split2(merged[...]), (table_high[...], table_low[...]), ((1,), (0,)))
    field_out[...] = field
    rate, _ = decay(ey[...], ez[...])
    first = field[:KZ]
    last = field[(ROWS - 1) * KZ :]
    for row in range(1, ROWS):
        first = field[row * KZ : (row + 1) * KZ] + rate * first
        back = ROWS - 1 - row
        last = field[back * KZ : (back + 1) * KZ] + rate * last
    moment_out[:KZ] = first
    moment_out[KZ:] = last


def back_y(place, field, totals, right, left, power, ends, *rest):
    table_high, table_low, ey, ez, tiles_out, solved = rest
    rate, scale = decay(ey[...], ez[...])
    across = rate
    for _ in range(9):
        across = across * across
    across = across * rate
    norm = rate / (1.0 - across * across)
    four = power[2]
    right_total = left_total = jnp.zeros((KZ, NY), F32)
    state, after = right_total, left_total
    for k in range(NPX // 4):
        state = jnp.where(k == place[0], right_total, state)
        right_total = totals[k, :KZ] + four * right_total
    for k in range(NPX // 4 - 1, -1, -1):
        after = jnp.where(k == place[0], left_total, after)
        left_total = totals[k, KZ:] + four * left_total
    state = right[...] + ends[0] * state - norm * (left_total - across * right_total) * ends[2]
    left = left[...] + ends[1] * after - norm * (right_total - across * left_total) * ends[3]
    for row in range(ROWS):
        state = field[row * KZ : (row + 1) * KZ] + rate * state
        solved[row * KZ : (row + 1) * KZ] = state
    for row in range(ROWS - 1, -1, -1):
        here = pl.ds(row * KZ, KZ)
        solved[here] = scale * (solved[here] + rate * left)
        left = field[here] + rate * left
    columns = dot3(split2(solved[...]), (table_high[...], table_low[...]), ((1,), (0,)))
    solved[...] = columns
    block = lanes(KZ) // COLS
    for peer in range(NPY):
        for tile in range(4):
            total = None
            for k in range(4):
                row = 4 * tile + k
                piece = solved[row * KZ : (row + 1) * KZ, peer // 4 * 128 : peer // 4 * 128 + 128]
                piece = rolled(piece, (k - peer % 4) * COLS)
                total = piece if total is None else jnp.where(block == k, piece, total)
            tiles_out[peer, :, tile * 128 : (tile + 1) * 128] = total


def slots_of(rows):
    return lanes(rows) // 32


def back_z(places, tiles, external, table_high, table_low, field_out, *rest):
    pieces, grid = rest[:6], rest[6]
    spectrum = tiles[...].reshape(NZ, ROWS * COLS)
    turned = spectrum.T
    field = dot3(split2(turned), (table_high[...], table_low[...]), ((1,), (0,)))
    field = field.reshape(ROWS, COLS, NZ)
    field_out[...] = field
    potential = field + external[...]
    for half in range(2):
        grid[half, :, :32] = jnp.zeros((ROWS, 32, 128), F32)
        grid[half, :, 32 + COLS :] = jnp.zeros((ROWS, FRAG, 128), F32)
        grid[half, :, 32 : 32 + COLS] = potential[:, :, half * 128 : half * 128 + 128]
    lane = lanes(FRAG)
    slot_of = slots_of(FRAG)
    for k, (down, along) in enumerate(STEPS):
        groups = 8 if down < 2 else 4

        def cut(number, carry, k=k, along=along, groups=groups):
            totals = []
            for part in range(4):
                total = None
                for slot in range(4):
                    frag = slot % 2
                    row = 4 * number + part + groups * (slot // 2)
                    col, depth = places[6 * k + 3 * frag + 1], places[6 * k + 3 * frag + 2]
                    cols = pl.ds(32 + col - 32 * along, FRAG)
                    window = jnp.where(lane >= depth, grid[0, row, cols, :], grid[1, row, cols, :])
                    window = pltpu.roll(window, (256 + 32 * slot - depth) & 127, 1)
                    total = window if total is None else jnp.where(slot_of == slot, window, total)
                totals.append(total)
            for part in range(4):
                pieces[k][4 * number + part] = totals[part]
            return carry

        lax.fori_loop(0, groups // 4, cut, 0)


def orbitals_in(orbitals, out, strips, turned):
    for frag in range(2):
        for tile in range(5):
            width = min(128, FRAG * FRAG - tile * 128)
            strips[frag, tile, :, :width] = orbitals[frag, :, tile * 128 : tile * 128 + width]
    lane = lanes(8)

    def plane(x, place):
        rows = []
        for yc in range(8):
            tile, off = divmod(72 * yc, 128)
            for frag in range(2):
                piece = rolled(strips[frag, tile, pl.ds(x, 8, stride=FRAG), :], -off)
                if off + 72 > 128:
                    other = rolled(strips[frag, tile + 1, pl.ds(x, 8, stride=FRAG), :], -off)
                    piece = jnp.where(lane < 128 - off, piece, other)
                rows.append(piece)
        place[...] = jnp.concatenate(rows, 0).T

    def planes(number, carry):
        for part in range(3):
            plane(3 * number + part, turned.at[part])
        for part in range(3):
            for k in range(9):
                rows = pl.ds(k // 3 * FRAG + k % 3, 8, stride=3)
                out[3 * number + part, k] = turned.at[part][rows, :]
        return carry

    lax.fori_loop(0, FRAG // 3, planes, 0)


def orbitals_out(planes, scale, out, strips, turned):
    lane = lanes(8)
    factor = scale[...]

    def plane(x, rows):
        for frag in range(2):
            for tile in range(5):
                total = None
                for yc in range(8):
                    start = 72 * yc - 128 * tile
                    if -72 < start < 128:
                        piece = rows[(2 * yc + frag) * 8 : (2 * yc + frag) * 8 + 8]
                        piece = rolled(piece, start)
                        if total is None:
                            total = piece
                        else:
                            total = jnp.where(lane >= start, piece, total)
                strips[frag, tile, pl.ds(x, 8, stride=FRAG), :] = total

    def trip(number, carry):
        for part in range(3):
            for k in range(9):
                rows = pl.ds(k // 3 * FRAG + k % 3, 8, stride=3)
                turned.at[part][rows, :] = planes[3 * number + part, k] * factor
        rows = [turned[part].T for part in range(3)]
        for part in range(3):
            plane(3 * number + part, rows[part])
        return carry

    lax.fori_loop(0, FRAG // 3, trip, 0)
    for frag in range(2):
        for tile in range(5):
            width = min(128, FRAG * FRAG - tile * 128)
            out[frag, :, tile * 128 : tile * 128 + width] = strips[frag, tile, :, :width]


def spread(value, lane):
    values = [value]
    for step in (4, 2, 1):
        clear = lane & step == 0
        values = [
            part
            for v in values
            for part in (
                jnp.where(clear, v, rolled(v, step)),
                jnp.where(clear, rolled(v, -step), v),
            )
        ]
    return values


def gather_sums(values, lane):
    for step in (4, 2, 1):
        clear = lane & step == 0
        count = len(values) // 2
        values = [
            jnp.where(
                clear,
                values[k] + rolled(values[k], -step),
                values[k + count] + rolled(values[k + count], step),
            )
            for k in range(count)
        ]
    return values[0]


def total_of(x):
    return jnp.sum(jnp.sum(x, axis=0, keepdims=True), axis=1, keepdims=True)


def filter_fragments(meta, *refs):
    pieces, start = refs[:6], refs[6]
    out, scale_out = refs[7:9]
    shares = refs[9:12]
    boxes, turned, compact, potential, other, spilled = refs[12:]
    lane = lanes(8)
    sub = lax.broadcasted_iota(jnp.int32, (8, 128), 0)
    second = (lane // 8) % 2 == 1
    for down in range(3):
        groups = 8 if down < 2 else 4

        def unpack(number, carry, down=down, groups=groups):
            moved_windows = []
            for part in range(4):
                group = 4 * number + part
                both = pieces[2 * down][group] + pieces[2 * down + 1][group]
                moved_windows.append([rolled(both, -32 * slot) for slot in range(4)])
            for part in range(4):
                for slot in range(4):
                    row = 16 * down + 4 * number + part + groups * (slot // 2)
                    rows = pl.ds(pl.multiple_of(row * FRAG, 8), FRAG)
                    boxes[slot % 2, rows, :] = moved_windows[part][slot]
            return carry

        lax.fori_loop(0, groups // 4, unpack, 0)
    lowest = None
    for part in range(3):
        rows = []
        for yc in range(8):
            for frag in range(2):
                base = (meta[frag] + 8 * part) * FRAG + 3 * yc
                took = [boxes[frag, pl.ds(base + yi, 8, stride=FRAG), :] for yi in range(3)]
                rows.append(
                    jnp.where(
                        lane < FRAG,
                        took[0],
                        jnp.where(lane < 2 * FRAG, rolled(took[1], FRAG), rolled(took[2], 2 * FRAG)),
                    )
                )
        turned[part] = jnp.concatenate(rows, 0).T
    for part in range(3):
        for k in range(9):
            value = turned.at[part][pl.ds(k // 3 * FRAG + k % 3, 8, stride=3), :]
            compact[9 * part + k] = value
            lowest = value if lowest is None else jnp.minimum(lowest, value)
            highest = value if part + k == 0 else jnp.maximum(highest, value)

    def window(keep):
        low = jnp.where(keep, lowest, jnp.inf)
        high = jnp.where(keep, highest, -jnp.inf)
        low = jnp.min(jnp.min(low, axis=0, keepdims=True), axis=1, keepdims=True) + WINDOW_GAP
        high = jnp.max(jnp.max(high, axis=0, keepdims=True), axis=1, keepdims=True) + KINETIC_TOP
        return 0.5 * (high + low), 0.5 * (high - low)

    centre_0, half_0 = window(~second)
    centre_1, half_1 = window(second)
    centre = jnp.where(second, centre_1, centre_0)
    inverse = 1.0 / jnp.where(second, half_1, half_0)
    for part in range(3):
        for k in range(9):
            value = (3.0 + compact[9 * part + k] - centre) * (2.0 * inverse)
            for x, wide in enumerate(spread(value, lane)):
                potential[8 * part + x, k] = wide
    coupling = -inverse
    degree = jnp.where(second, meta[5], meta[4])

    def apply(source, target, earlier=None, initial=False, step=None):
        live = None if step is None else step <= degree
        earlier = target if earlier is None else earlier

        def chunk(number, carry):
            behind, here = list(carry[:9]), list(carry[9:])
            for k4 in range(8):
                x = 8 * number + k4
                ahead_x = jnp.minimum(x + 1, FRAG - 1)
                ahead = [source[ahead_x, k] for k in range(9)]
                if k4 == 7:
                    ahead = [jnp.where(x + 1 < FRAG, v, 0.0) for v in ahead]
                for k in range(9):
                    yi, zi = divmod(k, 3)
                    total = behind[k] + ahead[k]
                    if yi > 0:
                        total = total + here[k - 3]
                    else:
                        total = total + jnp.where(lane >= 16, rolled(here[6 + zi], 16), 0.0)
                    if yi < 2:
                        total = total + here[k + 3]
                    else:
                        total = total + jnp.where(lane < 112, rolled(here[zi], -16), 0.0)
                    if zi > 0:
                        total = total + here[k - 1]
                    else:
                        total = total + jnp.where(sub >= 1, rolled(here[k + 2], 1, 0), 0.0)
                    if zi < 2:
                        total = total + here[k + 1]
                    else:
                        total = total + jnp.where(sub < 7, rolled(here[k - 2], -1, 0), 0.0)
                    image = potential[x, k] * here[k] + coupling * total
                    following = 0.5 * image if initial else image - earlier[x, k]
                    if live is not None:
                        following = jnp.where(live, following, here[k])
                    target[x, k] = following
                behind, here = here, ahead
            return tuple(behind + here)

        zero = [jnp.zeros((8, 128), F32)] * 9
        lax.fori_loop(0, 3, chunk, tuple(zero + [source[0, k] for k in range(9)]))

    apply(start, other, initial=True)
    apply(other, out, earlier=start)
    fewest = jnp.minimum(meta[4], meta[5])
    most = jnp.maximum(meta[4], meta[5])
    plain = (fewest - 2) // 2
    pairs = (most - 1) // 2

    def free_pair(pair, carry):
        apply(out, other)
        apply(other, out)
        return carry

    def held_pair(pair, carry):
        apply(out, other, step=2 * pair + 3)
        apply(other, out, step=2 * pair + 4)
        return carry

    lax.fori_loop(0, plain, free_pair, 0)
    lax.fori_loop(plain, pairs, held_pair, 0)

    def squares(x, sums):
        return tuple(sums[k] + out[x, k] * out[x, k] for k in range(9))

    sums = lax.fori_loop(0, FRAG, squares, (jnp.zeros((8, 128), F32),) * 9)
    sums = sum(sums[1:], sums[0])
    sums = jnp.sum(sums, axis=0, keepdims=True)
    sums = jnp.broadcast_to(sums, (8, 128))
    for step in (16, 32, 64):
        sums = sums + rolled(sums, step)
    scale = jnp.sqrt(float(FRAG**3) / (sums + 1e-06))
    scale_out[...] = scale
    weight = jnp.where(second, meta[3], meta[2]).astype(F32) / NORB

    def clear(row, carry):
        for frag in range(2):
            spilled[frag, pl.ds(pl.multiple_of(row * FRAG, 8), FRAG), :] = jnp.zeros((FRAG, 128), F32)
        return carry

    lax.fori_loop(0, 40, clear, 0)
    for part in range(3):
        for k in range(9):
            values = []
            for x in range(8):
                value = out[8 * part + x, k] * scale
                values.append(value * value)
            turned.at[part][pl.ds(k // 3 * FRAG + k % 3, 8, stride=3), :] = gather_sums(values, lane) * weight
    for part in range(3):
        rows = turned[part].T
        for yc in range(8):
            for frag in range(2):
                piece = rows[(2 * yc + frag) * 8 : (2 * yc + frag) * 8 + 8]
                base = (meta[frag] + 8 * part) * FRAG + 3 * yc
                for yi in range(3):
                    spilled[frag, pl.ds(base + yi, 8, stride=FRAG), :] = rolled(piece, -FRAG * yi)
    slot_of = slots_of(FRAG)
    for down in range(3):
        groups = 8 if down < 2 else 4

        def share(number, carry, down=down, groups=groups):
            totals = []
            for part in range(4):
                total = None
                for slot in range(4):
                    row = 16 * down + 4 * number + part + groups * (slot // 2)
                    piece = spilled[slot % 2, pl.ds(pl.multiple_of(row * FRAG, 8), FRAG), :]
                    piece = rolled(piece, 32 * slot)
                    total = piece if total is None else jnp.where(slot_of == slot, piece, total)
                totals.append(total)
            for part in range(4):
                shares[down][4 * number + part] = totals[part]
            return carry

        lax.fori_loop(0, groups // 4, share, 0)


def patch(places, *refs):
    shares, out, grid = refs[:6], refs[6], refs[7]

    def clear(row, carry):
        for half in range(2):
            grid[half, row] = jnp.zeros((PADDED, 128), F32)
        return carry

    lax.fori_loop(0, ROWS, clear, 0)
    lane = lanes(FRAG)
    for k, (down, along) in enumerate(STEPS):
        groups = 8 if down < 2 else 4

        def add(number, carry, k=k, along=along, groups=groups):
            pieces = []
            for part in range(4):
                both = shares[k][4 * number + part]
                for slot in range(4):
                    depth = places[6 * k + 3 * (slot % 2) + 2]
                    pieces.append(pltpu.roll(both, (256 + depth - 32 * slot) & 127, 1))
            for part in range(4):
                for slot in range(4):
                    frag = slot % 2
                    row = 4 * number + part + groups * (slot // 2)
                    col, depth = places[6 * k + 3 * frag + 1], places[6 * k + 3 * frag + 2]
                    piece = jnp.where(((lane - depth) & 127) < FRAG, pieces[4 * part + slot], 0.0)
                    cols = pl.ds(32 + col - 32 * along, FRAG)
                    grid[0, row, cols, :] += jnp.where(lane >= depth, piece, 0.0)
                    grid[1, row, cols, :] += jnp.where(lane >= depth, 0.0, piece)
            return carry

        lax.fori_loop(0, groups // 4, add, 0)
    for half in range(2):
        out[:, :, half * 128 : half * 128 + 128] = grid[half, :, 32 : 32 + COLS]


def moved(x, down, along):
    pairs = [
        (p * NPY + q, (p + down) * NPY + q + along)
        for p in range(NPX)
        for q in range(NPY)
        if 0 <= p + down < NPX and 0 <= q + along < NPY
    ]
    return lax.ppermute(x, ALL, pairs)


def body(density, external, orbitals, anchors, weights, degrees):
    row_place = lax.axis_index(PX)
    col_place = lax.axis_index("py")
    origin = jnp.stack([row_place * ROWS, col_place * COLS, 0])
    local = (anchors - origin[None, :]).astype(jnp.int32)
    own = jnp.pad(local.reshape(6), (0, 2))
    above = jnp.stack([own, moved(own, 1, 0), moved(own, 2, 0)])
    places = jnp.stack([above, moved(above, 0, 1)], 1)[:, :, :6].reshape(36)
    meta = jnp.concatenate([local[:, 0], weights, degrees, weights]).astype(jnp.int32)

    sine_y = [jnp.asarray(t) for t in SINE_Y]
    sine_z = [jnp.asarray(t) for t in SINE_Z]
    ey = jnp.asarray(EIGEN_Y)
    ez = lax.dynamic_slice(jnp.asarray(EIGEN_Z), (col_place * KZ, 0), (KZ, 1))

    planes = call(
        orbitals_in,
        shape(FRAG, 9, 8, 128),
        [pltpu.VMEM((2, 5, NORB * FRAG, 128), F32), pltpu.VMEM((3, 128, 128), F32)],
    )(orbitals.reshape(2, NORB * FRAG, FRAG * FRAG))
    power, weight, ends = call(
        scan_powers,
        (shape(3, KZ, NY), shape(2, KZ, NY), shape(4, KZ, NY)),
        smem=(0,),
        count=3,
    )(row_place.reshape(1).astype(jnp.int32), ey, ez)

    tiles = call(
        forward_z,
        shape(NPY, KZ, ROWS * COLS),
        [
            pltpu.VMEM((ROWS, COLS, NZ), F32),
            pltpu.VMEM((NZ, NZ), BF16),
            pltpu.VMEM((NZ, NZ), BF16),
            pltpu.SemaphoreType.DMA((3,)),
        ],
        count=3,
        space=ANYWHERE,
    )(density, *sine_z)
    tiles = lax.all_to_all(tiles, "py", split_axis=0, concat_axis=0, tiled=True)
    field, totals = call(
        forward_y,
        (shape(ROWS * KZ, NY), shape(2 * KZ, NY)),
        [pltpu.VMEM((ROWS * KZ, NY), F32)],
        count=5,
    )(tiles, *sine_y, ey, ez)

    right, left = jnp.zeros((KZ, NY), F32), jnp.zeros((KZ, NY), F32)
    for bit in range(2):
        pairs = [(p * NPY + q, (p ^ (1 << bit)) * NPY + q) for p in range(NPX) for q in range(NPY)]
        got = lax.ppermute(totals, ALL, pairs)
        upper = (row_place >> bit) % 2 == 1
        high, low = jnp.where(upper, totals, got), jnp.where(upper, got, totals)
        right = right + jnp.where(upper, weight[bit] * got[:KZ], 0.0)
        left = left + jnp.where(upper, 0.0, weight[bit] * got[KZ:])
        totals = jnp.concatenate([high[:KZ] + power[bit] * low[:KZ], low[KZ:] + power[bit] * high[KZ:]])
    totals = lax.all_to_all(
        jnp.broadcast_to(totals, (NPX // 4, 2 * KZ, NY)), "px_0", split_axis=0, concat_axis=0, tiled=True
    )

    tiles = call(
        back_y,
        shape(NPY, KZ, ROWS * COLS),
        [pltpu.VMEM((ROWS * KZ, NY), F32)],
        smem=(0,),
        count=11,
    )(
        (row_place // 4).reshape(1).astype(jnp.int32), field, totals, right, left, power, ends, *sine_y, ey, ez
    )
    tiles = lax.all_to_all(tiles, "py", split_axis=0, concat_axis=0, tiled=True)
    hartree_field, *pieces = call(
        back_z,
        [shape(ROWS, COLS, NZ)] + [shape(8 if down < 2 else 4, FRAG, 128) for down, _ in STEPS],
        [pltpu.VMEM((2, ROWS, PADDED, 128), F32)],
        smem=(0,),
        count=5,
    )(places, tiles, external, *sine_z)
    pieces = [pieces[k] if k == 0 else moved(pieces[k], -STEPS[k][0], -STEPS[k][1]) for k in range(6)]
    planes, scale, *shares = call(
        filter_fragments,
        [shape(FRAG, 9, 8, 128), shape(8, 128)] + [shape(n, FRAG, 128) for n in (8, 8, 4)],
        [
            pltpu.VMEM((2, 40 * FRAG, 128), F32),
            pltpu.VMEM((3, 128, 128), F32),
            pltpu.VMEM((27, 8, 128), F32),
            pltpu.VMEM((FRAG, 9, 8, 128), F32),
            pltpu.VMEM((FRAG, 9, 8, 128), F32),
            pltpu.VMEM((2, 40 * FRAG, 128), F32),
        ],
        smem=(0,),
        count=8,
    )(meta, *pieces, planes)
    received = [
        shares[down] if k == 0 else moved(shares[down], down, along)
        for k, (down, along) in enumerate(STEPS)
    ]
    filtered = call(
        orbitals_out,
        shape(2, NORB * FRAG, FRAG * FRAG),
        [pltpu.VMEM((2, 5, NORB * FRAG, 128), F32), pltpu.VMEM((3, 128, 128), F32)],
        count=2,
    )(planes, scale)
    new_density = call(
        patch,
        shape(ROWS, COLS, NZ),
        [pltpu.VMEM((2, ROWS, PADDED, 128), F32)],
        smem=(0,),
        count=7,
    )(places, *received)
    return hartree_field, filtered.reshape(orbitals.shape), new_density


def solution(mesh):
    torus = Mesh(mesh.devices.reshape(8, 2, 2, NPY), ALL)
    grid = P(PX, "py", None)
    return jax.shard_map(
        body,
        mesh=torus,
        in_specs=(grid, grid, P(ALL, None, None, None), P(ALL, None), P(ALL), P(ALL)),
        out_specs=(grid, P(ALL, None, None, None), grid),
        check_vma=False,
    )
```

```python
import jax
import jax.numpy as jnp
import numpy as np
from jax import lax
from jax.experimental import pallas as pl
from jax.experimental.pallas import tpu as pltpu
from jax.sharding import Mesh
from jax.sharding import PartitionSpec as P

NX, NY, NZ = 512, 512, 256
NPX, NPY = 32, 16
ROWS, COLS = NX // NPX, NY // NPY
KZ = NZ // NPY
FRAG, NORB = 24, 8
PX = ("px_0", "px_1", "px_2")
ALL = PX + ("py",)
SCREENING, WINDOW_GAP, KINETIC_TOP = 0.002, 0.1, 6.0
STEPS = ((0, 0), (0, 1), (1, 0), (1, 1), (2, 0), (2, 1))
PADDED = COLS + 32 + FRAG
F32 = jnp.float32
BF16 = jnp.bfloat16
VMEM = pl.BlockSpec(memory_space=pltpu.VMEM)
SMEM = pl.BlockSpec(memory_space=pltpu.SMEM)


def sine_table(length):
    index = np.arange(1, length + 1, dtype=np.int64)
    product = index[:, None] * index[None, :] % (2 * length + 2)
    return np.sin(product * (np.pi / (length + 1))) * np.sqrt(2.0 / (length + 1))


def halves_of(table):
    high = np.asarray(table, np.float32).astype(BF16)
    low = (table - high.astype(np.float64)).astype(np.float32).astype(BF16)
    return high, low


def eigen_values(length):
    wave = np.arange(1, length + 1, dtype=np.float64) * (np.pi / (length + 1))
    return (4.0 * np.sin(wave / 2.0) ** 2).astype(np.float32)


SINE_Y = halves_of(sine_table(NY))
SINE_Z = np.stack(halves_of(sine_table(NZ)))
EIGEN_Y = eigen_values(NY)[None, :]
EIGEN_Z = eigen_values(NZ)[:, None]


def split2(x):
    high = x.astype(BF16)
    return high, (x - high.astype(F32)).astype(BF16)


def dot3(left, right, dims):
    def one(a, b):
        return lax.dot_general(a, b, (dims, ((), ())), preferred_element_type=F32)

    return one(left[0], right[0]) + (one(left[0], right[1]) + one(left[1], right[0]))


def call(kernel, outs, scratch=(), smem=(), count=1):
    return pl.pallas_call(
        kernel,
        out_shape=outs,
        in_specs=[SMEM if k in smem else VMEM for k in range(count)],
        out_specs=jax.tree.map(lambda _: VMEM, outs),
        scratch_shapes=list(scratch),
        compiler_params=pltpu.CompilerParams(vmem_limit_bytes=48 * 1024 * 1024),
    )


def shape(*dims):
    return jax.ShapeDtypeStruct(dims, F32)


def lanes(rows):
    return lax.broadcasted_iota(jnp.int32, (rows, 128), 1)


def rolled(x, by, axis=1):
    by %= x.shape[axis]
    return pltpu.roll(x, by, axis) if by else x


def decay(ey, ez):
    gap = ey + ez + SCREENING
    root = jnp.sqrt(gap + 0.25 * gap * gap)
    return 1.0 / (1.0 + 0.5 * gap + root), 0.5 / root


def forward_z(density, table, out):
    cells = density[...].reshape(ROWS * COLS, NZ)
    spectrum = dot3((table[0], table[1]), split2(cells), ((1,), (1,)))
    out[...] = spectrum.reshape(NPY, KZ, ROWS * COLS)


def scan_powers(place, ey, ez, power_out, weight_out, ends_out):
    rate, _ = decay(ey[...], ez[...])
    power = rate
    for _ in range(4):
        power = power * power
    before = jnp.ones((KZ, NY), F32)
    after = before
    for bit in range(5):
        upper = (place[0] >> bit) % 2 == 1
        if bit < 3:
            power_out[bit] = power
        if bit < 2:
            weight_out[bit] = jnp.where(upper, before, after)
        if bit == 2:
            ends_out[0] = before
            ends_out[1] = after
        before, after = jnp.where(upper, before * power, before), jnp.where(upper, after, after * power)
        power = power * power
    ends_out[2] = before
    ends_out[3] = after


def forward_y(tiles, table_high, table_low, ey, ez, field_out, moment_out, merged):
    block = lanes(KZ) // COLS
    for row in range(ROWS):
        for tile in range(4):
            total = None
            for k in range(4):
                piece = tiles[4 * tile + k, :, row // 4 * 128 : row // 4 * 128 + 128]
                piece = rolled(piece, (k - row % 4) * COLS)
                total = piece if total is None else jnp.where(block == k, piece, total)
            merged[row * KZ : (row + 1) * KZ, tile * 128 : (tile + 1) * 128] = total
    field = dot3(split2(merged[...]), (table_high[...], table_low[...]), ((1,), (0,)))
    field_out[...] = field
    rate, _ = decay(ey[...], ez[...])
    first = field[:KZ]
    last = field[(ROWS - 1) * KZ :]
    for row in range(1, ROWS):
        first = field[row * KZ : (row + 1) * KZ] + rate * first
        back = ROWS - 1 - row
        last = field[back * KZ : (back + 1) * KZ] + rate * last
    moment_out[:KZ] = first
    moment_out[KZ:] = last


def back_y(place, field, totals, right, left, power, ends, *rest):
    table_high, table_low, ey, ez, tiles_out, solved = rest
    rate, scale = decay(ey[...], ez[...])
    across = rate
    for _ in range(9):
        across = across * across
    across = across * rate
    norm = rate / (1.0 - across * across)
    four = power[2]
    right_total = left_total = jnp.zeros((KZ, NY), F32)
    state, after = right_total, left_total
    for k in range(NPX // 4):
        state = jnp.where(k == place[0], right_total, state)
        right_total = totals[k, :KZ] + four * right_total
    for k in range(NPX // 4 - 1, -1, -1):
        after = jnp.where(k == place[0], left_total, after)
        left_total = totals[k, KZ:] + four * left_total
    state = right[...] + ends[0] * state - norm * (left_total - across * right_total) * ends[2]
    left = left[...] + ends[1] * after - norm * (right_total - across * left_total) * ends[3]
    for row in range(ROWS):
        state = field[row * KZ : (row + 1) * KZ] + rate * state
        solved[row * KZ : (row + 1) * KZ] = state
    for row in range(ROWS - 1, -1, -1):
        here = pl.ds(row * KZ, KZ)
        solved[here] = scale * (solved[here] + rate * left)
        left = field[here] + rate * left
    columns = dot3(split2(solved[...]), (table_high[...], table_low[...]), ((1,), (0,)))
    solved[...] = columns
    block = lanes(KZ) // COLS
    for peer in range(NPY):
        for tile in range(4):
            total = None
            for k in range(4):
                row = 4 * tile + k
                piece = solved[row * KZ : (row + 1) * KZ, peer // 4 * 128 : peer // 4 * 128 + 128]
                piece = rolled(piece, (k - peer % 4) * COLS)
                total = piece if total is None else jnp.where(block == k, piece, total)
            tiles_out[peer, :, tile * 128 : (tile + 1) * 128] = total


def slots_of(rows):
    return lanes(rows) // 32


def back_z(places, tiles, external, table, field_out, *rest):
    owned, beside, grid = rest[:3], rest[3], rest[4]
    spectrum = tiles[...].reshape(NZ, ROWS * COLS)
    turned = spectrum.T
    field = dot3(split2(turned), (table[0], table[1]), ((1,), (0,)))
    field = field.reshape(ROWS, COLS, NZ)
    field_out[...] = field
    potential = field + external[...]
    for half in range(2):
        grid[half, :, :32] = jnp.zeros((ROWS, 32, 128), F32)
        grid[half, :, 32 + COLS :] = jnp.zeros((ROWS, FRAG, 128), F32)
        grid[half, :, 32 : 32 + COLS] = potential[:, :, half * 128 : half * 128 + 128]
    lane = lanes(FRAG)
    slot_of = slots_of(FRAG)
    for k, (down, along) in enumerate(STEPS):
        groups = 8 if down < 2 else 4

        def cut(number, carry, k=k, down=down, along=along, groups=groups):
            totals = []
            for part in range(4):
                total = None
                for slot in range(4):
                    frag = slot % 2
                    row = 4 * number + part + groups * (slot // 2)
                    col, depth = places[6 * k + 3 * frag + 1], places[6 * k + 3 * frag + 2]
                    cols = pl.ds(32 + col - 32 * along, FRAG)
                    window = jnp.where(lane >= depth, grid[0, row, cols, :], grid[1, row, cols, :])
                    window = pltpu.roll(window, (256 + 32 * slot - depth) & 127, 1)
                    total = window if total is None else jnp.where(slot_of == slot, window, total)
                totals.append(total)
            for part in range(4):
                if along:
                    beside[8 * down + 4 * number + part] = totals[part]
                else:
                    owned[down][4 * number + part] = totals[part]
            return carry

        lax.fori_loop(0, groups // 4, cut, 0)


def orbitals_in(orbitals, out, strips, turned):
    for frag in range(2):
        for tile in range(5):
            width = min(128, FRAG * FRAG - tile * 128)
            strips[frag, tile, :, :width] = orbitals[frag, :, tile * 128 : tile * 128 + width]
    lane = lanes(8)

    def plane(x, place):
        rows = []
        for yc in range(8):
            tile, off = divmod(72 * yc, 128)
            for frag in range(2):
                piece = rolled(strips[frag, tile, pl.ds(x, 8, stride=FRAG), :], -off)
                if off + 72 > 128:
                    other = rolled(strips[frag, tile + 1, pl.ds(x, 8, stride=FRAG), :], -off)
                    piece = jnp.where(lane < 128 - off, piece, other)
                rows.append(piece)
        place[...] = jnp.concatenate(rows, 0).T

    def planes(number, carry):
        for part in range(3):
            plane(3 * number + part, turned.at[part])
        for part in range(3):
            for k in range(9):
                rows = pl.ds(k // 3 * FRAG + k % 3, 8, stride=3)
                out[3 * number + part, k] = turned.at[part][rows, :]
        return carry

    lax.fori_loop(0, FRAG // 3, planes, 0)


def orbitals_out(planes, scale, out, strips, turned):
    lane = lanes(8)
    factor = scale[...]

    def plane(x, rows):
        for frag in range(2):
            for tile in range(5):
                total = None
                for yc in range(8):
                    start = 72 * yc - 128 * tile
                    if -72 < start < 128:
                        piece = rows[(2 * yc + frag) * 8 : (2 * yc + frag) * 8 + 8]
                        piece = rolled(piece, start)
                        if total is None:
                            total = piece
                        else:
                            total = jnp.where(lane >= start, piece, total)
                strips[frag, tile, pl.ds(x, 8, stride=FRAG), :] = total

    def trip(number, carry):
        for part in range(3):
            for k in range(9):
                rows = pl.ds(k // 3 * FRAG + k % 3, 8, stride=3)
                turned.at[part][rows, :] = planes[3 * number + part, k] * factor
        rows = [turned[part].T for part in range(3)]
        for part in range(3):
            plane(3 * number + part, rows[part])
        return carry

    lax.fori_loop(0, FRAG // 3, trip, 0)
    for frag in range(2):
        for tile in range(5):
            width = min(128, FRAG * FRAG - tile * 128)
            out[frag, :, tile * 128 : tile * 128 + width] = strips[frag, tile, :, :width]


def spread(value, lane):
    values = [value]
    for step in (4, 2, 1):
        clear = lane & step == 0
        values = [
            part
            for v in values
            for part in (
                jnp.where(clear, v, rolled(v, step)),
                jnp.where(clear, rolled(v, -step), v),
            )
        ]
    return values


def gather_sums(values, lane):
    for step in (4, 2, 1):
        clear = lane & step == 0
        count = len(values) // 2
        values = [
            jnp.where(
                clear,
                values[k] + rolled(values[k], -step),
                values[k + count] + rolled(values[k + count], step),
            )
            for k in range(count)
        ]
    return values[0]


def total_of(x):
    return jnp.sum(jnp.sum(x, axis=0, keepdims=True), axis=1, keepdims=True)


def filter_fragments(meta, *refs):
    owned, beside, next_rows, last_rows, start = refs[:5]
    out, scale_out = refs[5:7]
    shares = refs[7:10]
    boxes, turned, compact, potential, other, spilled = refs[10:]
    lane = lanes(8)
    sub = lax.broadcasted_iota(jnp.int32, (8, 128), 0)
    second = (lane // 8) % 2 == 1
    for down in range(3):
        groups = 8 if down < 2 else 4

        def unpack(number, carry, down=down, groups=groups):
            moved_windows = []
            for part in range(4):
                group = 4 * number + part
                if down == 0:
                    both = owned[group] + beside[group]
                else:
                    both = (next_rows if down == 1 else last_rows)[group]
                moved_windows.append([rolled(both, -32 * slot) for slot in range(4)])
            for part in range(4):
                for slot in range(4):
                    row = 16 * down + 4 * number + part + groups * (slot // 2)
                    rows = pl.ds(pl.multiple_of(row * FRAG, 8), FRAG)
                    boxes[slot % 2, rows, :] = moved_windows[part][slot]
            return carry

        lax.fori_loop(0, groups // 4, unpack, 0)
    lowest = None
    for part in range(3):
        rows = []
        for yc in range(8):
            for frag in range(2):
                base = (meta[frag] + 8 * part) * FRAG + 3 * yc
                took = [boxes[frag, pl.ds(base + yi, 8, stride=FRAG), :] for yi in range(3)]
                rows.append(
                    jnp.where(
                        lane < FRAG,
                        took[0],
                        jnp.where(lane < 2 * FRAG, rolled(took[1], FRAG), rolled(took[2], 2 * FRAG)),
                    )
                )
        turned[part] = jnp.concatenate(rows, 0).T
    for part in range(3):
        for k in range(9):
            value = turned.at[part][pl.ds(k // 3 * FRAG + k % 3, 8, stride=3), :]
            compact[9 * part + k] = value
            lowest = value if lowest is None else jnp.minimum(lowest, value)
            highest = value if part + k == 0 else jnp.maximum(highest, value)

    def window(keep):
        low = jnp.where(keep, lowest, jnp.inf)
        high = jnp.where(keep, highest, -jnp.inf)
        low = jnp.min(jnp.min(low, axis=0, keepdims=True), axis=1, keepdims=True) + WINDOW_GAP
        high = jnp.max(jnp.max(high, axis=0, keepdims=True), axis=1, keepdims=True) + KINETIC_TOP
        return 0.5 * (high + low), 0.5 * (high - low)

    centre_0, half_0 = window(~second)
    centre_1, half_1 = window(second)
    centre = jnp.where(second, centre_1, centre_0)
    inverse = 1.0 / jnp.where(second, half_1, half_0)
    for part in range(3):
        for k in range(9):
            value = -2.0 * (3.0 + compact[9 * part + k] - centre)
            for x, wide in enumerate(spread(value, lane)):
                potential[8 * part + x, k] = wide
    odd_scale = -inverse
    even_scale = inverse * inverse
    degree = jnp.where(second, meta[5], meta[4])

    def apply(source, target, earlier=None, initial=False, even=False, step=None):
        if step is not None:
            live, just_done = step <= degree, step == degree + 1
        earlier = target if earlier is None else earlier

        def chunk(number, carry):
            behind, here = list(carry[:9]), list(carry[9:])
            for k4 in range(8):
                x = 8 * number + k4
                ahead_x = jnp.minimum(x + 1, FRAG - 1)
                ahead = [source[ahead_x, k] for k in range(9)]
                if k4 == 7:
                    ahead = [jnp.where(x + 1 < FRAG, v, 0.0) for v in ahead]
                for k in range(9):
                    yi, zi = divmod(k, 3)
                    total = behind[k] + ahead[k]
                    if yi > 0:
                        total = total + here[k - 3]
                    else:
                        total = total + jnp.where(lane >= 16, rolled(here[6 + zi], 16), 0.0)
                    if yi < 2:
                        total = total + here[k + 3]
                    else:
                        total = total + jnp.where(lane < 112, rolled(here[zi], -16), 0.0)
                    if zi > 0:
                        total = total + here[k - 1]
                    else:
                        total = total + jnp.where(sub >= 1, rolled(here[k + 2], 1, 0), 0.0)
                    if zi < 2:
                        total = total + here[k + 1]
                    else:
                        total = total + jnp.where(sub < 7, rolled(here[k - 2], -1, 0), 0.0)
                    following = potential[x, k] * here[k] + total
                    if initial:
                        following = 0.5 * following
                    else:
                        past = earlier[x, k]
                        following = even_scale * following - past if even else following - past
                    if step is not None:
                        kept = jnp.where(just_done, odd_scale * here[k], past)
                        following = jnp.where(live, following, kept)
                    target[x, k] = following
                behind, here = here, ahead
            return tuple(behind + here)

        zero = [jnp.zeros((8, 128), F32)] * 9
        lax.fori_loop(0, 3, chunk, tuple(zero + [source[0, k] for k in range(9)]))

    apply(start, other, initial=True)
    apply(other, out, earlier=start, even=True)
    fewest = jnp.minimum(meta[4], meta[5])
    most = jnp.maximum(meta[4], meta[5])
    plain = (fewest - 2) // 2
    pairs = (most - 1) // 2

    def free_pair(pair, carry):
        apply(out, other)
        apply(other, out, even=True)
        return carry

    def held_pair(pair, carry):
        apply(out, other)
        apply(other, out, even=True, step=2 * pair + 4)
        return carry

    lax.fori_loop(0, plain, free_pair, 0)
    lax.fori_loop(plain, pairs, held_pair, 0)

    def squares(x, sums):
        return tuple(sums[k] + out[x, k] * out[x, k] for k in range(9))

    sums = lax.fori_loop(0, FRAG, squares, (jnp.zeros((8, 128), F32),) * 9)
    sums = sum(sums[1:], sums[0])
    sums = jnp.sum(sums, axis=0, keepdims=True)
    sums = jnp.broadcast_to(sums, (8, 128))
    for step in (16, 32, 64):
        sums = sums + rolled(sums, step)
    scale = jnp.sqrt(float(FRAG**3) / (sums + 1e-06))
    scale_out[...] = scale
    weight = jnp.where(second, meta[3], meta[2]).astype(F32) / NORB

    def clear(row, carry):
        for frag in range(2):
            spilled[frag, pl.ds(pl.multiple_of(row * FRAG, 8), FRAG), :] = jnp.zeros((FRAG, 128), F32)
        return carry

    lax.fori_loop(0, 40, clear, 0)
    for part in range(3):
        for k in range(9):
            values = []
            for x in range(8):
                value = out[8 * part + x, k] * scale
                values.append(value * value)
            turned.at[part][pl.ds(k // 3 * FRAG + k % 3, 8, stride=3), :] = gather_sums(values, lane) * weight
    for part in range(3):
        rows = turned[part].T
        for yc in range(8):
            for frag in range(2):
                piece = rows[(2 * yc + frag) * 8 : (2 * yc + frag) * 8 + 8]
                base = (meta[frag] + 8 * part) * FRAG + 3 * yc
                for yi in range(3):
                    spilled[frag, pl.ds(base + yi, 8, stride=FRAG), :] = rolled(piece, -FRAG * yi)
    slot_of = slots_of(FRAG)
    for down in range(3):
        groups = 8 if down < 2 else 4

        def share(number, carry, down=down, groups=groups):
            totals = []
            for part in range(4):
                total = None
                for slot in range(4):
                    row = 16 * down + 4 * number + part + groups * (slot // 2)
                    piece = spilled[slot % 2, pl.ds(pl.multiple_of(row * FRAG, 8), FRAG), :]
                    piece = rolled(piece, 32 * slot)
                    total = piece if total is None else jnp.where(slot_of == slot, piece, total)
                totals.append(total)
            for part in range(4):
                shares[down][4 * number + part] = totals[part]
            return carry

        lax.fori_loop(0, groups // 4, share, 0)


def patch(places, *refs):
    shares, beside, out, grid = refs[:3], refs[3], refs[4], refs[5]

    def clear(row, carry):
        for half in range(2):
            grid[half, row] = jnp.zeros((PADDED, 128), F32)
        return carry

    lax.fori_loop(0, ROWS, clear, 0)
    lane = lanes(FRAG)
    for k, (down, along) in enumerate(STEPS):
        groups = 8 if down < 2 else 4

        def add(number, carry, k=k, down=down, along=along, groups=groups):
            pieces = []
            for part in range(4):
                group = 4 * number + part
                both = beside[8 * down + group] if along else shares[down][group]
                for slot in range(4):
                    depth = places[6 * k + 3 * (slot % 2) + 2]
                    pieces.append(pltpu.roll(both, (256 + depth - 32 * slot) & 127, 1))
            for part in range(4):
                for slot in range(4):
                    frag = slot % 2
                    row = 4 * number + part + groups * (slot // 2)
                    col, depth = places[6 * k + 3 * frag + 1], places[6 * k + 3 * frag + 2]
                    piece = jnp.where(((lane - depth) & 127) < FRAG, pieces[4 * part + slot], 0.0)
                    cols = pl.ds(32 + col - 32 * along, FRAG)
                    grid[0, row, cols, :] += jnp.where(lane >= depth, piece, 0.0)
                    grid[1, row, cols, :] += jnp.where(lane >= depth, 0.0, piece)
            return carry

        lax.fori_loop(0, groups // 4, add, 0)
    for half in range(2):
        out[:, :, half * 128 : half * 128 + 128] = grid[half, :, 32 : 32 + COLS]


def moved(x, down, along):
    pairs = [
        (p * NPY + q, (p + down) * NPY + q + along)
        for p in range(NPX)
        for q in range(NPY)
        if 0 <= p + down < NPX and 0 <= q + along < NPY
    ]
    return lax.ppermute(x, ALL, pairs)


def body(density, external, orbitals, anchors, weights, degrees):
    row_place = lax.axis_index(PX)
    col_place = lax.axis_index("py")
    origin = jnp.stack([row_place * ROWS, col_place * COLS, 0])
    local = (anchors - origin[None, :]).astype(jnp.int32)
    own = jnp.pad(local.reshape(6), (0, 2))
    above = jnp.stack([own, moved(own, 1, 0), moved(own, 2, 0)])
    meta = jnp.concatenate([local[:, 0], weights, degrees, weights]).astype(jnp.int32)

    sine_y = [jnp.asarray(t) for t in SINE_Y]
    sine_z = jnp.asarray(SINE_Z)
    ey = jnp.asarray(EIGEN_Y)
    ez = lax.dynamic_slice(jnp.asarray(EIGEN_Z), (col_place * KZ, 0), (KZ, 1))
    ez, above = lax.optimization_barrier((ez, above))
    places = jnp.stack([above, moved(above, 0, 1)], 1)[:, :, :6].reshape(36)

    planes = call(
        orbitals_in,
        shape(FRAG, 9, 8, 128),
        [pltpu.VMEM((2, 5, NORB * FRAG, 128), F32), pltpu.VMEM((3, 128, 128), F32)],
    )(orbitals.reshape(2, NORB * FRAG, FRAG * FRAG))
    power, weight, ends = call(
        scan_powers,
        (shape(3, KZ, NY), shape(2, KZ, NY), shape(4, KZ, NY)),
        smem=(0,),
        count=3,
    )(row_place.reshape(1).astype(jnp.int32), ey, ez)

    tiles = call(forward_z, shape(NPY, KZ, ROWS * COLS), count=2)(density, sine_z)
    tiles = lax.all_to_all(tiles, "py", split_axis=0, concat_axis=0, tiled=True)
    field, totals = call(
        forward_y,
        (shape(ROWS * KZ, NY), shape(2 * KZ, NY)),
        [pltpu.VMEM((ROWS * KZ, NY), F32)],
        count=5,
    )(tiles, *sine_y, ey, ez)

    right, left = jnp.zeros((KZ, NY), F32), jnp.zeros((KZ, NY), F32)
    for bit in range(2):
        pairs = [(p * NPY + q, (p ^ (1 << bit)) * NPY + q) for p in range(NPX) for q in range(NPY)]
        got = lax.ppermute(totals, ALL, pairs)
        upper = (row_place >> bit) % 2 == 1
        high, low = jnp.where(upper, totals, got), jnp.where(upper, got, totals)
        right = right + jnp.where(upper, weight[bit] * got[:KZ], 0.0)
        left = left + jnp.where(upper, 0.0, weight[bit] * got[KZ:])
        totals = jnp.concatenate([high[:KZ] + power[bit] * low[:KZ], low[KZ:] + power[bit] * high[KZ:]])
    totals = lax.all_to_all(
        jnp.broadcast_to(totals, (NPX // 4, 2 * KZ, NY)), "px_0", split_axis=0, concat_axis=0, tiled=True
    )

    tiles = call(
        back_y,
        shape(NPY, KZ, ROWS * COLS),
        [pltpu.VMEM((ROWS * KZ, NY), F32)],
        smem=(0,),
        count=11,
    )(
        (row_place // 4).reshape(1).astype(jnp.int32), field, totals, right, left, power, ends, *sine_y, ey, ez
    )
    tiles = lax.all_to_all(tiles, "py", split_axis=0, concat_axis=0, tiled=True)
    groups = (8, 8, 4)
    hartree_field, *owned, beside = call(
        back_z,
        [shape(ROWS, COLS, NZ)] + [shape(n, FRAG, 128) for n in groups + (20,)],
        [pltpu.VMEM((2, ROWS, PADDED, 128), F32)],
        smem=(0,),
        count=4,
    )(places, tiles, external, sine_z)
    beside = moved(beside, 0, -1)
    next_rows = moved(owned[1] + beside[8:16], -1, 0)
    last_rows = moved(owned[2] + beside[16:], -2, 0)
    planes, scale, *shares = call(
        filter_fragments,
        [shape(FRAG, 9, 8, 128), shape(8, 128)] + [shape(n, FRAG, 128) for n in groups],
        [
            pltpu.VMEM((2, 40 * FRAG, 128), F32),
            pltpu.VMEM((3, 128, 128), F32),
            pltpu.VMEM((27, 8, 128), F32),
            pltpu.VMEM((FRAG, 9, 8, 128), F32),
            pltpu.VMEM((FRAG, 9, 8, 128), F32),
            pltpu.VMEM((2, 40 * FRAG, 128), F32),
        ],
        smem=(0,),
        count=6,
    )(meta, owned[0], beside, next_rows, last_rows, planes)
    received = [shares[0], moved(shares[1], 1, 0), moved(shares[2], 2, 0)]
    beside = moved(jnp.concatenate(received), 0, 1)
    filtered = call(
        orbitals_out,
        shape(2, NORB * FRAG, FRAG * FRAG),
        [pltpu.VMEM((2, 5, NORB * FRAG, 128), F32), pltpu.VMEM((3, 128, 128), F32)],
        count=2,
    )(planes, scale)
    new_density = call(
        patch,
        shape(ROWS, COLS, NZ),
        [pltpu.VMEM((2, ROWS, PADDED, 128), F32)],
        smem=(0,),
        count=5,
    )(places, *received, beside)
    return hartree_field, filtered.reshape(orbitals.shape), new_density


def solution(mesh):
    torus = Mesh(mesh.devices.reshape(8, 2, 2, NPY), ALL)
    grid = P(PX, "py", None)
    return jax.shard_map(
        body,
        mesh=torus,
        in_specs=(grid, grid, P(ALL, None, None, None), P(ALL, None), P(ALL), P(ALL)),
        out_specs=(grid, P(ALL, None, None, None), grid),
        check_vma=False,
    )
```

```python
import jax
import jax.numpy as jnp
import numpy as np
from jax import lax
from jax.experimental import pallas as pl
from jax.experimental.pallas import tpu as pltpu
from jax.sharding import Mesh
from jax.sharding import PartitionSpec as P

NX, NY, NZ = 512, 512, 256
NPX, NPY = 32, 16
ROWS, COLS = NX // NPX, NY // NPY
KZ = NZ // NPY
FRAG, NORB = 24, 8
PX = ("px_0", "px_1", "px_2")
ALL = PX + ("py",)
SCREENING, WINDOW_GAP, KINETIC_TOP = 0.002, 0.1, 6.0
STEPS = ((0, 0), (0, 1), (1, 0), (1, 1), (2, 0), (2, 1))
PADDED = COLS + 32 + FRAG
F32 = jnp.float32
BF16 = jnp.bfloat16
VMEM = pl.BlockSpec(memory_space=pltpu.VMEM)
SMEM = pl.BlockSpec(memory_space=pltpu.SMEM)


def sine_table(length):
    index = np.arange(1, length + 1, dtype=np.int64)
    product = index[:, None] * index[None, :] % (2 * length + 2)
    return np.sin(product * (np.pi / (length + 1))) * np.sqrt(2.0 / (length + 1))


def halves_of(table):
    high = np.asarray(table, np.float32).astype(BF16)
    low = (table - high.astype(np.float64)).astype(np.float32).astype(BF16)
    return high, low


def eigen_values(length):
    wave = np.arange(1, length + 1, dtype=np.float64) * (np.pi / (length + 1))
    return (4.0 * np.sin(wave / 2.0) ** 2).astype(np.float32)


SINE_Y = halves_of(sine_table(NY))
SINE_Z = np.stack(halves_of(sine_table(NZ)))
EIGEN_Y = eigen_values(NY)[None, :]
EIGEN_Z = eigen_values(NZ)[:, None]


def split2(x):
    high = x.astype(BF16)
    return high, (x - high.astype(F32)).astype(BF16)


def dot3(left, right, dims):
    def one(a, b):
        return lax.dot_general(a, b, (dims, ((), ())), preferred_element_type=F32)

    return one(left[0], right[0]) + (one(left[0], right[1]) + one(left[1], right[0]))


def call(kernel, outs, scratch=(), smem=(), count=1):
    return pl.pallas_call(
        kernel,
        out_shape=outs,
        in_specs=[SMEM if k in smem else VMEM for k in range(count)],
        out_specs=jax.tree.map(lambda _: VMEM, outs),
        scratch_shapes=list(scratch),
        compiler_params=pltpu.CompilerParams(vmem_limit_bytes=48 * 1024 * 1024),
    )


def shape(*dims):
    return jax.ShapeDtypeStruct(dims, F32)


def lanes(rows):
    return lax.broadcasted_iota(jnp.int32, (rows, 128), 1)


def rolled(x, by, axis=1):
    by %= x.shape[axis]
    return pltpu.roll(x, by, axis) if by else x


def decay(ey, ez):
    gap = ey + ez + SCREENING
    root = jnp.sqrt(gap + 0.25 * gap * gap)
    return 1.0 / (1.0 + 0.5 * gap + root), 0.5 / root


def forward_z(density, table, out):
    cells = density[...].reshape(ROWS * COLS, NZ)
    spectrum = dot3((table[0], table[1]), split2(cells), ((1,), (1,)))
    out[...] = spectrum.reshape(NPY, KZ, ROWS * COLS)


def scan_powers(place, ey, ez, power_out, weight_out, ends_out):
    rate, _ = decay(ey[...], ez[...])
    power = rate
    for _ in range(4):
        power = power * power
    before = jnp.ones((KZ, NY), F32)
    after = before
    for bit in range(5):
        upper = (place[0] >> bit) % 2 == 1
        power_out[bit] = power
        weight_out[bit] = jnp.where(upper, before, after)
        before, after = jnp.where(upper, before * power, before), jnp.where(upper, after, after * power)
        power = power * power
    ends_out[0] = before
    ends_out[1] = after


def forward_y(tiles, table_high, table_low, ey, ez, field_out, moment_out, merged):
    block = lanes(KZ) // COLS
    for row in range(ROWS):
        for tile in range(4):
            total = None
            for k in range(4):
                piece = tiles[4 * tile + k, :, row // 4 * 128 : row // 4 * 128 + 128]
                piece = rolled(piece, (k - row % 4) * COLS)
                total = piece if total is None else jnp.where(block == k, piece, total)
            merged[row * KZ : (row + 1) * KZ, tile * 128 : (tile + 1) * 128] = total
    field = dot3(split2(merged[...]), (table_high[...], table_low[...]), ((1,), (0,)))
    field_out[...] = field
    rate, _ = decay(ey[...], ez[...])
    first = field[:KZ]
    last = field[(ROWS - 1) * KZ :]
    for row in range(1, ROWS):
        first = field[row * KZ : (row + 1) * KZ] + rate * first
        back = ROWS - 1 - row
        last = field[back * KZ : (back + 1) * KZ] + rate * last
    moment_out[:KZ] = first
    moment_out[KZ:] = last


def back_y(field, totals, right, left, ends, table_high, table_low, ey, ez, tiles_out, solved):
    rate, scale = decay(ey[...], ez[...])
    across = rate
    for _ in range(9):
        across = across * across
    across = across * rate
    norm = rate / (1.0 - across * across)
    right_total, left_total = totals[:KZ], totals[KZ:]
    state = right[...] - norm * (left_total - across * right_total) * ends[0]
    left = left[...] - norm * (right_total - across * left_total) * ends[1]
    for row in range(ROWS):
        state = field[row * KZ : (row + 1) * KZ] + rate * state
        solved[row * KZ : (row + 1) * KZ] = state
    for row in range(ROWS - 1, -1, -1):
        here = pl.ds(row * KZ, KZ)
        solved[here] = scale * (solved[here] + rate * left)
        left = field[here] + rate * left
    columns = dot3(split2(solved[...]), (table_high[...], table_low[...]), ((1,), (0,)))
    solved[...] = columns
    block = lanes(KZ) // COLS
    for peer in range(NPY):
        for tile in range(4):
            total = None
            for k in range(4):
                row = 4 * tile + k
                piece = solved[row * KZ : (row + 1) * KZ, peer // 4 * 128 : peer // 4 * 128 + 128]
                piece = rolled(piece, (k - peer % 4) * COLS)
                total = piece if total is None else jnp.where(block == k, piece, total)
            tiles_out[peer, :, tile * 128 : (tile + 1) * 128] = total


def slots_of(rows):
    return lanes(rows) // 32


def fill_grid(grid, potential):
    for half in range(2):
        grid[half, :, :32] = jnp.zeros((ROWS, 32, 128), F32)
        grid[half, :, 32 + COLS :] = jnp.zeros((ROWS, FRAG, 128), F32)
        grid[half, :, 32 : 32 + COLS] = potential[:, :, half * 128 : half * 128 + 128]


def cut_windows(places, grid, along, outs):
    lane = lanes(FRAG)
    slot_of = slots_of(FRAG)
    for down in range(3):
        groups = 8 if down < 2 else 4
        k = 2 * down + along

        def cut(number, carry, k=k, down=down, groups=groups):
            totals = []
            for part in range(4):
                total = None
                for slot in range(4):
                    frag = slot % 2
                    row = 4 * number + part + groups * (slot // 2)
                    col, depth = places[6 * k + 3 * frag + 1], places[6 * k + 3 * frag + 2]
                    cols = pl.ds(32 + col - 32 * along, FRAG)
                    window = jnp.where(lane >= depth, grid[0, row, cols, :], grid[1, row, cols, :])
                    window = pltpu.roll(window, (256 + 32 * slot - depth) & 127, 1)
                    total = window if total is None else jnp.where(slot_of == slot, window, total)
                totals.append(total)
            for part in range(4):
                if along:
                    outs[0][8 * down + 4 * number + part] = totals[part]
                else:
                    outs[down][4 * number + part] = totals[part]
            return carry

        lax.fori_loop(0, groups // 4, cut, 0)


def back_z(places, tiles, external, table, field_out, beside, grid):
    spectrum = tiles[...].reshape(NZ, ROWS * COLS)
    turned = spectrum.T
    field = dot3(split2(turned), (table[0], table[1]), ((1,), (0,)))
    field = field.reshape(ROWS, COLS, NZ)
    field_out[...] = field
    fill_grid(grid, field + external[...])
    cut_windows(places, grid, 1, (beside,))


def cut_owned(places, field, external, *rest):
    fill_grid(rest[3], field[...] + external[...])
    cut_windows(places, rest[3], 0, rest[:3])


def orbitals_in(orbitals, out, strips, turned):
    for frag in range(2):
        for tile in range(5):
            width = min(128, FRAG * FRAG - tile * 128)
            strips[frag, tile, :, :width] = orbitals[frag, :, tile * 128 : tile * 128 + width]
    lane = lanes(8)

    def plane(x, place):
        rows = []
        for yc in range(8):
            tile, off = divmod(72 * yc, 128)
            for frag in range(2):
                piece = rolled(strips[frag, tile, pl.ds(x, 8, stride=FRAG), :], -off)
                if off + 72 > 128:
                    other = rolled(strips[frag, tile + 1, pl.ds(x, 8, stride=FRAG), :], -off)
                    piece = jnp.where(lane < 128 - off, piece, other)
                rows.append(piece)
        place[...] = jnp.concatenate(rows, 0).T

    def planes(number, carry):
        for part in range(3):
            plane(3 * number + part, turned.at[part])
        for part in range(3):
            for k in range(9):
                rows = pl.ds(k // 3 * FRAG + k % 3, 8, stride=3)
                out[3 * number + part, k] = turned.at[part][rows, :]
        return carry

    lax.fori_loop(0, FRAG // 3, planes, 0)


def orbitals_out(planes, scale, out, strips, turned):
    lane = lanes(8)
    factor = scale[...]

    def plane(x, rows):
        for frag in range(2):
            for tile in range(5):
                total = None
                for yc in range(8):
                    start = 72 * yc - 128 * tile
                    if -72 < start < 128:
                        piece = rows[(2 * yc + frag) * 8 : (2 * yc + frag) * 8 + 8]
                        piece = rolled(piece, start)
                        if total is None:
                            total = piece
                        else:
                            total = jnp.where(lane >= start, piece, total)
                strips[frag, tile, pl.ds(x, 8, stride=FRAG), :] = total

    def trip(number, carry):
        for part in range(3):
            for k in range(9):
                rows = pl.ds(k // 3 * FRAG + k % 3, 8, stride=3)
                turned.at[part][rows, :] = planes[3 * number + part, k] * factor
        rows = [turned[part].T for part in range(3)]
        for part in range(3):
            plane(3 * number + part, rows[part])
        return carry

    lax.fori_loop(0, FRAG // 3, trip, 0)
    for frag in range(2):
        for tile in range(5):
            width = min(128, FRAG * FRAG - tile * 128)
            out[frag, :, tile * 128 : tile * 128 + width] = strips[frag, tile, :, :width]


def spread(value, lane):
    values = [value]
    for step in (4, 2, 1):
        clear = lane & step == 0
        values = [
            part
            for v in values
            for part in (
                jnp.where(clear, v, rolled(v, step)),
                jnp.where(clear, rolled(v, -step), v),
            )
        ]
    return values


def gather_sums(values, lane):
    for step in (4, 2, 1):
        clear = lane & step == 0
        count = len(values) // 2
        values = [
            jnp.where(
                clear,
                values[k] + rolled(values[k], -step),
                values[k + count] + rolled(values[k + count], step),
            )
            for k in range(count)
        ]
    return values[0]


def total_of(x):
    return jnp.sum(jnp.sum(x, axis=0, keepdims=True), axis=1, keepdims=True)


def filter_fragments(meta, *refs):
    owned, beside, next_rows, last_rows, start = refs[:5]
    out, scale_out = refs[5:7]
    shares = refs[7:10]
    boxes, turned, compact, potential, other, spilled = refs[10:]
    lane = lanes(8)
    sub = lax.broadcasted_iota(jnp.int32, (8, 128), 0)
    second = (lane // 8) % 2 == 1
    for down in range(3):
        groups = 8 if down < 2 else 4

        def unpack(number, carry, down=down, groups=groups):
            moved_windows = []
            for part in range(4):
                group = 4 * number + part
                if down == 0:
                    both = owned[group] + beside[group]
                else:
                    both = (next_rows if down == 1 else last_rows)[group]
                moved_windows.append([rolled(both, -32 * slot) for slot in range(4)])
            for part in range(4):
                for slot in range(4):
                    row = 16 * down + 4 * number + part + groups * (slot // 2)
                    rows = pl.ds(pl.multiple_of(row * FRAG, 8), FRAG)
                    boxes[slot % 2, rows, :] = moved_windows[part][slot]
            return carry

        lax.fori_loop(0, groups // 4, unpack, 0)
    lowest = None
    for part in range(3):
        rows = []
        for yc in range(8):
            for frag in range(2):
                base = (meta[frag] + 8 * part) * FRAG + 3 * yc
                took = [boxes[frag, pl.ds(base + yi, 8, stride=FRAG), :] for yi in range(3)]
                rows.append(
                    jnp.where(
                        lane < FRAG,
                        took[0],
                        jnp.where(lane < 2 * FRAG, rolled(took[1], FRAG), rolled(took[2], 2 * FRAG)),
                    )
                )
        turned[part] = jnp.concatenate(rows, 0).T
    for part in range(3):
        for k in range(9):
            value = turned.at[part][pl.ds(k // 3 * FRAG + k % 3, 8, stride=3), :]
            compact[9 * part + k] = value
            lowest = value if lowest is None else jnp.minimum(lowest, value)
            highest = value if part + k == 0 else jnp.maximum(highest, value)

    def window(keep):
        low = jnp.where(keep, lowest, jnp.inf)
        high = jnp.where(keep, highest, -jnp.inf)
        low = jnp.min(jnp.min(low, axis=0, keepdims=True), axis=1, keepdims=True) + WINDOW_GAP
        high = jnp.max(jnp.max(high, axis=0, keepdims=True), axis=1, keepdims=True) + KINETIC_TOP
        return 0.5 * (high + low), 0.5 * (high - low)

    centre_0, half_0 = window(~second)
    centre_1, half_1 = window(second)
    centre = jnp.where(second, centre_1, centre_0)
    inverse = 1.0 / jnp.where(second, half_1, half_0)
    for part in range(3):
        for k in range(9):
            value = -2.0 * (3.0 + compact[9 * part + k] - centre)
            for x, wide in enumerate(spread(value, lane)):
                potential[8 * part + x, k] = wide
    odd_scale = -inverse
    even_scale = inverse * inverse
    degree = jnp.where(second, meta[5], meta[4])

    def apply(source, target, earlier=None, initial=False, even=False, step=None):
        if step is not None:
            live, just_done = step <= degree, step == degree + 1
        earlier = target if earlier is None else earlier

        def chunk(number, carry):
            behind, here = list(carry[:9]), list(carry[9:])
            for k4 in range(8):
                x = 8 * number + k4
                ahead_x = jnp.minimum(x + 1, FRAG - 1)
                ahead = [source[ahead_x, k] for k in range(9)]
                if k4 == 7:
                    ahead = [jnp.where(x + 1 < FRAG, v, 0.0) for v in ahead]
                for k in range(9):
                    yi, zi = divmod(k, 3)
                    total = behind[k] + ahead[k]
                    if yi > 0:
                        total = total + here[k - 3]
                    else:
                        total = total + jnp.where(lane >= 16, rolled(here[6 + zi], 16), 0.0)
                    if yi < 2:
                        total = total + here[k + 3]
                    else:
                        total = total + jnp.where(lane < 112, rolled(here[zi], -16), 0.0)
                    if zi > 0:
                        total = total + here[k - 1]
                    else:
                        total = total + jnp.where(sub >= 1, rolled(here[k + 2], 1, 0), 0.0)
                    if zi < 2:
                        total = total + here[k + 1]
                    else:
                        total = total + jnp.where(sub < 7, rolled(here[k - 2], -1, 0), 0.0)
                    following = potential[x, k] * here[k] + total
                    if initial:
                        following = 0.5 * following
                    else:
                        past = earlier[x, k]
                        following = even_scale * following - past if even else following - past
                    if step is not None:
                        kept = jnp.where(just_done, odd_scale * here[k], past)
                        following = jnp.where(live, following, kept)
                    target[x, k] = following
                behind, here = here, ahead
            return tuple(behind + here)

        zero = [jnp.zeros((8, 128), F32)] * 9
        lax.fori_loop(0, 3, chunk, tuple(zero + [source[0, k] for k in range(9)]))

    apply(start, other, initial=True)
    apply(other, out, earlier=start, even=True)
    fewest = jnp.minimum(meta[4], meta[5])
    most = jnp.maximum(meta[4], meta[5])
    plain = (fewest - 2) // 2
    pairs = (most - 1) // 2

    def free_pair(pair, carry):
        apply(out, other)
        apply(other, out, even=True)
        return carry

    def held_pair(pair, carry):
        apply(out, other)
        apply(other, out, even=True, step=2 * pair + 4)
        return carry

    lax.fori_loop(0, plain, free_pair, 0)
    lax.fori_loop(plain, pairs, held_pair, 0)

    def squares(x, sums):
        return tuple(sums[k] + out[x, k] * out[x, k] for k in range(9))

    sums = lax.fori_loop(0, FRAG, squares, (jnp.zeros((8, 128), F32),) * 9)
    sums = sum(sums[1:], sums[0])
    sums = jnp.sum(sums, axis=0, keepdims=True)
    sums = jnp.broadcast_to(sums, (8, 128))
    for step in (16, 32, 64):
        sums = sums + rolled(sums, step)
    scale = jnp.sqrt(float(FRAG**3) / (sums + 1e-06))
    scale_out[...] = scale
    weight = jnp.where(second, meta[3], meta[2]).astype(F32) / NORB

    def clear(row, carry):
        for frag in range(2):
            spilled[frag, pl.ds(pl.multiple_of(row * FRAG, 8), FRAG), :] = jnp.zeros((FRAG, 128), F32)
        return carry

    lax.fori_loop(0, 40, clear, 0)
    for part in range(3):
        for k in range(9):
            values = []
            for x in range(8):
                value = out[8 * part + x, k] * scale
                values.append(value * value)
            turned.at[part][pl.ds(k // 3 * FRAG + k % 3, 8, stride=3), :] = gather_sums(values, lane) * weight
    for part in range(3):
        rows = turned[part].T
        for yc in range(8):
            for frag in range(2):
                piece = rows[(2 * yc + frag) * 8 : (2 * yc + frag) * 8 + 8]
                base = (meta[frag] + 8 * part) * FRAG + 3 * yc
                for yi in range(3):
                    spilled[frag, pl.ds(base + yi, 8, stride=FRAG), :] = rolled(piece, -FRAG * yi)
    slot_of = slots_of(FRAG)
    for down in range(3):
        groups = 8 if down < 2 else 4

        def share(number, carry, down=down, groups=groups):
            totals = []
            for part in range(4):
                total = None
                for slot in range(4):
                    row = 16 * down + 4 * number + part + groups * (slot // 2)
                    piece = spilled[slot % 2, pl.ds(pl.multiple_of(row * FRAG, 8), FRAG), :]
                    piece = rolled(piece, 32 * slot)
                    total = piece if total is None else jnp.where(slot_of == slot, piece, total)
                totals.append(total)
            for part in range(4):
                shares[down][4 * number + part] = totals[part]
            return carry

        lax.fori_loop(0, groups // 4, share, 0)


def add_windows(places, grid, along, shares):
    lane = lanes(FRAG)
    for down in range(3):
        groups = 8 if down < 2 else 4
        k = 2 * down + along

        def add(number, carry, k=k, down=down, groups=groups):
            pieces = []
            for part in range(4):
                group = 4 * number + part
                both = shares[0][8 * down + group] if along else shares[down][group]
                for slot in range(4):
                    depth = places[6 * k + 3 * (slot % 2) + 2]
                    pieces.append(pltpu.roll(both, (256 + depth - 32 * slot) & 127, 1))
            for part in range(4):
                for slot in range(4):
                    frag = slot % 2
                    row = 4 * number + part + groups * (slot // 2)
                    col, depth = places[6 * k + 3 * frag + 1], places[6 * k + 3 * frag + 2]
                    piece = jnp.where(((lane - depth) & 127) < FRAG, pieces[4 * part + slot], 0.0)
                    cols = pl.ds(32 + col - 32 * along, FRAG)
                    grid[0, row, cols, :] += jnp.where(lane >= depth, piece, 0.0)
                    grid[1, row, cols, :] += jnp.where(lane >= depth, 0.0, piece)
            return carry

        lax.fori_loop(0, groups // 4, add, 0)


def patch_owned(places, first, second, third, out, grid):
    def clear(row, carry):
        for half in range(2):
            grid[half, row] = jnp.zeros((PADDED, 128), F32)
        return carry

    lax.fori_loop(0, ROWS, clear, 0)
    add_windows(places, grid, 0, (first, second, third))
    for half in range(2):
        out[:, :, half * 128 : half * 128 + 128] = grid[half, :, 32 : 32 + COLS]


def patch_beside(places, owned, beside, out, grid):
    fill_grid(grid, owned[...])
    add_windows(places, grid, 1, (beside,))
    for half in range(2):
        out[:, :, half * 128 : half * 128 + 128] = grid[half, :, 32 : 32 + COLS]


def moved(x, down, along):
    pairs = [
        (p * NPY + q, (p + down) * NPY + q + along)
        for p in range(NPX)
        for q in range(NPY)
        if 0 <= p + down < NPX and 0 <= q + along < NPY
    ]
    return lax.ppermute(x, ALL, pairs)


def body(density, external, orbitals, anchors, weights, degrees):
    row_place = lax.axis_index(PX)
    col_place = lax.axis_index("py")
    origin = jnp.stack([row_place * ROWS, col_place * COLS, 0])
    local = (anchors - origin[None, :]).astype(jnp.int32)
    own = jnp.pad(local.reshape(6), (0, 2))
    above = jnp.stack([own, moved(own, 1, 0), moved(own, 2, 0)])
    meta = jnp.concatenate([local[:, 0], weights, degrees, weights]).astype(jnp.int32)

    sine_y = [jnp.asarray(t) for t in SINE_Y]
    sine_z = jnp.asarray(SINE_Z)
    ey = jnp.asarray(EIGEN_Y)
    ez = lax.dynamic_slice(jnp.asarray(EIGEN_Z), (col_place * KZ, 0), (KZ, 1))
    ez, above = lax.optimization_barrier((ez, above))
    places = jnp.stack([above, moved(above, 0, 1)], 1)[:, :, :6].reshape(36)

    planes = call(
        orbitals_in,
        shape(FRAG, 9, 8, 128),
        [pltpu.VMEM((2, 5, NORB * FRAG, 128), F32), pltpu.VMEM((3, 128, 128), F32)],
    )(orbitals.reshape(2, NORB * FRAG, FRAG * FRAG))
    power, weight, ends = call(
        scan_powers,
        (shape(5, KZ, NY), shape(5, KZ, NY), shape(2, KZ, NY)),
        smem=(0,),
        count=3,
    )(row_place.reshape(1).astype(jnp.int32), ey, ez)

    tiles = call(forward_z, shape(NPY, KZ, ROWS * COLS), count=2)(density, sine_z)
    tiles = lax.all_to_all(tiles, "py", split_axis=0, concat_axis=0, tiled=True)
    field, totals = call(
        forward_y,
        (shape(ROWS * KZ, NY), shape(2 * KZ, NY)),
        [pltpu.VMEM((ROWS * KZ, NY), F32)],
        count=5,
    )(tiles, *sine_y, ey, ez)

    right, left = jnp.zeros((KZ, NY), F32), jnp.zeros((KZ, NY), F32)
    for bit, partner in enumerate((1, 2, 4, 8, 24)):
        pairs = [(p * NPY + q, (p ^ partner) * NPY + q) for p in range(NPX) for q in range(NPY)]
        got = lax.ppermute(totals, ALL, pairs)
        upper = (row_place >> bit) % 2 == 1
        high, low = jnp.where(upper, totals, got), jnp.where(upper, got, totals)
        right = right + jnp.where(upper, weight[bit] * got[:KZ], 0.0)
        left = left + jnp.where(upper, 0.0, weight[bit] * got[KZ:])
        totals = jnp.concatenate([high[:KZ] + power[bit] * low[:KZ], low[KZ:] + power[bit] * high[KZ:]])

    tiles = call(back_y, shape(NPY, KZ, ROWS * COLS), [pltpu.VMEM((ROWS * KZ, NY), F32)], count=9)(
        field, totals, right, left, ends, *sine_y, ey, ez
    )
    tiles = lax.all_to_all(tiles, "py", split_axis=0, concat_axis=0, tiled=True)
    groups = (8, 8, 4)
    grid = [pltpu.VMEM((2, ROWS, PADDED, 128), F32)]
    hartree_field, beside = call(
        back_z, [shape(ROWS, COLS, NZ), shape(20, FRAG, 128)], grid, smem=(0,), count=4
    )(places, tiles, external, sine_z)
    owned = call(cut_owned, [shape(n, FRAG, 128) for n in groups], grid, smem=(0,), count=3)(
        places, hartree_field, external
    )
    beside = moved(beside, 0, -1)
    next_rows = moved(owned[1] + beside[8:16], -1, 0)
    last_rows = moved(owned[2] + beside[16:], -2, 0)
    planes, scale, *shares = call(
        filter_fragments,
        [shape(FRAG, 9, 8, 128), shape(8, 128)] + [shape(n, FRAG, 128) for n in groups],
        [
            pltpu.VMEM((2, 40 * FRAG, 128), F32),
            pltpu.VMEM((3, 128, 128), F32),
            pltpu.VMEM((27, 8, 128), F32),
            pltpu.VMEM((FRAG, 9, 8, 128), F32),
            pltpu.VMEM((FRAG, 9, 8, 128), F32),
            pltpu.VMEM((2, 40 * FRAG, 128), F32),
        ],
        smem=(0,),
        count=6,
    )(meta, owned[0], beside, next_rows, last_rows, planes)
    received = [shares[0], moved(shares[1], 1, 0), moved(shares[2], 2, 0)]
    beside = moved(jnp.concatenate(received), 0, 1)
    filtered = call(
        orbitals_out,
        shape(2, NORB * FRAG, FRAG * FRAG),
        [pltpu.VMEM((2, 5, NORB * FRAG, 128), F32), pltpu.VMEM((3, 128, 128), F32)],
        count=2,
    )(planes, scale)
    density_owned = call(patch_owned, shape(ROWS, COLS, NZ), grid, smem=(0,), count=4)(places, *received)
    new_density = call(patch_beside, shape(ROWS, COLS, NZ), grid, smem=(0,), count=3)(
        places, density_owned, beside
    )
    return hartree_field, filtered.reshape(orbitals.shape), new_density


def solution(mesh):
    torus = Mesh(mesh.devices.reshape(8, 2, 2, NPY), ALL)
    grid = P(PX, "py", None)
    return jax.shard_map(
        body,
        mesh=torus,
        in_specs=(grid, grid, P(ALL, None, None, None), P(ALL, None), P(ALL), P(ALL)),
        out_specs=(grid, P(ALL, None, None, None), grid),
        check_vma=False,
    )
```

```python
import jax
import jax.numpy as jnp
import numpy as np
from jax import lax
from jax.experimental import pallas as pl
from jax.experimental.pallas import tpu as pltpu
from jax.sharding import Mesh
from jax.sharding import PartitionSpec as P

NX, NY, NZ = 512, 512, 256
NPX, NPY = 32, 16
ROWS, COLS = NX // NPX, NY // NPY
KZ = NZ // NPY
FRAG, NORB = 24, 8
PX = ("px_0", "px_1", "px_2")
ALL = PX + ("py",)
SCREENING, WINDOW_GAP, KINETIC_TOP = 0.002, 0.1, 6.0
STEPS = ((0, 0), (0, 1), (1, 0), (1, 1), (2, 0), (2, 1))
PADDED = COLS + 32 + FRAG
F32 = jnp.float32
BF16 = jnp.bfloat16
VMEM = pl.BlockSpec(memory_space=pltpu.VMEM)
SMEM = pl.BlockSpec(memory_space=pltpu.SMEM)


def sine_table(length):
    index = np.arange(1, length + 1, dtype=np.int64)
    product = index[:, None] * index[None, :] % (2 * length + 2)
    return np.sin(product * (np.pi / (length + 1))) * np.sqrt(2.0 / (length + 1))


def halves_of(table):
    high = np.asarray(table, np.float32).astype(BF16)
    low = (table - high.astype(np.float64)).astype(np.float32).astype(BF16)
    return high, low


def eigen_values(length):
    wave = np.arange(1, length + 1, dtype=np.float64) * (np.pi / (length + 1))
    return (4.0 * np.sin(wave / 2.0) ** 2).astype(np.float32)


SINE_Y = halves_of(sine_table(NY))
SINE_Z = np.stack(halves_of(sine_table(NZ)))
EIGEN_Y = eigen_values(NY)[None, :]
EIGEN_Z = eigen_values(NZ)[:, None]


def split2(x):
    high = x.astype(BF16)
    return high, (x - high.astype(F32)).astype(BF16)


def dot3(left, right, dims):
    def one(a, b):
        return lax.dot_general(a, b, (dims, ((), ())), preferred_element_type=F32)

    return one(left[0], right[0]) + (one(left[0], right[1]) + one(left[1], right[0]))


def call(kernel, outs, scratch=(), smem=(), count=1):
    return pl.pallas_call(
        kernel,
        out_shape=outs,
        in_specs=[SMEM if k in smem else VMEM for k in range(count)],
        out_specs=jax.tree.map(lambda _: VMEM, outs),
        scratch_shapes=list(scratch),
        compiler_params=pltpu.CompilerParams(vmem_limit_bytes=48 * 1024 * 1024),
    )


def shape(*dims):
    return jax.ShapeDtypeStruct(dims, F32)


def lanes(rows):
    return lax.broadcasted_iota(jnp.int32, (rows, 128), 1)


def rolled(x, by, axis=1):
    by %= x.shape[axis]
    return pltpu.roll(x, by, axis) if by else x


def decay(ey, ez):
    gap = ey + ez + SCREENING
    root = jnp.sqrt(gap + 0.25 * gap * gap)
    return 1.0 / (1.0 + 0.5 * gap + root), 0.5 / root


def forward_z(density, table, out):
    cells = density[...].reshape(ROWS * COLS, NZ)
    spectrum = dot3((table[0], table[1]), split2(cells), ((1,), (1,)))
    out[...] = spectrum.reshape(NPY, KZ, ROWS * COLS)


def block_power(rate):
    for _ in range(4):
        rate = rate * rate
    return rate


def put_rows(ref, first, value):
    for half in range(2):
        for k in range(4):
            rows = pl.ds(64 * half + first + k, 8, stride=8)
            ref[rows, :] = value[8 * half : 8 * half + 8, 128 * k : 128 * k + 128]


def take_rows(ref, first):
    return jnp.concatenate(
        [
            jnp.concatenate(
                [ref[pl.ds(64 * half + first + k, 8, stride=8), :] for half in range(2)], 0
            )
            for k in range(4)
        ],
        1,
    )


def pair_moments(core, own, other, ey, ez, out):
    power = block_power(decay(ey[...], ez[...])[0])
    upper = core[0] == 1
    high = jnp.where(upper, own[...], other[...])
    low = jnp.where(upper, other[...], own[...])
    put_rows(out, 0, high[:KZ] + power * low[:KZ])
    put_rows(out, 4, low[KZ:] + power * high[KZ:])


def scan_chips(moments, ey, ez, out):
    rate, _ = decay(ey[...], ez[...])
    power = block_power(rate)
    power = power * power
    right, left = take_rows(moments, 0), take_rows(moments, 4)
    count = NPX // 2
    row = lax.broadcasted_iota(jnp.int32, (count, NY), 0)
    before, after = jnp.ones((count, NY), F32), jnp.ones((count, NY), F32)
    step = 1
    while step < count:
        right = right + power * jnp.where(row >= step, rolled(right, step, 0), 0.0)
        left = left + power * jnp.where(row < count - step, rolled(left, -step, 0), 0.0)
        upper = row & step != 0
        before = jnp.where(upper, before * power, before)
        after = jnp.where(upper, after, after * power)
        power = power * power
        step *= 2
    across = power * rate
    norm = rate / (1.0 - across * across)
    right_total, left_total = right[count - 1 :], left[:1]
    state = jnp.where(row >= 1, rolled(right, 1, 0), 0.0)
    put_rows(out, 0, state - norm * (left_total - across * right_total) * before)
    state = jnp.where(row < count - 1, rolled(left, -1, 0), 0.0)
    put_rows(out, 4, state - norm * (right_total - across * left_total) * after)


def forward_y(tiles, table_high, table_low, ey, ez, field_out, moment_out, merged):
    block = lanes(KZ) // COLS
    for row in range(ROWS):
        for tile in range(4):
            total = None
            for k in range(4):
                piece = tiles[4 * tile + k, :, row // 4 * 128 : row // 4 * 128 + 128]
                piece = rolled(piece, (k - row % 4) * COLS)
                total = piece if total is None else jnp.where(block == k, piece, total)
            merged[row * KZ : (row + 1) * KZ, tile * 128 : (tile + 1) * 128] = total
    field = dot3(split2(merged[...]), (table_high[...], table_low[...]), ((1,), (0,)))
    field_out[...] = field
    rate, _ = decay(ey[...], ez[...])
    first = field[:KZ]
    last = field[(ROWS - 1) * KZ :]
    for row in range(1, ROWS):
        first = field[row * KZ : (row + 1) * KZ] + rate * first
        back = ROWS - 1 - row
        last = field[back * KZ : (back + 1) * KZ] + rate * last
    moment_out[:KZ] = first
    moment_out[KZ:] = last


def back_y(core, field, other, states, table_high, table_low, ey, ez, tiles_out, solved):
    rate, scale = decay(ey[...], ez[...])
    power = block_power(rate)
    upper = core[0] == 1
    state, left = take_rows(states, 0), take_rows(states, 4)
    state = jnp.where(upper, other[:KZ] + power * state, state)
    left = jnp.where(upper, left, other[KZ:] + power * left)
    for row in range(ROWS):
        state = field[row * KZ : (row + 1) * KZ] + rate * state
        solved[row * KZ : (row + 1) * KZ] = state
    for row in range(ROWS - 1, -1, -1):
        here = pl.ds(row * KZ, KZ)
        solved[here] = scale * (solved[here] + rate * left)
        left = field[here] + rate * left
    columns = dot3(split2(solved[...]), (table_high[...], table_low[...]), ((1,), (0,)))
    solved[...] = columns
    block = lanes(KZ) // COLS
    for peer in range(NPY):
        for tile in range(4):
            total = None
            for k in range(4):
                row = 4 * tile + k
                piece = solved[row * KZ : (row + 1) * KZ, peer // 4 * 128 : peer // 4 * 128 + 128]
                piece = rolled(piece, (k - peer % 4) * COLS)
                total = piece if total is None else jnp.where(block == k, piece, total)
            tiles_out[peer, :, tile * 128 : (tile + 1) * 128] = total


def slots_of(rows):
    return lanes(rows) // 32


def fill_grid(grid, potential):
    for half in range(2):
        grid[half, :, :32] = jnp.zeros((ROWS, 32, 128), F32)
        grid[half, :, 32 + COLS :] = jnp.zeros((ROWS, FRAG, 128), F32)
        grid[half, :, 32 : 32 + COLS] = potential[:, :, half * 128 : half * 128 + 128]


def cut_windows(places, grid, along, outs):
    lane = lanes(FRAG)
    slot_of = slots_of(FRAG)
    for down in range(3):
        groups = 8 if down < 2 else 4
        k = 2 * down + along

        def cut(number, carry, k=k, down=down, groups=groups):
            totals = []
            for part in range(4):
                total = None
                for slot in range(4):
                    frag = slot % 2
                    row = 4 * number + part + groups * (slot // 2)
                    col, depth = places[6 * k + 3 * frag + 1], places[6 * k + 3 * frag + 2]
                    cols = pl.ds(32 + col - 32 * along, FRAG)
                    window = jnp.where(lane >= depth, grid[0, row, cols, :], grid[1, row, cols, :])
                    window = pltpu.roll(window, (256 + 32 * slot - depth) & 127, 1)
                    total = window if total is None else jnp.where(slot_of == slot, window, total)
                totals.append(total)
            for part in range(4):
                if along:
                    outs[0][8 * down + 4 * number + part] = totals[part]
                else:
                    outs[down][4 * number + part] = totals[part]
            return carry

        lax.fori_loop(0, groups // 4, cut, 0)


def back_z(places, tiles, external, table, field_out, beside, grid):
    spectrum = tiles[...].reshape(NZ, ROWS * COLS)
    turned = spectrum.T
    field = dot3(split2(turned), (table[0], table[1]), ((1,), (0,)))
    field = field.reshape(ROWS, COLS, NZ)
    field_out[...] = field
    fill_grid(grid, field + external[...])
    cut_windows(places, grid, 1, (beside,))


def cut_owned(places, field, external, *rest):
    fill_grid(rest[3], field[...] + external[...])
    cut_windows(places, rest[3], 0, rest[:3])


def orbitals_in(orbitals, out, strips, turned):
    for frag in range(2):
        for tile in range(5):
            width = min(128, FRAG * FRAG - tile * 128)
            strips[frag, tile, :, :width] = orbitals[frag, :, tile * 128 : tile * 128 + width]
    lane = lanes(8)

    def plane(x, place):
        rows = []
        for yc in range(8):
            tile, off = divmod(72 * yc, 128)
            for frag in range(2):
                piece = rolled(strips[frag, tile, pl.ds(x, 8, stride=FRAG), :], -off)
                if off + 72 > 128:
                    other = rolled(strips[frag, tile + 1, pl.ds(x, 8, stride=FRAG), :], -off)
                    piece = jnp.where(lane < 128 - off, piece, other)
                rows.append(piece)
        place[...] = jnp.concatenate(rows, 0).T

    def planes(number, carry):
        for part in range(3):
            plane(3 * number + part, turned.at[part])
        for part in range(3):
            for k in range(9):
                rows = pl.ds(k // 3 * FRAG + k % 3, 8, stride=3)
                out[3 * number + part, k] = turned.at[part][rows, :]
        return carry

    lax.fori_loop(0, FRAG // 3, planes, 0)


def orbitals_out(planes, scale, out, strips, turned):
    lane = lanes(8)
    factor = scale[...]

    def plane(x, rows):
        for frag in range(2):
            for tile in range(5):
                total = None
                for yc in range(8):
                    start = 72 * yc - 128 * tile
                    if -72 < start < 128:
                        piece = rows[(2 * yc + frag) * 8 : (2 * yc + frag) * 8 + 8]
                        piece = rolled(piece, start)
                        if total is None:
                            total = piece
                        else:
                            total = jnp.where(lane >= start, piece, total)
                strips[frag, tile, pl.ds(x, 8, stride=FRAG), :] = total

    def trip(number, carry):
        for part in range(3):
            for k in range(9):
                rows = pl.ds(k // 3 * FRAG + k % 3, 8, stride=3)
                turned.at[part][rows, :] = planes[3 * number + part, k] * factor
        rows = [turned[part].T for part in range(3)]
        for part in range(3):
            plane(3 * number + part, rows[part])
        return carry

    lax.fori_loop(0, FRAG // 3, trip, 0)
    for frag in range(2):
        for tile in range(5):
            width = min(128, FRAG * FRAG - tile * 128)
            out[frag, :, tile * 128 : tile * 128 + width] = strips[frag, tile, :, :width]


def spread(value, lane):
    values = [value]
    for step in (4, 2, 1):
        clear = lane & step == 0
        values = [
            part
            for v in values
            for part in (
                jnp.where(clear, v, rolled(v, step)),
                jnp.where(clear, rolled(v, -step), v),
            )
        ]
    return values


def gather_sums(values, lane):
    for step in (4, 2, 1):
        clear = lane & step == 0
        count = len(values) // 2
        values = [
            jnp.where(
                clear,
                values[k] + rolled(values[k], -step),
                values[k + count] + rolled(values[k + count], step),
            )
            for k in range(count)
        ]
    return values[0]


def total_of(x):
    return jnp.sum(jnp.sum(x, axis=0, keepdims=True), axis=1, keepdims=True)


def filter_fragments(meta, *refs):
    owned, beside, next_rows, last_rows, start = refs[:5]
    out, scale_out = refs[5:7]
    shares = refs[7:10]
    boxes, turned, compact, potential, other, spilled = refs[10:]
    lane = lanes(8)
    sub = lax.broadcasted_iota(jnp.int32, (8, 128), 0)
    second = (lane // 8) % 2 == 1
    for down in range(3):
        groups = 8 if down < 2 else 4

        def unpack(number, carry, down=down, groups=groups):
            moved_windows = []
            for part in range(4):
                group = 4 * number + part
                if down == 0:
                    both = owned[group] + beside[group]
                else:
                    both = (next_rows if down == 1 else last_rows)[group]
                moved_windows.append([rolled(both, -32 * slot) for slot in range(4)])
            for part in range(4):
                for slot in range(4):
                    row = 16 * down + 4 * number + part + groups * (slot // 2)
                    rows = pl.ds(pl.multiple_of(row * FRAG, 8), FRAG)
                    boxes[slot % 2, rows, :] = moved_windows[part][slot]
            return carry

        lax.fori_loop(0, groups // 4, unpack, 0)
    lowest = None
    for part in range(3):
        rows = []
        for yc in range(8):
            for frag in range(2):
                base = (meta[frag] + 8 * part) * FRAG + 3 * yc
                took = [boxes[frag, pl.ds(base + yi, 8, stride=FRAG), :] for yi in range(3)]
                rows.append(
                    jnp.where(
                        lane < FRAG,
                        took[0],
                        jnp.where(lane < 2 * FRAG, rolled(took[1], FRAG), rolled(took[2], 2 * FRAG)),
                    )
                )
        turned[part] = jnp.concatenate(rows, 0).T
    for part in range(3):
        for k in range(9):
            value = turned.at[part][pl.ds(k // 3 * FRAG + k % 3, 8, stride=3), :]
            compact[9 * part + k] = value
            lowest = value if lowest is None else jnp.minimum(lowest, value)
            highest = value if part + k == 0 else jnp.maximum(highest, value)

    def window(keep):
        low = jnp.where(keep, lowest, jnp.inf)
        high = jnp.where(keep, highest, -jnp.inf)
        low = jnp.min(jnp.min(low, axis=0, keepdims=True), axis=1, keepdims=True) + WINDOW_GAP
        high = jnp.max(jnp.max(high, axis=0, keepdims=True), axis=1, keepdims=True) + KINETIC_TOP
        return 0.5 * (high + low), 0.5 * (high - low)

    centre_0, half_0 = window(~second)
    centre_1, half_1 = window(second)
    centre = jnp.where(second, centre_1, centre_0)
    inverse = 1.0 / jnp.where(second, half_1, half_0)
    for part in range(3):
        for k in range(9):
            value = -2.0 * (3.0 + compact[9 * part + k] - centre)
            for x, wide in enumerate(spread(value, lane)):
                potential[8 * part + x, k] = wide
    odd_scale = -inverse
    even_scale = inverse * inverse
    degree = jnp.where(second, meta[5], meta[4])

    def apply(source, target, earlier=None, initial=False, even=False, step=None):
        if step is not None:
            live, just_done = step <= degree, step == degree + 1
        earlier = target if earlier is None else earlier

        def chunk(number, carry):
            behind, here = list(carry[:9]), list(carry[9:])
            for k4 in range(8):
                x = 8 * number + k4
                ahead_x = jnp.minimum(x + 1, FRAG - 1)
                ahead = [source[ahead_x, k] for k in range(9)]
                if k4 == 7:
                    ahead = [jnp.where(x + 1 < FRAG, v, 0.0) for v in ahead]
                for k in range(9):
                    yi, zi = divmod(k, 3)
                    total = behind[k] + ahead[k]
                    if yi > 0:
                        total = total + here[k - 3]
                    else:
                        total = total + jnp.where(lane >= 16, rolled(here[6 + zi], 16), 0.0)
                    if yi < 2:
                        total = total + here[k + 3]
                    else:
                        total = total + jnp.where(lane < 112, rolled(here[zi], -16), 0.0)
                    if zi > 0:
                        total = total + here[k - 1]
                    else:
                        total = total + jnp.where(sub >= 1, rolled(here[k + 2], 1, 0), 0.0)
                    if zi < 2:
                        total = total + here[k + 1]
                    else:
                        total = total + jnp.where(sub < 7, rolled(here[k - 2], -1, 0), 0.0)
                    following = potential[x, k] * here[k] + total
                    if initial:
                        following = 0.5 * following
                    else:
                        past = earlier[x, k]
                        following = even_scale * following - past if even else following - past
                    if step is not None:
                        kept = jnp.where(just_done, odd_scale * here[k], past)
                        following = jnp.where(live, following, kept)
                    target[x, k] = following
                behind, here = here, ahead
            return tuple(behind + here)

        zero = [jnp.zeros((8, 128), F32)] * 9
        lax.fori_loop(0, 3, chunk, tuple(zero + [source[0, k] for k in range(9)]))

    apply(start, other, initial=True)
    apply(other, out, earlier=start, even=True)
    fewest = jnp.minimum(meta[4], meta[5])
    most = jnp.maximum(meta[4], meta[5])
    plain = (fewest - 2) // 2
    pairs = (most - 1) // 2

    def free_pair(pair, carry):
        apply(out, other)
        apply(other, out, even=True)
        return carry

    def held_pair(pair, carry):
        apply(out, other)
        apply(other, out, even=True, step=2 * pair + 4)
        return carry

    lax.fori_loop(0, plain, free_pair, 0)
    lax.fori_loop(plain, pairs, held_pair, 0)

    def squares(x, sums):
        return tuple(sums[k] + out[x, k] * out[x, k] for k in range(9))

    sums = lax.fori_loop(0, FRAG, squares, (jnp.zeros((8, 128), F32),) * 9)
    sums = sum(sums[1:], sums[0])
    sums = jnp.sum(sums, axis=0, keepdims=True)
    sums = jnp.broadcast_to(sums, (8, 128))
    for step in (16, 32, 64):
        sums = sums + rolled(sums, step)
    scale = jnp.sqrt(float(FRAG**3) / (sums + 1e-06))
    scale_out[...] = scale
    weight = jnp.where(second, meta[3], meta[2]).astype(F32) / NORB

    def clear(row, carry):
        for frag in range(2):
            spilled[frag, pl.ds(pl.multiple_of(row * FRAG, 8), FRAG), :] = jnp.zeros((FRAG, 128), F32)
        return carry

    lax.fori_loop(0, 40, clear, 0)
    for part in range(3):
        for k in range(9):
            values = []
            for x in range(8):
                value = out[8 * part + x, k] * scale
                values.append(value * value)
            turned.at[part][pl.ds(k // 3 * FRAG + k % 3, 8, stride=3), :] = gather_sums(values, lane) * weight
    for part in range(3):
        rows = turned[part].T
        for yc in range(8):
            for frag in range(2):
                piece = rows[(2 * yc + frag) * 8 : (2 * yc + frag) * 8 + 8]
                base = (meta[frag] + 8 * part) * FRAG + 3 * yc
                for yi in range(3):
                    spilled[frag, pl.ds(base + yi, 8, stride=FRAG), :] = rolled(piece, -FRAG * yi)
    slot_of = slots_of(FRAG)
    for down in range(3):
        groups = 8 if down < 2 else 4

        def share(number, carry, down=down, groups=groups):
            totals = []
            for part in range(4):
                total = None
                for slot in range(4):
                    row = 16 * down + 4 * number + part + groups * (slot // 2)
                    piece = spilled[slot % 2, pl.ds(pl.multiple_of(row * FRAG, 8), FRAG), :]
                    piece = rolled(piece, 32 * slot)
                    total = piece if total is None else jnp.where(slot_of == slot, piece, total)
                totals.append(total)
            for part in range(4):
                shares[down][4 * number + part] = totals[part]
            return carry

        lax.fori_loop(0, groups // 4, share, 0)


def add_windows(places, grid, along, shares):
    lane = lanes(FRAG)
    for down in range(3):
        groups = 8 if down < 2 else 4
        k = 2 * down + along

        def add(number, carry, k=k, down=down, groups=groups):
            pieces = []
            for part in range(4):
                group = 4 * number + part
                both = shares[0][8 * down + group] if along else shares[down][group]
                for slot in range(4):
                    depth = places[6 * k + 3 * (slot % 2) + 2]
                    pieces.append(pltpu.roll(both, (256 + depth - 32 * slot) & 127, 1))
            for part in range(4):
                for slot in range(4):
                    frag = slot % 2
                    row = 4 * number + part + groups * (slot // 2)
                    col, depth = places[6 * k + 3 * frag + 1], places[6 * k + 3 * frag + 2]
                    piece = jnp.where(((lane - depth) & 127) < FRAG, pieces[4 * part + slot], 0.0)
                    cols = pl.ds(32 + col - 32 * along, FRAG)
                    grid[0, row, cols, :] += jnp.where(lane >= depth, piece, 0.0)
                    grid[1, row, cols, :] += jnp.where(lane >= depth, 0.0, piece)
            return carry

        lax.fori_loop(0, groups // 4, add, 0)


def patch_owned(places, first, second, third, out, grid):
    def clear(row, carry):
        for half in range(2):
            grid[half, row] = jnp.zeros((PADDED, 128), F32)
        return carry

    lax.fori_loop(0, ROWS, clear, 0)
    add_windows(places, grid, 0, (first, second, third))
    for half in range(2):
        out[:, :, half * 128 : half * 128 + 128] = grid[half, :, 32 : 32 + COLS]


def patch_beside(places, owned, beside, out, grid):
    fill_grid(grid, owned[...])
    add_windows(places, grid, 1, (beside,))
    for half in range(2):
        out[:, :, half * 128 : half * 128 + 128] = grid[half, :, 32 : 32 + COLS]


def moved(x, down, along):
    pairs = [
        (p * NPY + q, (p + down) * NPY + q + along)
        for p in range(NPX)
        for q in range(NPY)
        if 0 <= p + down < NPX and 0 <= q + along < NPY
    ]
    return lax.ppermute(x, ALL, pairs)


def swapped(tiles):
    return lax.all_to_all(tiles, "py", split_axis=0, concat_axis=0, tiled=True)


def over_chips(rows):
    tiles = rows.reshape(NPX // 2, 8, 128)
    return lax.all_to_all(tiles, PX[:2], split_axis=0, concat_axis=0, tiled=True).reshape(rows.shape)


def body(density, external, orbitals, anchors, weights, degrees):
    row_place = lax.axis_index(PX)
    col_place = lax.axis_index("py")
    origin = jnp.stack([row_place * ROWS, col_place * COLS, 0])
    local = (anchors - origin[None, :]).astype(jnp.int32)
    own = jnp.pad(local.reshape(6), (0, 2))
    above = jnp.stack([own, moved(own, 1, 0), moved(own, 2, 0)])
    meta = jnp.concatenate([local[:, 0], weights, degrees, weights]).astype(jnp.int32)

    sine_y = [jnp.asarray(t) for t in SINE_Y]
    sine_z = jnp.asarray(SINE_Z)
    ey = jnp.asarray(EIGEN_Y)
    ez = lax.dynamic_slice(jnp.asarray(EIGEN_Z), (col_place * KZ, 0), (KZ, 1))
    ez, above = lax.optimization_barrier((ez, above))
    places = jnp.stack([above, moved(above, 0, 1)], 1)[:, :, :6].reshape(36)

    planes = call(
        orbitals_in,
        shape(FRAG, 9, 8, 128),
        [pltpu.VMEM((2, 5, NORB * FRAG, 128), F32), pltpu.VMEM((3, 128, 128), F32)],
    )(orbitals.reshape(2, NORB * FRAG, FRAG * FRAG))
    tiles = call(forward_z, shape(NPY, KZ, ROWS * COLS), count=2)(density, sine_z)
    tiles = swapped(tiles)
    field, moments = call(
        forward_y,
        (shape(ROWS * KZ, NY), shape(2 * KZ, NY)),
        [pltpu.VMEM((ROWS * KZ, NY), F32)],
        count=5,
    )(tiles, *sine_y, ey, ez)

    core = lax.axis_index("px_2").reshape(1).astype(jnp.int32)
    chip = row_place // 2
    other = lax.ppermute(moments, "px_2", [(0, 1), (1, 0)])
    chips = call(pair_moments, shape(128, 128), smem=(0,), count=5)(core, moments, other, ey, ez)
    chips = over_chips(chips)
    chip_ez = lax.dynamic_slice(jnp.asarray(EIGEN_Z), (col_place * KZ + chip, 0), (1, 1))
    chips = call(scan_chips, shape(128, 128), count=3)(chips, ey, chip_ez)
    states = over_chips(chips)

    tiles = call(
        back_y, shape(NPY, KZ, ROWS * COLS), [pltpu.VMEM((ROWS * KZ, NY), F32)], smem=(0,), count=8
    )(core, field, other, states, *sine_y, ey, ez)
    tiles = swapped(tiles)
    groups = (8, 8, 4)
    grid = [pltpu.VMEM((2, ROWS, PADDED, 128), F32)]
    hartree_field, beside = call(
        back_z, [shape(ROWS, COLS, NZ), shape(20, FRAG, 128)], grid, smem=(0,), count=4
    )(places, tiles, external, sine_z)
    owned = call(cut_owned, [shape(n, FRAG, 128) for n in groups], grid, smem=(0,), count=3)(
        places, hartree_field, external
    )
    beside = moved(beside, 0, -1)
    next_rows = moved(owned[1] + beside[8:16], -1, 0)
    last_rows = moved(owned[2] + beside[16:], -2, 0)
    planes, scale, *shares = call(
        filter_fragments,
        [shape(FRAG, 9, 8, 128), shape(8, 128)] + [shape(n, FRAG, 128) for n in groups],
        [
            pltpu.VMEM((2, 40 * FRAG, 128), F32),
            pltpu.VMEM((3, 128, 128), F32),
            pltpu.VMEM((27, 8, 128), F32),
            pltpu.VMEM((FRAG, 9, 8, 128), F32),
            pltpu.VMEM((FRAG, 9, 8, 128), F32),
            pltpu.VMEM((2, 40 * FRAG, 128), F32),
        ],
        smem=(0,),
        count=6,
    )(meta, owned[0], beside, next_rows, last_rows, planes)
    received = [shares[0], moved(shares[1], 1, 0), moved(shares[2], 2, 0)]
    beside = moved(jnp.concatenate(received), 0, 1)
    filtered = call(
        orbitals_out,
        shape(2, NORB * FRAG, FRAG * FRAG),
        [pltpu.VMEM((2, 5, NORB * FRAG, 128), F32), pltpu.VMEM((3, 128, 128), F32)],
        count=2,
    )(planes, scale)
    density_owned = call(patch_owned, shape(ROWS, COLS, NZ), grid, smem=(0,), count=4)(places, *received)
    new_density = call(patch_beside, shape(ROWS, COLS, NZ), grid, smem=(0,), count=3)(
        places, density_owned, beside
    )
    return hartree_field, filtered.reshape(orbitals.shape), new_density


def solution(mesh):
    torus = Mesh(mesh.devices.reshape(8, 2, 2, NPY), ALL)
    grid = P(PX, "py", None)
    return jax.shard_map(
        body,
        mesh=torus,
        in_specs=(grid, grid, P(ALL, None, None, None), P(ALL, None), P(ALL), P(ALL)),
        out_specs=(grid, P(ALL, None, None, None), grid),
        check_vma=False,
    )
```

```python
import jax
import jax.numpy as jnp
import numpy as np
from jax import lax
from jax.experimental import pallas as pl
from jax.experimental.pallas import tpu as pltpu
from jax.sharding import Mesh
from jax.sharding import PartitionSpec as P

NX, NY, NZ = 512, 512, 256
NPX, NPY = 32, 16
ROWS, COLS = NX // NPX, NY // NPY
KZ = NZ // NPY
FRAG, NORB = 24, 8
PX = ("px_0", "px_1", "px_2")
ALL = PX + ("py",)
SCREENING, WINDOW_GAP, KINETIC_TOP = 0.002, 0.1, 6.0
STEPS = ((0, 0), (0, 1), (1, 0), (1, 1), (2, 0), (2, 1))
PADDED = COLS + 32 + FRAG
F32 = jnp.float32
BF16 = jnp.bfloat16
VMEM = pl.BlockSpec(memory_space=pltpu.VMEM)
SMEM = pl.BlockSpec(memory_space=pltpu.SMEM)


def sine_table(length):
    index = np.arange(1, length + 1, dtype=np.int64)
    product = index[:, None] * index[None, :] % (2 * length + 2)
    return np.sin(product * (np.pi / (length + 1))) * np.sqrt(2.0 / (length + 1))


def halves_of(table):
    high = np.asarray(table, np.float32).astype(BF16)
    low = (table - high.astype(np.float64)).astype(np.float32).astype(BF16)
    return high, low


def eigen_values(length):
    wave = np.arange(1, length + 1, dtype=np.float64) * (np.pi / (length + 1))
    return (4.0 * np.sin(wave / 2.0) ** 2).astype(np.float32)


SINE_Y = halves_of(sine_table(NY))
SINE_Z = np.stack(halves_of(sine_table(NZ)))
EIGEN_Y = eigen_values(NY)[None, :]
EIGEN_Z = eigen_values(NZ)[:, None]


def split2(x):
    high = x.astype(BF16)
    return high, (x - high.astype(F32)).astype(BF16)


def dot3(left, right, dims):
    def one(a, b):
        return lax.dot_general(a, b, (dims, ((), ())), preferred_element_type=F32)

    return one(left[0], right[0]) + (one(left[0], right[1]) + one(left[1], right[0]))


def call(kernel, outs, scratch=(), smem=(), count=1):
    return pl.pallas_call(
        kernel,
        out_shape=outs,
        in_specs=[SMEM if k in smem else VMEM for k in range(count)],
        out_specs=jax.tree.map(lambda _: VMEM, outs),
        scratch_shapes=list(scratch),
        compiler_params=pltpu.CompilerParams(vmem_limit_bytes=48 * 1024 * 1024),
    )


def shape(*dims):
    return jax.ShapeDtypeStruct(dims, F32)


def lanes(rows):
    return lax.broadcasted_iota(jnp.int32, (rows, 128), 1)


def rolled(x, by, axis=1):
    by %= x.shape[axis]
    return pltpu.roll(x, by, axis) if by else x


def decay(ey, ez):
    gap = ey + ez + SCREENING
    root = jnp.sqrt(gap + 0.25 * gap * gap)
    return 1.0 / (1.0 + 0.5 * gap + root), 0.5 / root


def forward_z(density, table, out):
    cells = density[...].reshape(ROWS * COLS, NZ)
    spectrum = dot3((table[0], table[1]), split2(cells), ((1,), (1,)))
    out[...] = spectrum.reshape(NPY, KZ, ROWS * COLS)


def block_power(rate):
    for _ in range(4):
        rate = rate * rate
    return rate


def put_rows(ref, first, value):
    for half in range(2):
        for k in range(4):
            rows = pl.ds(64 * half + first + k, 8, stride=8)
            ref[rows, :] = value[8 * half : 8 * half + 8, 128 * k : 128 * k + 128]


def take_rows(ref, first):
    return jnp.concatenate(
        [
            jnp.concatenate(
                [ref[pl.ds(64 * half + first + k, 8, stride=8), :] for half in range(2)], 0
            )
            for k in range(4)
        ],
        1,
    )


def pair_moments(core, own, other, ey, ez, out):
    power = block_power(decay(ey[...], ez[...])[0])
    upper = core[0] == 1
    high = jnp.where(upper, own[...], other[...])
    low = jnp.where(upper, other[...], own[...])
    put_rows(out, 0, high[:KZ] + power * low[:KZ])
    put_rows(out, 4, low[KZ:] + power * high[KZ:])


def scan_chips(moments, ey, ez, out):
    rate, _ = decay(ey[...], ez[...])
    power = block_power(rate)
    power = power * power
    right, left = take_rows(moments, 0), take_rows(moments, 4)
    count = NPX // 2
    row = lax.broadcasted_iota(jnp.int32, (count, NY), 0)
    before, after = jnp.ones((count, NY), F32), jnp.ones((count, NY), F32)
    step = 1
    while step < count:
        right = right + power * jnp.where(row >= step, rolled(right, step, 0), 0.0)
        left = left + power * jnp.where(row < count - step, rolled(left, -step, 0), 0.0)
        upper = row & step != 0
        before = jnp.where(upper, before * power, before)
        after = jnp.where(upper, after, after * power)
        power = power * power
        step *= 2
    across = power * rate
    norm = rate / (1.0 - across * across)
    right_total, left_total = right[count - 1 :], left[:1]
    state = jnp.where(row >= 1, rolled(right, 1, 0), 0.0)
    put_rows(out, 0, state - norm * (left_total - across * right_total) * before)
    state = jnp.where(row < count - 1, rolled(left, -1, 0), 0.0)
    put_rows(out, 4, state - norm * (right_total - across * left_total) * after)


def forward_y(tiles, table_high, table_low, ey, ez, field_out, moment_out, merged):
    block = lanes(KZ) // COLS
    for row in range(ROWS):
        for tile in range(4):
            total = None
            for k in range(4):
                piece = tiles[4 * tile + k, :, row // 4 * 128 : row // 4 * 128 + 128]
                piece = rolled(piece, (k - row % 4) * COLS)
                total = piece if total is None else jnp.where(block == k, piece, total)
            merged[row * KZ : (row + 1) * KZ, tile * 128 : (tile + 1) * 128] = total
    field = dot3(split2(merged[...]), (table_high[...], table_low[...]), ((1,), (0,)))
    field_out[...] = field
    rate, _ = decay(ey[...], ez[...])
    first = field[:KZ]
    last = field[(ROWS - 1) * KZ :]
    for row in range(1, ROWS):
        first = field[row * KZ : (row + 1) * KZ] + rate * first
        back = ROWS - 1 - row
        last = field[back * KZ : (back + 1) * KZ] + rate * last
    moment_out[:KZ] = first
    moment_out[KZ:] = last


def back_y(core, field, other, states, table_high, table_low, ey, ez, tiles_out, solved):
    rate, scale = decay(ey[...], ez[...])
    power = block_power(rate)
    upper = core[0] == 1
    state, left = take_rows(states, 0), take_rows(states, 4)
    state = jnp.where(upper, other[:KZ] + power * state, state)
    left = jnp.where(upper, left, other[KZ:] + power * left)
    for row in range(ROWS):
        state = field[row * KZ : (row + 1) * KZ] + rate * state
        solved[row * KZ : (row + 1) * KZ] = state
    for row in range(ROWS - 1, -1, -1):
        here = pl.ds(row * KZ, KZ)
        solved[here] = scale * (solved[here] + rate * left)
        left = field[here] + rate * left
    columns = dot3(split2(solved[...]), (table_high[...], table_low[...]), ((1,), (0,)))
    solved[...] = columns
    block = lanes(KZ) // COLS
    for peer in range(NPY):
        for tile in range(4):
            total = None
            for k in range(4):
                row = 4 * tile + k
                piece = solved[row * KZ : (row + 1) * KZ, peer // 4 * 128 : peer // 4 * 128 + 128]
                piece = rolled(piece, (k - peer % 4) * COLS)
                total = piece if total is None else jnp.where(block == k, piece, total)
            tiles_out[peer, :, tile * 128 : (tile + 1) * 128] = total


def slots_of(rows):
    return lanes(rows) // 32


def fill_grid(grid, potential):
    for half in range(2):
        grid[half, :, :32] = jnp.zeros((ROWS, 32, 128), F32)
        grid[half, :, 32 + COLS :] = jnp.zeros((ROWS, FRAG, 128), F32)
        grid[half, :, 32 : 32 + COLS] = potential[:, :, half * 128 : half * 128 + 128]


def cut_windows(places, grid, along, outs):
    lane = lanes(FRAG)
    slot_of = slots_of(FRAG)
    for down in range(3):
        groups = 8 if down < 2 else 4
        k = 2 * down + along

        def cut(number, carry, k=k, down=down, groups=groups):
            totals = []
            for part in range(4):
                total = None
                for slot in range(4):
                    frag = slot % 2
                    row = 4 * number + part + groups * (slot // 2)
                    col, depth = places[6 * k + 3 * frag + 1], places[6 * k + 3 * frag + 2]
                    cols = pl.ds(32 + col - 32 * along, FRAG)
                    window = jnp.where(lane >= depth, grid[0, row, cols, :], grid[1, row, cols, :])
                    window = pltpu.roll(window, (256 + 32 * slot - depth) & 127, 1)
                    total = window if total is None else jnp.where(slot_of == slot, window, total)
                totals.append(total)
            for part in range(4):
                if along:
                    outs[0][8 * down + 4 * number + part] = totals[part]
                else:
                    outs[down][4 * number + part] = totals[part]
            return carry

        lax.fori_loop(0, groups // 4, cut, 0)


def back_z(places, tiles, external, table, field_out, beside, grid):
    spectrum = tiles[...].reshape(NZ, ROWS * COLS)
    turned = spectrum.T
    field = dot3(split2(turned), (table[0], table[1]), ((1,), (0,)))
    field = field.reshape(ROWS, COLS, NZ)
    field_out[...] = field
    fill_grid(grid, field + external[...])
    cut_windows(places, grid, 1, (beside,))


def cut_owned(places, field, external, *rest):
    fill_grid(rest[3], field[...] + external[...])
    cut_windows(places, rest[3], 0, rest[:3])


def orbitals_in(orbitals, out, strips, turned):
    for frag in range(2):
        for tile in range(5):
            width = min(128, FRAG * FRAG - tile * 128)
            strips[frag, tile, :, :width] = orbitals[frag, :, tile * 128 : tile * 128 + width]
    lane = lanes(8)

    def plane(x, place):
        rows = []
        for yc in range(8):
            tile, off = divmod(72 * yc, 128)
            for frag in range(2):
                piece = rolled(strips[frag, tile, pl.ds(x, 8, stride=FRAG), :], -off)
                if off + 72 > 128:
                    other = rolled(strips[frag, tile + 1, pl.ds(x, 8, stride=FRAG), :], -off)
                    piece = jnp.where(lane < 128 - off, piece, other)
                rows.append(piece)
        place[...] = jnp.concatenate(rows, 0).T

    def planes(number, carry):
        for part in range(3):
            plane(3 * number + part, turned.at[part])
        for part in range(3):
            for k in range(9):
                rows = pl.ds(k // 3 * FRAG + k % 3, 8, stride=3)
                out[3 * number + part, k] = turned.at[part][rows, :]
        return carry

    lax.fori_loop(0, FRAG // 3, planes, 0)


def orbitals_out(planes, scale, out, strips, turned):
    lane = lanes(8)
    factor = scale[...]

    def plane(x, rows):
        for frag in range(2):
            for tile in range(5):
                total = None
                for yc in range(8):
                    start = 72 * yc - 128 * tile
                    if -72 < start < 128:
                        piece = rows[(2 * yc + frag) * 8 : (2 * yc + frag) * 8 + 8]
                        piece = rolled(piece, start)
                        if total is None:
                            total = piece
                        else:
                            total = jnp.where(lane >= start, piece, total)
                strips[frag, tile, pl.ds(x, 8, stride=FRAG), :] = total

    def trip(number, carry):
        for part in range(3):
            for k in range(9):
                rows = pl.ds(k // 3 * FRAG + k % 3, 8, stride=3)
                turned.at[part][rows, :] = planes[3 * number + part, k] * factor
        rows = [turned[part].T for part in range(3)]
        for part in range(3):
            plane(3 * number + part, rows[part])
        return carry

    lax.fori_loop(0, FRAG // 3, trip, 0)
    for frag in range(2):
        for tile in range(5):
            width = min(128, FRAG * FRAG - tile * 128)
            out[frag, :, tile * 128 : tile * 128 + width] = strips[frag, tile, :, :width]


def spread(value, lane):
    values = [value]
    for step in (4, 2, 1):
        clear = lane & step == 0
        values = [
            part
            for v in values
            for part in (
                jnp.where(clear, v, rolled(v, step)),
                jnp.where(clear, rolled(v, -step), v),
            )
        ]
    return values


def gather_sums(values, lane):
    for step in (4, 2, 1):
        clear = lane & step == 0
        count = len(values) // 2
        values = [
            jnp.where(
                clear,
                values[k] + rolled(values[k], -step),
                values[k + count] + rolled(values[k + count], step),
            )
            for k in range(count)
        ]
    return values[0]


def total_of(x):
    return jnp.sum(jnp.sum(x, axis=0, keepdims=True), axis=1, keepdims=True)


def filter_fragments(meta, *refs):
    owned, beside, next_rows, last_rows, start = refs[:5]
    out, scale_out = refs[5:7]
    shares = refs[7:10]
    boxes, turned, compact, potential, other, spilled = refs[10:]
    lane = lanes(8)
    sub = lax.broadcasted_iota(jnp.int32, (8, 128), 0)
    second = (lane // 8) % 2 == 1
    for down in range(3):
        groups = 8 if down < 2 else 4

        def unpack(number, carry, down=down, groups=groups):
            moved_windows = []
            for part in range(4):
                group = 4 * number + part
                if down == 0:
                    both = owned[group] + beside[group]
                else:
                    both = (next_rows if down == 1 else last_rows)[group]
                moved_windows.append([rolled(both, -32 * slot) for slot in range(4)])
            for part in range(4):
                for slot in range(4):
                    row = 16 * down + 4 * number + part + groups * (slot // 2)
                    rows = pl.ds(pl.multiple_of(row * FRAG, 8), FRAG)
                    boxes[slot % 2, rows, :] = moved_windows[part][slot]
            return carry

        lax.fori_loop(0, groups // 4, unpack, 0)
    lowest = None
    for part in range(3):
        rows = []
        for yc in range(8):
            for frag in range(2):
                base = (meta[frag] + 8 * part) * FRAG + 3 * yc
                took = [boxes[frag, pl.ds(base + yi, 8, stride=FRAG), :] for yi in range(3)]
                rows.append(
                    jnp.where(
                        lane < FRAG,
                        took[0],
                        jnp.where(lane < 2 * FRAG, rolled(took[1], FRAG), rolled(took[2], 2 * FRAG)),
                    )
                )
        turned[part] = jnp.concatenate(rows, 0).T
    for part in range(3):
        for k in range(9):
            value = turned.at[part][pl.ds(k // 3 * FRAG + k % 3, 8, stride=3), :]
            compact[9 * part + k] = value
            lowest = value if lowest is None else jnp.minimum(lowest, value)
            highest = value if part + k == 0 else jnp.maximum(highest, value)

    def window(keep):
        low = jnp.where(keep, lowest, jnp.inf)
        high = jnp.where(keep, highest, -jnp.inf)
        low = jnp.min(jnp.min(low, axis=0, keepdims=True), axis=1, keepdims=True) + WINDOW_GAP
        high = jnp.max(jnp.max(high, axis=0, keepdims=True), axis=1, keepdims=True) + KINETIC_TOP
        return 0.5 * (high + low), 0.5 * (high - low)

    centre_0, half_0 = window(~second)
    centre_1, half_1 = window(second)
    centre = jnp.where(second, centre_1, centre_0)
    inverse = 1.0 / jnp.where(second, half_1, half_0)
    for part in range(3):
        for k in range(9):
            value = -2.0 * (3.0 + compact[9 * part + k] - centre)
            for x, wide in enumerate(spread(value, lane)):
                potential[8 * part + x, k] = wide
    odd_scale = -inverse
    even_scale = inverse * inverse
    degree = jnp.where(second, meta[5], meta[4])

    def apply(source, target, earlier=None, initial=False, even=False, step=None):
        if step is not None:
            live, just_done = step <= degree, step == degree + 1
        earlier = target if earlier is None else earlier

        def chunk(number, carry):
            behind, here = list(carry[:9]), list(carry[9:])
            for k4 in range(24):
                x = 24 * number + k4
                ahead_x = jnp.minimum(x + 1, FRAG - 1)
                ahead = [source[ahead_x, k] for k in range(9)]
                if k4 == 23:
                    ahead = [jnp.where(x + 1 < FRAG, v, 0.0) for v in ahead]
                for k in range(9):
                    yi, zi = divmod(k, 3)
                    total = behind[k] + ahead[k]
                    if yi > 0:
                        total = total + here[k - 3]
                    else:
                        total = total + jnp.where(lane >= 16, rolled(here[6 + zi], 16), 0.0)
                    if yi < 2:
                        total = total + here[k + 3]
                    else:
                        total = total + jnp.where(lane < 112, rolled(here[zi], -16), 0.0)
                    if zi > 0:
                        total = total + here[k - 1]
                    else:
                        total = total + jnp.where(sub >= 1, rolled(here[k + 2], 1, 0), 0.0)
                    if zi < 2:
                        total = total + here[k + 1]
                    else:
                        total = total + jnp.where(sub < 7, rolled(here[k - 2], -1, 0), 0.0)
                    following = potential[x, k] * here[k] + total
                    if initial:
                        following = 0.5 * following
                    else:
                        past = earlier[x, k]
                        following = even_scale * following - past if even else following - past
                    if step is not None:
                        kept = jnp.where(just_done, odd_scale * here[k], past)
                        following = jnp.where(live, following, kept)
                    target[x, k] = following
                behind, here = here, ahead
            return tuple(behind + here)

        zero = [jnp.zeros((8, 128), F32)] * 9
        lax.fori_loop(0, 1, chunk, tuple(zero + [source[0, k] for k in range(9)]))

    apply(start, other, initial=True)
    apply(other, out, earlier=start, even=True)
    fewest = jnp.minimum(meta[4], meta[5])
    most = jnp.maximum(meta[4], meta[5])
    plain = (fewest - 2) // 2
    pairs = (most - 1) // 2

    def free_pair(pair, carry):
        apply(out, other)
        apply(other, out, even=True)
        return carry

    def held_pair(pair, carry):
        apply(out, other)
        apply(other, out, even=True, step=2 * pair + 4)
        return carry

    lax.fori_loop(0, plain, free_pair, 0)
    lax.fori_loop(plain, pairs, held_pair, 0)

    def squares(x, sums):
        return tuple(sums[k] + out[x, k] * out[x, k] for k in range(9))

    sums = lax.fori_loop(0, FRAG, squares, (jnp.zeros((8, 128), F32),) * 9)
    sums = sum(sums[1:], sums[0])
    sums = jnp.sum(sums, axis=0, keepdims=True)
    sums = jnp.broadcast_to(sums, (8, 128))
    for step in (16, 32, 64):
        sums = sums + rolled(sums, step)
    scale = jnp.sqrt(float(FRAG**3) / (sums + 1e-06))
    scale_out[...] = scale
    weight = jnp.where(second, meta[3], meta[2]).astype(F32) / NORB

    def clear(row, carry):
        for frag in range(2):
            spilled[frag, pl.ds(pl.multiple_of(row * FRAG, 8), FRAG), :] = jnp.zeros((FRAG, 128), F32)
        return carry

    lax.fori_loop(0, 40, clear, 0)
    for part in range(3):
        for k in range(9):
            values = []
            for x in range(8):
                value = out[8 * part + x, k] * scale
                values.append(value * value)
            turned.at[part][pl.ds(k // 3 * FRAG + k % 3, 8, stride=3), :] = gather_sums(values, lane) * weight
    for part in range(3):
        rows = turned[part].T
        for yc in range(8):
            for frag in range(2):
                piece = rows[(2 * yc + frag) * 8 : (2 * yc + frag) * 8 + 8]
                base = (meta[frag] + 8 * part) * FRAG + 3 * yc
                for yi in range(3):
                    spilled[frag, pl.ds(base + yi, 8, stride=FRAG), :] = rolled(piece, -FRAG * yi)
    slot_of = slots_of(FRAG)
    for down in range(3):
        groups = 8 if down < 2 else 4

        def share(number, carry, down=down, groups=groups):
            totals = []
            for part in range(4):
                total = None
                for slot in range(4):
                    row = 16 * down + 4 * number + part + groups * (slot // 2)
                    piece = spilled[slot % 2, pl.ds(pl.multiple_of(row * FRAG, 8), FRAG), :]
                    piece = rolled(piece, 32 * slot)
                    total = piece if total is None else jnp.where(slot_of == slot, piece, total)
                totals.append(total)
            for part in range(4):
                shares[down][4 * number + part] = totals[part]
            return carry

        lax.fori_loop(0, groups // 4, share, 0)


def add_windows(places, grid, along, shares):
    lane = lanes(FRAG)
    for down in range(3):
        groups = 8 if down < 2 else 4
        k = 2 * down + along

        def add(number, carry, k=k, down=down, groups=groups):
            pieces = []
            for part in range(4):
                group = 4 * number + part
                both = shares[0][8 * down + group] if along else shares[down][group]
                for slot in range(4):
                    depth = places[6 * k + 3 * (slot % 2) + 2]
                    pieces.append(pltpu.roll(both, (256 + depth - 32 * slot) & 127, 1))
            for part in range(4):
                for slot in range(4):
                    frag = slot % 2
                    row = 4 * number + part + groups * (slot // 2)
                    col, depth = places[6 * k + 3 * frag + 1], places[6 * k + 3 * frag + 2]
                    piece = jnp.where(((lane - depth) & 127) < FRAG, pieces[4 * part + slot], 0.0)
                    cols = pl.ds(32 + col - 32 * along, FRAG)
                    grid[0, row, cols, :] += jnp.where(lane >= depth, piece, 0.0)
                    grid[1, row, cols, :] += jnp.where(lane >= depth, 0.0, piece)
            return carry

        lax.fori_loop(0, groups // 4, add, 0)


def patch_owned(places, first, second, third, out, grid):
    def clear(row, carry):
        for half in range(2):
            grid[half, row] = jnp.zeros((PADDED, 128), F32)
        return carry

    lax.fori_loop(0, ROWS, clear, 0)
    add_windows(places, grid, 0, (first, second, third))
    for half in range(2):
        out[:, :, half * 128 : half * 128 + 128] = grid[half, :, 32 : 32 + COLS]


def patch_beside(places, owned, beside, out, grid):
    fill_grid(grid, owned[...])
    add_windows(places, grid, 1, (beside,))
    for half in range(2):
        out[:, :, half * 128 : half * 128 + 128] = grid[half, :, 32 : 32 + COLS]


def moved(x, down, along):
    pairs = [
        (p * NPY + q, (p + down) * NPY + q + along)
        for p in range(NPX)
        for q in range(NPY)
        if 0 <= p + down < NPX and 0 <= q + along < NPY
    ]
    return lax.ppermute(x, ALL, pairs)


def swapped(tiles):
    return lax.all_to_all(tiles, "py", split_axis=0, concat_axis=0, tiled=True)


def over_chips(rows):
    tiles = rows.reshape(NPX // 2, 8, 128)
    return lax.all_to_all(tiles, PX[:2], split_axis=0, concat_axis=0, tiled=True).reshape(rows.shape)


def body(density, external, orbitals, anchors, weights, degrees):
    row_place = lax.axis_index(PX)
    col_place = lax.axis_index("py")
    origin = jnp.stack([row_place * ROWS, col_place * COLS, 0])
    local = (anchors - origin[None, :]).astype(jnp.int32)
    own = jnp.pad(local.reshape(6), (0, 2))
    above = jnp.stack([own, moved(own, 1, 0), moved(own, 2, 0)])
    meta = jnp.concatenate([local[:, 0], weights, degrees, weights]).astype(jnp.int32)

    sine_y = [jnp.asarray(t) for t in SINE_Y]
    sine_z = jnp.asarray(SINE_Z)
    ey = jnp.asarray(EIGEN_Y)
    ez = lax.dynamic_slice(jnp.asarray(EIGEN_Z), (col_place * KZ, 0), (KZ, 1))
    chip_ez = lax.dynamic_slice(jnp.asarray(EIGEN_Z), (col_place * KZ + row_place // 2, 0), (1, 1))
    ez, chip_ez, above = lax.optimization_barrier((ez, chip_ez, above))
    places = jnp.stack([above, moved(above, 0, 1)], 1)[:, :, :6].reshape(36)

    planes = call(
        orbitals_in,
        shape(FRAG, 9, 8, 128),
        [pltpu.VMEM((2, 5, NORB * FRAG, 128), F32), pltpu.VMEM((3, 128, 128), F32)],
    )(orbitals.reshape(2, NORB * FRAG, FRAG * FRAG))
    tiles = call(forward_z, shape(NPY, KZ, ROWS * COLS), count=2)(density, sine_z)
    tiles = swapped(tiles)
    field, moments = call(
        forward_y,
        (shape(ROWS * KZ, NY), shape(2 * KZ, NY)),
        [pltpu.VMEM((ROWS * KZ, NY), F32)],
        count=5,
    )(tiles, *sine_y, ey, ez)

    core = lax.axis_index("px_2").reshape(1).astype(jnp.int32)
    other = lax.ppermute(moments, "px_2", [(0, 1), (1, 0)])
    chips = call(pair_moments, shape(128, 128), smem=(0,), count=5)(core, moments, other, ey, ez)
    chips = over_chips(chips)
    chips = call(scan_chips, shape(128, 128), count=3)(chips, ey, chip_ez)
    states = over_chips(chips)

    tiles = call(
        back_y, shape(NPY, KZ, ROWS * COLS), [pltpu.VMEM((ROWS * KZ, NY), F32)], smem=(0,), count=8
    )(core, field, other, states, *sine_y, ey, ez)
    tiles = swapped(tiles)
    groups = (8, 8, 4)
    grid = [pltpu.VMEM((2, ROWS, PADDED, 128), F32)]
    hartree_field, beside = call(
        back_z, [shape(ROWS, COLS, NZ), shape(20, FRAG, 128)], grid, smem=(0,), count=4
    )(places, tiles, external, sine_z)
    owned = call(cut_owned, [shape(n, FRAG, 128) for n in groups], grid, smem=(0,), count=3)(
        places, hartree_field, external
    )
    beside = moved(beside, 0, -1)
    next_rows = moved(owned[1] + beside[8:16], -1, 0)
    last_rows = moved(owned[2] + beside[16:], -2, 0)
    planes, scale, *shares = call(
        filter_fragments,
        [shape(FRAG, 9, 8, 128), shape(8, 128)] + [shape(n, FRAG, 128) for n in groups],
        [
            pltpu.VMEM((2, 40 * FRAG, 128), F32),
            pltpu.VMEM((3, 128, 128), F32),
            pltpu.VMEM((27, 8, 128), F32),
            pltpu.VMEM((FRAG, 9, 8, 128), F32),
            pltpu.VMEM((FRAG, 9, 8, 128), F32),
            pltpu.VMEM((2, 40 * FRAG, 128), F32),
        ],
        smem=(0,),
        count=6,
    )(meta, owned[0], beside, next_rows, last_rows, planes)
    received = [shares[0], moved(shares[1], 1, 0), moved(shares[2], 2, 0)]
    beside = moved(jnp.concatenate(received), 0, 1)
    filtered = call(
        orbitals_out,
        shape(2, NORB * FRAG, FRAG * FRAG),
        [pltpu.VMEM((2, 5, NORB * FRAG, 128), F32), pltpu.VMEM((3, 128, 128), F32)],
        count=2,
    )(planes, scale)
    density_owned = call(patch_owned, shape(ROWS, COLS, NZ), grid, smem=(0,), count=4)(places, *received)
    new_density = call(patch_beside, shape(ROWS, COLS, NZ), grid, smem=(0,), count=3)(
        places, density_owned, beside
    )
    return hartree_field, filtered.reshape(orbitals.shape), new_density


def solution(mesh):
    torus = Mesh(mesh.devices.reshape(8, 2, 2, NPY), ALL)
    grid = P(PX, "py", None)
    return jax.shard_map(
        body,
        mesh=torus,
        in_specs=(grid, grid, P(ALL, None, None, None), P(ALL, None), P(ALL), P(ALL)),
        out_specs=(grid, P(ALL, None, None, None), grid),
        check_vma=False,
    )
```

```python
import jax
import jax.numpy as jnp
import numpy as np
from jax import lax
from jax.experimental import pallas as pl
from jax.experimental.pallas import tpu as pltpu
from jax.sharding import Mesh
from jax.sharding import PartitionSpec as P

NX, NY, NZ = 512, 512, 256
NPX, NPY = 32, 16
ROWS, COLS = NX // NPX, NY // NPY
KZ = NZ // NPY
FRAG, NORB = 24, 8
PX = ("px_0", "px_1", "px_2")
ALL = PX + ("py",)
SCREENING, WINDOW_GAP, KINETIC_TOP = 0.002, 0.1, 6.0
STEPS = ((0, 0), (0, 1), (1, 0), (1, 1), (2, 0), (2, 1))
PADDED = COLS + 32 + FRAG
F32 = jnp.float32
BF16 = jnp.bfloat16
VMEM = pl.BlockSpec(memory_space=pltpu.VMEM)
SMEM = pl.BlockSpec(memory_space=pltpu.SMEM)


def sine_table(length):
    index = np.arange(1, length + 1, dtype=np.int64)
    product = index[:, None] * index[None, :] % (2 * length + 2)
    return np.sin(product * (np.pi / (length + 1))) * np.sqrt(2.0 / (length + 1))


def halves_of(table):
    high = np.asarray(table, np.float32).astype(BF16)
    low = (table - high.astype(np.float64)).astype(np.float32).astype(BF16)
    return high, low


def eigen_values(length):
    wave = np.arange(1, length + 1, dtype=np.float64) * (np.pi / (length + 1))
    return (4.0 * np.sin(wave / 2.0) ** 2).astype(np.float32)


SINE_Y = halves_of(sine_table(NY))
SINE_Z = np.stack(halves_of(sine_table(NZ)))
EIGEN_Y = eigen_values(NY)[None, :]
EIGEN_Z = eigen_values(NZ)[:, None]


def split2(x):
    high = x.astype(BF16)
    return high, (x - high.astype(F32)).astype(BF16)


def dot3(left, right, dims):
    def one(a, b):
        return lax.dot_general(a, b, (dims, ((), ())), preferred_element_type=F32)

    return one(left[0], right[0]) + (one(left[0], right[1]) + one(left[1], right[0]))


def call(kernel, outs, scratch=(), smem=(), count=1):
    return pl.pallas_call(
        kernel,
        out_shape=outs,
        in_specs=[SMEM if k in smem else VMEM for k in range(count)],
        out_specs=jax.tree.map(lambda _: VMEM, outs),
        scratch_shapes=list(scratch),
        compiler_params=pltpu.CompilerParams(vmem_limit_bytes=48 * 1024 * 1024),
    )


def shape(*dims):
    return jax.ShapeDtypeStruct(dims, F32)


def lanes(rows):
    return lax.broadcasted_iota(jnp.int32, (rows, 128), 1)


def rolled(x, by, axis=1):
    by %= x.shape[axis]
    return pltpu.roll(x, by, axis) if by else x


def decay(ey, ez):
    gap = ey + ez + SCREENING
    root = jnp.sqrt(gap + 0.25 * gap * gap)
    return 1.0 / (1.0 + 0.5 * gap + root), 0.5 / root


def forward_z(density, table, out):
    cells = density[...].reshape(ROWS * COLS, NZ)
    spectrum = dot3((table[0], table[1]), split2(cells), ((1,), (1,)))
    out[...] = spectrum.reshape(NPY, KZ, ROWS * COLS)


def block_power(rate):
    for _ in range(4):
        rate = rate * rate
    return rate


def put_rows(ref, first, value, width=8):
    for half in range(2):
        for k in range(4):
            rows = pl.ds(8 * width * half + first + k, 8, stride=width)
            ref[rows, :] = value[8 * half : 8 * half + 8, 128 * k : 128 * k + 128]


def take_rows(ref, first, width=8):
    return jnp.concatenate(
        [
            jnp.concatenate(
                [ref[pl.ds(8 * width * half + first + k, 8, stride=width), :] for half in range(2)], 0
            )
            for k in range(4)
        ],
        1,
    )


def pair_moments(core, own, other, ey, ez, out):
    power = block_power(decay(ey[...], ez[...])[0])
    upper = core[0] == 1
    high = jnp.where(upper, own[...], other[...])
    low = jnp.where(upper, other[...], own[...])
    put_rows(out, 0, high[:KZ] + power * low[:KZ], 16)
    put_rows(out, 4, low[KZ : 2 * KZ] + power * high[KZ : 2 * KZ], 16)
    corners = jnp.concatenate([low[2 * KZ : 2 * KZ + 1, :128], high[2 * KZ : 2 * KZ + 1, :128]], 0)
    corners = jnp.concatenate([corners, jnp.zeros((6, 128), F32)], 0)
    for chip in range(NPX // 2):
        out[16 * chip + 8 : 16 * chip + 16, :] = corners


def scan_chips(moments, ey, ez, out):
    rate, _ = decay(ey[...], ez[...])
    power = block_power(rate)
    power = power * power
    right, left = take_rows(moments, 0, 16), take_rows(moments, 4, 16)
    count = NPX // 2
    row = lax.broadcasted_iota(jnp.int32, (count, NY), 0)
    before, after = jnp.ones((count, NY), F32), jnp.ones((count, NY), F32)
    step = 1
    while step < count:
        right = right + power * jnp.where(row >= step, rolled(right, step, 0), 0.0)
        left = left + power * jnp.where(row < count - step, rolled(left, -step, 0), 0.0)
        upper = row & step != 0
        before = jnp.where(upper, before * power, before)
        after = jnp.where(upper, after, after * power)
        power = power * power
        step *= 2
    across = power * rate
    norm = rate / (1.0 - across * across)
    right_total, left_total = right[count - 1 :], left[:1]
    state = jnp.where(row >= 1, rolled(right, 1, 0), 0.0)
    put_rows(out, 0, state - norm * (left_total - across * right_total) * before)
    state = jnp.where(row < count - 1, rolled(left, -1, 0), 0.0)
    put_rows(out, 4, state - norm * (right_total - across * left_total) * after)


def forward_y(tiles, table_high, table_low, ey, ez, own_places, field_out, moment_out, merged):
    block = lanes(KZ) // COLS
    for row in range(ROWS):
        for tile in range(4):
            total = None
            for k in range(4):
                piece = tiles[4 * tile + k, :, row // 4 * 128 : row // 4 * 128 + 128]
                piece = rolled(piece, (k - row % 4) * COLS)
                total = piece if total is None else jnp.where(block == k, piece, total)
            merged[row * KZ : (row + 1) * KZ, tile * 128 : (tile + 1) * 128] = total
    field = dot3(split2(merged[...]), (table_high[...], table_low[...]), ((1,), (0,)))
    field_out[...] = field
    rate, _ = decay(ey[...], ez[...])
    first = field[:KZ]
    last = field[(ROWS - 1) * KZ :]
    for row in range(1, ROWS):
        first = field[row * KZ : (row + 1) * KZ] + rate * first
        back = ROWS - 1 - row
        last = field[back * KZ : (back + 1) * KZ] + rate * last
    moment_out[:KZ] = first
    moment_out[KZ : 2 * KZ] = last
    moment_out[2 * KZ :] = jnp.zeros((8, NY), F32)
    moment_out[2 * KZ :, :128] = own_places[...]


def back_y(core, field, other, states, table_high, table_low, ey, ez, tiles_out, solved):
    rate, scale = decay(ey[...], ez[...])
    power = block_power(rate)
    upper = core[0] == 1
    state, left = take_rows(states, 0), take_rows(states, 4)
    state = jnp.where(upper, other[:KZ] + power * state, state)
    left = jnp.where(upper, left, other[KZ : 2 * KZ] + power * left)
    for row in range(ROWS):
        state = field[row * KZ : (row + 1) * KZ] + rate * state
        solved[row * KZ : (row + 1) * KZ] = state
    for row in range(ROWS - 1, -1, -1):
        here = pl.ds(row * KZ, KZ)
        solved[here] = scale * (solved[here] + rate * left)
        left = field[here] + rate * left
    columns = dot3(split2(solved[...]), (table_high[...], table_low[...]), ((1,), (0,)))
    solved[...] = columns
    block = lanes(KZ) // COLS
    for peer in range(NPY):
        for tile in range(4):
            total = None
            for k in range(4):
                row = 4 * tile + k
                piece = solved[row * KZ : (row + 1) * KZ, peer // 4 * 128 : peer // 4 * 128 + 128]
                piece = rolled(piece, (k - peer % 4) * COLS)
                total = piece if total is None else jnp.where(block == k, piece, total)
            tiles_out[peer, :, tile * 128 : (tile + 1) * 128] = total


def slots_of(rows):
    return lanes(rows) // 32


def fill_grid(grid, potential):
    for half in range(2):
        grid[half, :, :32] = jnp.zeros((ROWS, 32, 128), F32)
        grid[half, :, 32 + COLS :] = jnp.zeros((ROWS, FRAG, 128), F32)
        grid[half, :, 32 : 32 + COLS] = potential[:, :, half * 128 : half * 128 + 128]


def cut_windows(places, grid, along, outs):
    lane = lanes(FRAG)
    slot_of = slots_of(FRAG)
    for down in range(3):
        groups = 8 if down < 2 else 4
        k = 2 * down + along

        def cut(number, carry, k=k, down=down, groups=groups):
            totals = []
            for part in range(4):
                total = None
                for slot in range(4):
                    frag = slot % 2
                    row = 4 * number + part + groups * (slot // 2)
                    col, depth = places[6 * k + 3 * frag + 1], places[6 * k + 3 * frag + 2]
                    cols = pl.ds(32 + col - 32 * along, FRAG)
                    window = jnp.where(lane >= depth, grid[0, row, cols, :], grid[1, row, cols, :])
                    window = pltpu.roll(window, (256 + 32 * slot - depth) & 127, 1)
                    total = window if total is None else jnp.where(slot_of == slot, window, total)
                totals.append(total)
            for part in range(4):
                if along:
                    outs[0][8 * down + 4 * number + part] = totals[part]
                else:
                    outs[down][4 * number + part] = totals[part]
            return carry

        lax.fori_loop(0, groups // 4, cut, 0)


def back_z(places, tiles, external, table, field_out, beside, grid):
    spectrum = tiles[...].reshape(NZ, ROWS * COLS)
    turned = spectrum.T
    field = dot3(split2(turned), (table[0], table[1]), ((1,), (0,)))
    field = field.reshape(ROWS, COLS, NZ)
    field_out[...] = field
    fill_grid(grid, field + external[...])
    cut_windows(places, grid, 1, (beside,))


def cut_owned(places, field, external, *rest):
    fill_grid(rest[3], field[...] + external[...])
    cut_windows(places, rest[3], 0, rest[:3])


def orbitals_in(orbitals, out, strips, turned):
    for frag in range(2):
        for tile in range(5):
            width = min(128, FRAG * FRAG - tile * 128)
            strips[frag, tile, :, :width] = orbitals[frag, :, tile * 128 : tile * 128 + width]
    lane = lanes(8)

    def plane(x, place):
        rows = []
        for yc in range(8):
            tile, off = divmod(72 * yc, 128)
            for frag in range(2):
                piece = rolled(strips[frag, tile, pl.ds(x, 8, stride=FRAG), :], -off)
                if off + 72 > 128:
                    other = rolled(strips[frag, tile + 1, pl.ds(x, 8, stride=FRAG), :], -off)
                    piece = jnp.where(lane < 128 - off, piece, other)
                rows.append(piece)
        place[...] = jnp.concatenate(rows, 0).T

    def planes(number, carry):
        for part in range(3):
            plane(3 * number + part, turned.at[part])
        for part in range(3):
            for k in range(9):
                rows = pl.ds(k // 3 * FRAG + k % 3, 8, stride=3)
                out[3 * number + part, k] = turned.at[part][rows, :]
        return carry

    lax.fori_loop(0, FRAG // 3, planes, 0)


def orbitals_out(planes, scale, out, strips, turned):
    lane = lanes(8)
    factor = scale[...]

    def plane(x, rows):
        for frag in range(2):
            for tile in range(5):
                total = None
                for yc in range(8):
                    start = 72 * yc - 128 * tile
                    if -72 < start < 128:
                        piece = rows[(2 * yc + frag) * 8 : (2 * yc + frag) * 8 + 8]
                        piece = rolled(piece, start)
                        if total is None:
                            total = piece
                        else:
                            total = jnp.where(lane >= start, piece, total)
                strips[frag, tile, pl.ds(x, 8, stride=FRAG), :] = total

    def trip(number, carry):
        for part in range(3):
            for k in range(9):
                rows = pl.ds(k // 3 * FRAG + k % 3, 8, stride=3)
                turned.at[part][rows, :] = planes[3 * number + part, k] * factor
        rows = [turned[part].T for part in range(3)]
        for part in range(3):
            plane(3 * number + part, rows[part])
        return carry

    lax.fori_loop(0, FRAG // 3, trip, 0)
    for frag in range(2):
        for tile in range(5):
            width = min(128, FRAG * FRAG - tile * 128)
            out[frag, :, tile * 128 : tile * 128 + width] = strips[frag, tile, :, :width]


def spread(value, lane):
    values = [value]
    for step in (4, 2, 1):
        clear = lane & step == 0
        values = [
            part
            for v in values
            for part in (
                jnp.where(clear, v, rolled(v, step)),
                jnp.where(clear, rolled(v, -step), v),
            )
        ]
    return values


def gather_sums(values, lane):
    for step in (4, 2, 1):
        clear = lane & step == 0
        count = len(values) // 2
        values = [
            jnp.where(
                clear,
                values[k] + rolled(values[k], -step),
                values[k + count] + rolled(values[k + count], step),
            )
            for k in range(count)
        ]
    return values[0]


def total_of(x):
    return jnp.sum(jnp.sum(x, axis=0, keepdims=True), axis=1, keepdims=True)


def filter_fragments(meta, *refs):
    owned, beside, next_rows, last_rows, start = refs[:5]
    out, scale_out = refs[5:7]
    shares = refs[7:10]
    boxes, turned, compact, potential, other, spilled = refs[10:]
    lane = lanes(8)
    sub = lax.broadcasted_iota(jnp.int32, (8, 128), 0)
    second = (lane // 8) % 2 == 1
    for down in range(3):
        groups = 8 if down < 2 else 4

        def unpack(number, carry, down=down, groups=groups):
            moved_windows = []
            for part in range(4):
                group = 4 * number + part
                if down == 0:
                    both = owned[group] + beside[group]
                else:
                    both = (next_rows if down == 1 else last_rows)[group]
                moved_windows.append([rolled(both, -32 * slot) for slot in range(4)])
            for part in range(4):
                for slot in range(4):
                    row = 16 * down + 4 * number + part + groups * (slot // 2)
                    rows = pl.ds(pl.multiple_of(row * FRAG, 8), FRAG)
                    boxes[slot % 2, rows, :] = moved_windows[part][slot]
            return carry

        lax.fori_loop(0, groups // 4, unpack, 0)
    lowest = None
    for part in range(3):
        rows = []
        for yc in range(8):
            for frag in range(2):
                base = (meta[frag] + 8 * part) * FRAG + 3 * yc
                took = [boxes[frag, pl.ds(base + yi, 8, stride=FRAG), :] for yi in range(3)]
                rows.append(
                    jnp.where(
                        lane < FRAG,
                        took[0],
                        jnp.where(lane < 2 * FRAG, rolled(took[1], FRAG), rolled(took[2], 2 * FRAG)),
                    )
                )
        turned[part] = jnp.concatenate(rows, 0).T
    for part in range(3):
        for k in range(9):
            value = turned.at[part][pl.ds(k // 3 * FRAG + k % 3, 8, stride=3), :]
            compact[9 * part + k] = value
            lowest = value if lowest is None else jnp.minimum(lowest, value)
            highest = value if part + k == 0 else jnp.maximum(highest, value)

    def window(keep):
        low = jnp.where(keep, lowest, jnp.inf)
        high = jnp.where(keep, highest, -jnp.inf)
        low = jnp.min(jnp.min(low, axis=0, keepdims=True), axis=1, keepdims=True) + WINDOW_GAP
        high = jnp.max(jnp.max(high, axis=0, keepdims=True), axis=1, keepdims=True) + KINETIC_TOP
        return 0.5 * (high + low), 0.5 * (high - low)

    centre_0, half_0 = window(~second)
    centre_1, half_1 = window(second)
    centre = jnp.where(second, centre_1, centre_0)
    inverse = 1.0 / jnp.where(second, half_1, half_0)
    for part in range(3):
        for k in range(9):
            value = -2.0 * (3.0 + compact[9 * part + k] - centre)
            for x, wide in enumerate(spread(value, lane)):
                potential[8 * part + x, k] = wide
    odd_scale = -inverse
    even_scale = inverse * inverse
    degree = jnp.where(second, meta[5], meta[4])

    def apply(source, target, earlier=None, initial=False, even=False, step=None):
        if step is not None:
            live, just_done = step <= degree, step == degree + 1
        earlier = target if earlier is None else earlier

        def chunk(number, carry):
            behind, here = list(carry[:9]), list(carry[9:])
            for k4 in range(24):
                x = 24 * number + k4
                ahead_x = jnp.minimum(x + 1, FRAG - 1)
                ahead = [source[ahead_x, k] for k in range(9)]
                if k4 == 23:
                    ahead = [jnp.where(x + 1 < FRAG, v, 0.0) for v in ahead]
                for k in range(9):
                    yi, zi = divmod(k, 3)
                    total = behind[k] + ahead[k]
                    if yi > 0:
                        total = total + here[k - 3]
                    else:
                        total = total + jnp.where(lane >= 16, rolled(here[6 + zi], 16), 0.0)
                    if yi < 2:
                        total = total + here[k + 3]
                    else:
                        total = total + jnp.where(lane < 112, rolled(here[zi], -16), 0.0)
                    if zi > 0:
                        total = total + here[k - 1]
                    else:
                        total = total + jnp.where(sub >= 1, rolled(here[k + 2], 1, 0), 0.0)
                    if zi < 2:
                        total = total + here[k + 1]
                    else:
                        total = total + jnp.where(sub < 7, rolled(here[k - 2], -1, 0), 0.0)
                    following = potential[x, k] * here[k] + total
                    if initial:
                        following = 0.5 * following
                    else:
                        past = earlier[x, k]
                        following = even_scale * following - past if even else following - past
                    if step is not None:
                        kept = jnp.where(just_done, odd_scale * here[k], past)
                        following = jnp.where(live, following, kept)
                    target[x, k] = following
                behind, here = here, ahead
            return tuple(behind + here)

        zero = [jnp.zeros((8, 128), F32)] * 9
        lax.fori_loop(0, 1, chunk, tuple(zero + [source[0, k] for k in range(9)]))

    apply(start, other, initial=True)
    apply(other, out, earlier=start, even=True)
    fewest = jnp.minimum(meta[4], meta[5])
    most = jnp.maximum(meta[4], meta[5])
    plain = (fewest - 2) // 2
    pairs = (most - 1) // 2

    def free_pair(pair, carry):
        apply(out, other)
        apply(other, out, even=True)
        return carry

    def held_pair(pair, carry):
        apply(out, other)
        apply(other, out, even=True, step=2 * pair + 4)
        return carry

    lax.fori_loop(0, plain, free_pair, 0)
    lax.fori_loop(plain, pairs, held_pair, 0)

    def squares(x, sums):
        return tuple(sums[k] + out[x, k] * out[x, k] for k in range(9))

    sums = lax.fori_loop(0, FRAG, squares, (jnp.zeros((8, 128), F32),) * 9)
    sums = sum(sums[1:], sums[0])
    sums = jnp.sum(sums, axis=0, keepdims=True)
    sums = jnp.broadcast_to(sums, (8, 128))
    for step in (16, 32, 64):
        sums = sums + rolled(sums, step)
    scale = jnp.sqrt(float(FRAG**3) / (sums + 1e-06))
    scale_out[...] = scale
    weight = jnp.where(second, meta[3], meta[2]).astype(F32) / NORB

    def clear(row, carry):
        for frag in range(2):
            spilled[frag, pl.ds(pl.multiple_of(row * FRAG, 8), FRAG), :] = jnp.zeros((FRAG, 128), F32)
        return carry

    lax.fori_loop(0, 40, clear, 0)
    for part in range(3):
        for k in range(9):
            values = []
            for x in range(8):
                value = out[8 * part + x, k] * scale
                values.append(value * value)
            turned.at[part][pl.ds(k // 3 * FRAG + k % 3, 8, stride=3), :] = gather_sums(values, lane) * weight
    for part in range(3):
        rows = turned[part].T
        for yc in range(8):
            for frag in range(2):
                piece = rows[(2 * yc + frag) * 8 : (2 * yc + frag) * 8 + 8]
                base = (meta[frag] + 8 * part) * FRAG + 3 * yc
                for yi in range(3):
                    spilled[frag, pl.ds(base + yi, 8, stride=FRAG), :] = rolled(piece, -FRAG * yi)
    slot_of = slots_of(FRAG)
    for down in range(3):
        groups = 8 if down < 2 else 4

        def share(number, carry, down=down, groups=groups):
            totals = []
            for part in range(4):
                total = None
                for slot in range(4):
                    row = 16 * down + 4 * number + part + groups * (slot // 2)
                    piece = spilled[slot % 2, pl.ds(pl.multiple_of(row * FRAG, 8), FRAG), :]
                    piece = rolled(piece, 32 * slot)
                    total = piece if total is None else jnp.where(slot_of == slot, piece, total)
                totals.append(total)
            for part in range(4):
                shares[down][4 * number + part] = totals[part]
            return carry

        lax.fori_loop(0, groups // 4, share, 0)


def add_windows(places, grid, along, shares):
    lane = lanes(FRAG)
    for down in range(3):
        groups = 8 if down < 2 else 4
        k = 2 * down + along

        def add(number, carry, k=k, down=down, groups=groups):
            pieces = []
            for part in range(4):
                group = 4 * number + part
                both = shares[0][8 * down + group] if along else shares[down][group]
                for slot in range(4):
                    depth = places[6 * k + 3 * (slot % 2) + 2]
                    pieces.append(pltpu.roll(both, (256 + depth - 32 * slot) & 127, 1))
            for part in range(4):
                for slot in range(4):
                    frag = slot % 2
                    row = 4 * number + part + groups * (slot // 2)
                    col, depth = places[6 * k + 3 * frag + 1], places[6 * k + 3 * frag + 2]
                    piece = jnp.where(((lane - depth) & 127) < FRAG, pieces[4 * part + slot], 0.0)
                    cols = pl.ds(32 + col - 32 * along, FRAG)
                    grid[0, row, cols, :] += jnp.where(lane >= depth, piece, 0.0)
                    grid[1, row, cols, :] += jnp.where(lane >= depth, 0.0, piece)
            return carry

        lax.fori_loop(0, groups // 4, add, 0)


def patch_owned(places, first, second, third, out, grid):
    def clear(row, carry):
        for half in range(2):
            grid[half, row] = jnp.zeros((PADDED, 128), F32)
        return carry

    lax.fori_loop(0, ROWS, clear, 0)
    add_windows(places, grid, 0, (first, second, third))
    for half in range(2):
        out[:, :, half * 128 : half * 128 + 128] = grid[half, :, 32 : 32 + COLS]


def patch_beside(places, owned, beside, out, grid):
    fill_grid(grid, owned[...])
    add_windows(places, grid, 1, (beside,))
    for half in range(2):
        out[:, :, half * 128 : half * 128 + 128] = grid[half, :, 32 : 32 + COLS]


def moved(x, down, along):
    pairs = [
        (p * NPY + q, (p + down) * NPY + q + along)
        for p in range(NPX)
        for q in range(NPY)
        if 0 <= p + down < NPX and 0 <= q + along < NPY
    ]
    return lax.ppermute(x, ALL, pairs)


def swapped(tiles):
    return lax.all_to_all(tiles, "py", split_axis=0, concat_axis=0, tiled=True)


def over_chips(rows):
    tiles = rows.reshape(NPX // 2, -1, 128)
    return lax.all_to_all(tiles, PX[:2], split_axis=0, concat_axis=0, tiled=True).reshape(rows.shape)


def body(density, external, orbitals, anchors, weights, degrees):
    row_place = lax.axis_index(PX)
    col_place = lax.axis_index("py")
    origin = jnp.stack([row_place * ROWS, col_place * COLS, 0])
    local = (anchors - origin[None, :]).astype(jnp.int32)
    own = jnp.pad(local.reshape(6), (0, 2))
    own_places = jnp.pad(own.astype(F32)[None, :], ((0, 7), (0, 120)))
    meta = jnp.concatenate([local[:, 0], weights, degrees, weights]).astype(jnp.int32)

    sine_y = [jnp.asarray(t) for t in SINE_Y]
    sine_z = jnp.asarray(SINE_Z)
    ey = jnp.asarray(EIGEN_Y)
    ez = lax.dynamic_slice(jnp.asarray(EIGEN_Z), (col_place * KZ, 0), (KZ, 1))
    chip = row_place // 2
    chip_ez = lax.dynamic_slice(jnp.asarray(EIGEN_Z), (col_place * KZ + chip, 0), (1, 1))
    ez, chip_ez, own_places = lax.optimization_barrier((ez, chip_ez, own_places))
    planes = call(
        orbitals_in,
        shape(FRAG, 9, 8, 128),
        [pltpu.VMEM((2, 5, NORB * FRAG, 128), F32), pltpu.VMEM((3, 128, 128), F32)],
    )(orbitals.reshape(2, NORB * FRAG, FRAG * FRAG))
    tiles = call(forward_z, shape(NPY, KZ, ROWS * COLS), count=2)(density, sine_z)
    tiles = swapped(tiles)
    field, moments = call(
        forward_y,
        (shape(ROWS * KZ, NY), shape(2 * KZ + 8, NY)),
        [pltpu.VMEM((ROWS * KZ, NY), F32)],
        count=6,
    )(tiles, *sine_y, ey, ez, own_places)

    core = lax.axis_index("px_2").reshape(1).astype(jnp.int32)
    other = lax.ppermute(moments, "px_2", [(0, 1), (1, 0)])
    chips = call(pair_moments, shape(256, 128), smem=(0,), count=5)(core, moments, other, ey, ez)
    chips = over_chips(chips)
    states = over_chips(call(scan_chips, shape(128, 128), count=3)(chips, ey, chip_ez))
    before = lax.dynamic_slice(chips, (16 * jnp.maximum(chip - 1, 0) + 8, 0), (2, 8)).astype(jnp.int32)
    mate = other[2 * KZ, :8].astype(jnp.int32)
    even = core[0] == 0
    above = jnp.stack([own, jnp.where(even, before[1], mate), jnp.where(even, before[0], before[1])])
    above, states = lax.optimization_barrier((above, states))
    places = jnp.stack([above, moved(above, 0, 1)], 1)[:, :, :6].reshape(36)

    tiles = call(
        back_y, shape(NPY, KZ, ROWS * COLS), [pltpu.VMEM((ROWS * KZ, NY), F32)], smem=(0,), count=8
    )(core, field, other, states, *sine_y, ey, ez)
    tiles = swapped(tiles)
    groups = (8, 8, 4)
    grid = [pltpu.VMEM((2, ROWS, PADDED, 128), F32)]
    hartree_field, beside = call(
        back_z, [shape(ROWS, COLS, NZ), shape(20, FRAG, 128)], grid, smem=(0,), count=4
    )(places, tiles, external, sine_z)
    owned = call(cut_owned, [shape(n, FRAG, 128) for n in groups], grid, smem=(0,), count=3)(
        places, hartree_field, external
    )
    beside = moved(beside, 0, -1)
    next_rows = moved(owned[1] + beside[8:16], -1, 0)
    last_rows = moved(owned[2] + beside[16:], -2, 0)
    planes, scale, *shares = call(
        filter_fragments,
        [shape(FRAG, 9, 8, 128), shape(8, 128)] + [shape(n, FRAG, 128) for n in groups],
        [
            pltpu.VMEM((2, 40 * FRAG, 128), F32),
            pltpu.VMEM((3, 128, 128), F32),
            pltpu.VMEM((27, 8, 128), F32),
            pltpu.VMEM((FRAG, 9, 8, 128), F32),
            pltpu.VMEM((FRAG, 9, 8, 128), F32),
            pltpu.VMEM((2, 40 * FRAG, 128), F32),
        ],
        smem=(0,),
        count=6,
    )(meta, owned[0], beside, next_rows, last_rows, planes)
    received = [shares[0], moved(shares[1], 1, 0), moved(shares[2], 2, 0)]
    beside = moved(jnp.concatenate(received), 0, 1)
    filtered = call(
        orbitals_out,
        shape(2, NORB * FRAG, FRAG * FRAG),
        [pltpu.VMEM((2, 5, NORB * FRAG, 128), F32), pltpu.VMEM((3, 128, 128), F32)],
        count=2,
    )(planes, scale)
    density_owned = call(patch_owned, shape(ROWS, COLS, NZ), grid, smem=(0,), count=4)(places, *received)
    new_density = call(patch_beside, shape(ROWS, COLS, NZ), grid, smem=(0,), count=3)(
        places, density_owned, beside
    )
    return hartree_field, filtered.reshape(orbitals.shape), new_density


def solution(mesh):
    torus = Mesh(mesh.devices.reshape(8, 2, 2, NPY), ALL)
    grid = P(PX, "py", None)
    return jax.shard_map(
        body,
        mesh=torus,
        in_specs=(grid, grid, P(ALL, None, None, None), P(ALL, None), P(ALL), P(ALL)),
        out_specs=(grid, P(ALL, None, None, None), grid),
        check_vma=False,
    )
```

```python
import jax
import jax.numpy as jnp
import numpy as np
from jax import lax
from jax.experimental import pallas as pl
from jax.experimental.pallas import tpu as pltpu
from jax.sharding import Mesh
from jax.sharding import PartitionSpec as P

NX, NY, NZ = 512, 512, 256
NPX, NPY = 32, 16
ROWS, COLS = NX // NPX, NY // NPY
KZ = NZ // NPY
FRAG, NORB = 24, 8
PX = ("px_0", "px_1", "px_2")
ALL = PX + ("py",)
SCREENING, WINDOW_GAP, KINETIC_TOP = 0.002, 0.1, 6.0
STEPS = ((0, 0), (0, 1), (1, 0), (1, 1), (2, 0), (2, 1))
PADDED = COLS + 32 + FRAG
F32 = jnp.float32
BF16 = jnp.bfloat16
VMEM = pl.BlockSpec(memory_space=pltpu.VMEM)
SMEM = pl.BlockSpec(memory_space=pltpu.SMEM)


def sine_table(length):
    index = np.arange(1, length + 1, dtype=np.int64)
    product = index[:, None] * index[None, :] % (2 * length + 2)
    return np.sin(product * (np.pi / (length + 1))) * np.sqrt(2.0 / (length + 1))


def halves_of(table):
    high = np.asarray(table, np.float32).astype(BF16)
    low = (table - high.astype(np.float64)).astype(np.float32).astype(BF16)
    return high, low


def eigen_values(length):
    wave = np.arange(1, length + 1, dtype=np.float64) * (np.pi / (length + 1))
    return (4.0 * np.sin(wave / 2.0) ** 2).astype(np.float32)


SINE_Y = halves_of(sine_table(NY))
SINE_Z = np.stack(halves_of(sine_table(NZ)))
EIGEN_Y = eigen_values(NY)[None, :]
EIGEN_Z = eigen_values(NZ)[:, None]


def split2(x):
    high = x.astype(BF16)
    return high, (x - high.astype(F32)).astype(BF16)


def dot3(left, right, dims):
    def one(a, b):
        return lax.dot_general(a, b, (dims, ((), ())), preferred_element_type=F32)

    return one(left[0], right[0]) + (one(left[0], right[1]) + one(left[1], right[0]))


def call(kernel, outs, scratch=(), smem=(), count=1):
    return pl.pallas_call(
        kernel,
        out_shape=outs,
        in_specs=[SMEM if k in smem else VMEM for k in range(count)],
        out_specs=jax.tree.map(lambda _: VMEM, outs),
        scratch_shapes=list(scratch),
        compiler_params=pltpu.CompilerParams(vmem_limit_bytes=48 * 1024 * 1024),
    )


def shape(*dims):
    return jax.ShapeDtypeStruct(dims, F32)


def lanes(rows):
    return lax.broadcasted_iota(jnp.int32, (rows, 128), 1)


def rolled(x, by, axis=1):
    by %= x.shape[axis]
    return pltpu.roll(x, by, axis) if by else x


def decay(ey, ez):
    gap = ey + ez + SCREENING
    root = jnp.sqrt(gap + 0.25 * gap * gap)
    return 1.0 / (1.0 + 0.5 * gap + root), 0.5 / root


def forward_z(density, table, out):
    cells = density[...].reshape(ROWS * COLS, NZ)
    spectrum = dot3((table[0], table[1]), split2(cells), ((1,), (1,)))
    out[...] = spectrum.reshape(NPY, KZ, ROWS * COLS)


def scan_powers(place, ey, ez, power_out, weight_out, ends_out):
    rate, _ = decay(ey[...], ez[...])
    power = rate
    for _ in range(4):
        power = power * power
    before = jnp.ones((KZ, NY), F32)
    after = before
    for bit in range(5):
        upper = (place[0] >> bit) % 2 == 1
        power_out[bit] = power
        weight_out[bit] = jnp.where(upper, before, after)
        before, after = jnp.where(upper, before * power, before), jnp.where(upper, after, after * power)
        power = power * power
    ends_out[0] = before
    ends_out[1] = after


def forward_y(tiles, table_high, table_low, ey, ez, field_out, moment_out, merged):
    block = lanes(KZ) // COLS
    for row in range(ROWS):
        for tile in range(4):
            total = None
            for k in range(4):
                piece = tiles[4 * tile + k, :, row // 4 * 128 : row // 4 * 128 + 128]
                piece = rolled(piece, (k - row % 4) * COLS)
                total = piece if total is None else jnp.where(block == k, piece, total)
            merged[row * KZ : (row + 1) * KZ, tile * 128 : (tile + 1) * 128] = total
    field = dot3(split2(merged[...]), (table_high[...], table_low[...]), ((1,), (0,)))
    field_out[...] = field
    rate, _ = decay(ey[...], ez[...])
    first = field[:KZ]
    last = field[(ROWS - 1) * KZ :]
    for row in range(1, ROWS):
        first = field[row * KZ : (row + 1) * KZ] + rate * first
        back = ROWS - 1 - row
        last = field[back * KZ : (back + 1) * KZ] + rate * last
    moment_out[:KZ] = first
    moment_out[KZ:] = last


def back_y(field, totals, right, left, ends, table_high, table_low, ey, ez, tiles_out, solved):
    rate, scale = decay(ey[...], ez[...])
    across = rate
    for _ in range(9):
        across = across * across
    across = across * rate
    norm = rate / (1.0 - across * across)
    right_total, left_total = totals[:KZ], totals[KZ:]
    state = right[...] - norm * (left_total - across * right_total) * ends[0]
    left = left[...] - norm * (right_total - across * left_total) * ends[1]
    for row in range(ROWS):
        state = field[row * KZ : (row + 1) * KZ] + rate * state
        solved[row * KZ : (row + 1) * KZ] = state
    for row in range(ROWS - 1, -1, -1):
        here = pl.ds(row * KZ, KZ)
        solved[here] = scale * (solved[here] + rate * left)
        left = field[here] + rate * left
    columns = dot3(split2(solved[...]), (table_high[...], table_low[...]), ((1,), (0,)))
    solved[...] = columns
    block = lanes(KZ) // COLS
    for peer in range(NPY):
        for tile in range(4):
            total = None
            for k in range(4):
                row = 4 * tile + k
                piece = solved[row * KZ : (row + 1) * KZ, peer // 4 * 128 : peer // 4 * 128 + 128]
                piece = rolled(piece, (k - peer % 4) * COLS)
                total = piece if total is None else jnp.where(block == k, piece, total)
            tiles_out[peer, :, tile * 128 : (tile + 1) * 128] = total


def slots_of(rows):
    return lanes(rows) // 32


def fill_grid(grid, potential):
    for half in range(2):
        grid[half, :, :32] = jnp.zeros((ROWS, 32, 128), F32)
        grid[half, :, 32 + COLS :] = jnp.zeros((ROWS, FRAG, 128), F32)
        grid[half, :, 32 : 32 + COLS] = potential[:, :, half * 128 : half * 128 + 128]


def cut_windows(places, grid, along, outs):
    lane = lanes(FRAG)
    slot_of = slots_of(FRAG)
    for down in range(3):
        groups = 8 if down < 2 else 4
        k = 2 * down + along

        def cut(number, carry, k=k, down=down, groups=groups):
            totals = []
            for part in range(4):
                total = None
                for slot in range(4):
                    frag = slot % 2
                    row = 4 * number + part + groups * (slot // 2)
                    col, depth = places[6 * k + 3 * frag + 1], places[6 * k + 3 * frag + 2]
                    cols = pl.ds(32 + col - 32 * along, FRAG)
                    window = jnp.where(lane >= depth, grid[0, row, cols, :], grid[1, row, cols, :])
                    window = pltpu.roll(window, (256 + 32 * slot - depth) & 127, 1)
                    total = window if total is None else jnp.where(slot_of == slot, window, total)
                totals.append(total)
            for part in range(4):
                if along:
                    outs[0][8 * down + 4 * number + part] = totals[part]
                else:
                    outs[down][4 * number + part] = totals[part]
            return carry

        lax.fori_loop(0, groups // 4, cut, 0)


def back_z(places, tiles, external, table, field_out, beside, grid):
    spectrum = tiles[...].reshape(NZ, ROWS * COLS)
    turned = spectrum.T
    field = dot3(split2(turned), (table[0], table[1]), ((1,), (0,)))
    field = field.reshape(ROWS, COLS, NZ)
    field_out[...] = field
    fill_grid(grid, field + external[...])
    cut_windows(places, grid, 1, (beside,))


def cut_owned(places, field, external, *rest):
    fill_grid(rest[3], field[...] + external[...])
    cut_windows(places, rest[3], 0, rest[:3])


def orbitals_in(orbitals, out, strips, turned):
    for frag in range(2):
        for tile in range(5):
            width = min(128, FRAG * FRAG - tile * 128)
            strips[frag, tile, :, :width] = orbitals[frag, :, tile * 128 : tile * 128 + width]
    lane = lanes(8)

    def plane(x, place):
        rows = []
        for yc in range(8):
            tile, off = divmod(72 * yc, 128)
            for frag in range(2):
                piece = rolled(strips[frag, tile, pl.ds(x, 8, stride=FRAG), :], -off)
                if off + 72 > 128:
                    other = rolled(strips[frag, tile + 1, pl.ds(x, 8, stride=FRAG), :], -off)
                    piece = jnp.where(lane < 128 - off, piece, other)
                rows.append(piece)
        place[...] = jnp.concatenate(rows, 0).T

    def planes(number, carry):
        for part in range(3):
            plane(3 * number + part, turned.at[part])
        for part in range(3):
            for k in range(9):
                rows = pl.ds(k // 3 * FRAG + k % 3, 8, stride=3)
                out[3 * number + part, k] = turned.at[part][rows, :]
        return carry

    lax.fori_loop(0, FRAG // 3, planes, 0)


def orbitals_out(planes, scale, out, strips, turned):
    lane = lanes(8)
    factor = scale[...]

    def plane(x, rows):
        for frag in range(2):
            for tile in range(5):
                total = None
                for yc in range(8):
                    start = 72 * yc - 128 * tile
                    if -72 < start < 128:
                        piece = rows[(2 * yc + frag) * 8 : (2 * yc + frag) * 8 + 8]
                        piece = rolled(piece, start)
                        if total is None:
                            total = piece
                        else:
                            total = jnp.where(lane >= start, piece, total)
                strips[frag, tile, pl.ds(x, 8, stride=FRAG), :] = total

    def trip(number, carry):
        for part in range(3):
            for k in range(9):
                rows = pl.ds(k // 3 * FRAG + k % 3, 8, stride=3)
                turned.at[part][rows, :] = planes[3 * number + part, k] * factor
        rows = [turned[part].T for part in range(3)]
        for part in range(3):
            plane(3 * number + part, rows[part])
        return carry

    lax.fori_loop(0, FRAG // 3, trip, 0)
    for frag in range(2):
        for tile in range(5):
            width = min(128, FRAG * FRAG - tile * 128)
            out[frag, :, tile * 128 : tile * 128 + width] = strips[frag, tile, :, :width]


def spread(value, lane):
    values = [value]
    for step in (4, 2, 1):
        clear = lane & step == 0
        values = [
            part
            for v in values
            for part in (
                jnp.where(clear, v, rolled(v, step)),
                jnp.where(clear, rolled(v, -step), v),
            )
        ]
    return values


def gather_sums(values, lane):
    for step in (4, 2, 1):
        clear = lane & step == 0
        count = len(values) // 2
        values = [
            jnp.where(
                clear,
                values[k] + rolled(values[k], -step),
                values[k + count] + rolled(values[k + count], step),
            )
            for k in range(count)
        ]
    return values[0]


def total_of(x):
    return jnp.sum(jnp.sum(x, axis=0, keepdims=True), axis=1, keepdims=True)


def filter_fragments(meta, *refs):
    owned, beside, next_rows, last_rows, start = refs[:5]
    out, scale_out = refs[5:7]
    shares = refs[7:10]
    boxes, turned, compact, potential, other, spilled = refs[10:]
    lane = lanes(8)
    sub = lax.broadcasted_iota(jnp.int32, (8, 128), 0)
    second = (lane // 8) % 2 == 1
    for down in range(3):
        groups = 8 if down < 2 else 4

        def unpack(number, carry, down=down, groups=groups):
            moved_windows = []
            for part in range(4):
                group = 4 * number + part
                if down == 0:
                    both = owned[group] + beside[group]
                else:
                    both = (next_rows if down == 1 else last_rows)[group]
                moved_windows.append([rolled(both, -32 * slot) for slot in range(4)])
            for part in range(4):
                for slot in range(4):
                    row = 16 * down + 4 * number + part + groups * (slot // 2)
                    rows = pl.ds(pl.multiple_of(row * FRAG, 8), FRAG)
                    boxes[slot % 2, rows, :] = moved_windows[part][slot]
            return carry

        lax.fori_loop(0, groups // 4, unpack, 0)
    lowest = None
    for part in range(3):
        rows = []
        for yc in range(8):
            for frag in range(2):
                base = (meta[frag] + 8 * part) * FRAG + 3 * yc
                took = [boxes[frag, pl.ds(base + yi, 8, stride=FRAG), :] for yi in range(3)]
                rows.append(
                    jnp.where(
                        lane < FRAG,
                        took[0],
                        jnp.where(lane < 2 * FRAG, rolled(took[1], FRAG), rolled(took[2], 2 * FRAG)),
                    )
                )
        turned[part] = jnp.concatenate(rows, 0).T
    for part in range(3):
        for k in range(9):
            value = turned.at[part][pl.ds(k // 3 * FRAG + k % 3, 8, stride=3), :]
            compact[9 * part + k] = value
            lowest = value if lowest is None else jnp.minimum(lowest, value)
            highest = value if part + k == 0 else jnp.maximum(highest, value)

    def window(keep):
        low = jnp.where(keep, lowest, jnp.inf)
        high = jnp.where(keep, highest, -jnp.inf)
        low = jnp.min(jnp.min(low, axis=0, keepdims=True), axis=1, keepdims=True) + WINDOW_GAP
        high = jnp.max(jnp.max(high, axis=0, keepdims=True), axis=1, keepdims=True) + KINETIC_TOP
        return 0.5 * (high + low), 0.5 * (high - low)

    centre_0, half_0 = window(~second)
    centre_1, half_1 = window(second)
    centre = jnp.where(second, centre_1, centre_0)
    inverse = 1.0 / jnp.where(second, half_1, half_0)
    for part in range(3):
        for k in range(9):
            value = -2.0 * (3.0 + compact[9 * part + k] - centre)
            for x, wide in enumerate(spread(value, lane)):
                potential[8 * part + x, k] = wide
    odd_scale = -inverse
    even_scale = inverse * inverse
    degree = jnp.where(second, meta[5], meta[4])

    def apply(source, target, earlier=None, initial=False, even=False, step=None):
        if step is not None:
            live, just_done = step <= degree, step == degree + 1
        earlier = target if earlier is None else earlier

        def chunk(number, carry):
            behind, here = list(carry[:9]), list(carry[9:])
            for k4 in range(24):
                x = 24 * number + k4
                ahead_x = jnp.minimum(x + 1, FRAG - 1)
                ahead = [source[ahead_x, k] for k in range(9)]
                if k4 == 23:
                    ahead = [jnp.where(x + 1 < FRAG, v, 0.0) for v in ahead]
                for k in range(9):
                    yi, zi = divmod(k, 3)
                    total = behind[k] + ahead[k]
                    if yi > 0:
                        total = total + here[k - 3]
                    else:
                        total = total + jnp.where(lane >= 16, rolled(here[6 + zi], 16), 0.0)
                    if yi < 2:
                        total = total + here[k + 3]
                    else:
                        total = total + jnp.where(lane < 112, rolled(here[zi], -16), 0.0)
                    if zi > 0:
                        total = total + here[k - 1]
                    else:
                        total = total + jnp.where(sub >= 1, rolled(here[k + 2], 1, 0), 0.0)
                    if zi < 2:
                        total = total + here[k + 1]
                    else:
                        total = total + jnp.where(sub < 7, rolled(here[k - 2], -1, 0), 0.0)
                    following = potential[x, k] * here[k] + total
                    if initial:
                        following = 0.5 * following
                    else:
                        past = earlier[x, k]
                        following = even_scale * following - past if even else following - past
                    if step is not None:
                        kept = jnp.where(just_done, odd_scale * here[k], past)
                        following = jnp.where(live, following, kept)
                    target[x, k] = following
                behind, here = here, ahead
            return tuple(behind + here)

        zero = [jnp.zeros((8, 128), F32)] * 9
        lax.fori_loop(0, 1, chunk, tuple(zero + [source[0, k] for k in range(9)]))

    apply(start, other, initial=True)
    apply(other, out, earlier=start, even=True)
    fewest = jnp.minimum(meta[4], meta[5])
    most = jnp.maximum(meta[4], meta[5])
    plain = (fewest - 2) // 2
    pairs = (most - 1) // 2

    def free_pair(pair, carry):
        apply(out, other)
        apply(other, out, even=True)
        return carry

    def held_pair(pair, carry):
        apply(out, other)
        apply(other, out, even=True, step=2 * pair + 4)
        return carry

    lax.fori_loop(0, plain, free_pair, 0)
    lax.fori_loop(plain, pairs, held_pair, 0)

    def squares(x, sums):
        return tuple(sums[k] + out[x, k] * out[x, k] for k in range(9))

    sums = lax.fori_loop(0, FRAG, squares, (jnp.zeros((8, 128), F32),) * 9)
    sums = sum(sums[1:], sums[0])
    sums = jnp.sum(sums, axis=0, keepdims=True)
    sums = jnp.broadcast_to(sums, (8, 128))
    for step in (16, 32, 64):
        sums = sums + rolled(sums, step)
    scale = jnp.sqrt(float(FRAG**3) / (sums + 1e-06))
    scale_out[...] = scale
    weight = jnp.where(second, meta[3], meta[2]).astype(F32) / NORB

    def clear(row, carry):
        for frag in range(2):
            spilled[frag, pl.ds(pl.multiple_of(row * FRAG, 8), FRAG), :] = jnp.zeros((FRAG, 128), F32)
        return carry

    lax.fori_loop(0, 40, clear, 0)
    for part in range(3):
        for k in range(9):
            values = []
            for x in range(8):
                value = out[8 * part + x, k] * scale
                values.append(value * value)
            turned.at[part][pl.ds(k // 3 * FRAG + k % 3, 8, stride=3), :] = gather_sums(values, lane) * weight
    for part in range(3):
        rows = turned[part].T
        for yc in range(8):
            for frag in range(2):
                piece = rows[(2 * yc + frag) * 8 : (2 * yc + frag) * 8 + 8]
                base = (meta[frag] + 8 * part) * FRAG + 3 * yc
                for yi in range(3):
                    spilled[frag, pl.ds(base + yi, 8, stride=FRAG), :] = rolled(piece, -FRAG * yi)
    slot_of = slots_of(FRAG)
    for down in range(3):
        groups = 8 if down < 2 else 4

        def share(number, carry, down=down, groups=groups):
            totals = []
            for part in range(4):
                total = None
                for slot in range(4):
                    row = 16 * down + 4 * number + part + groups * (slot // 2)
                    piece = spilled[slot % 2, pl.ds(pl.multiple_of(row * FRAG, 8), FRAG), :]
                    piece = rolled(piece, 32 * slot)
                    total = piece if total is None else jnp.where(slot_of == slot, piece, total)
                totals.append(total)
            for part in range(4):
                shares[down][4 * number + part] = totals[part]
            return carry

        lax.fori_loop(0, groups // 4, share, 0)


def add_windows(places, grid, along, shares):
    lane = lanes(FRAG)
    for down in range(3):
        groups = 8 if down < 2 else 4
        k = 2 * down + along

        def add(number, carry, k=k, down=down, groups=groups):
            pieces = []
            for part in range(4):
                group = 4 * number + part
                both = shares[0][8 * down + group] if along else shares[down][group]
                for slot in range(4):
                    depth = places[6 * k + 3 * (slot % 2) + 2]
                    pieces.append(pltpu.roll(both, (256 + depth - 32 * slot) & 127, 1))
            for part in range(4):
                for slot in range(4):
                    frag = slot % 2
                    row = 4 * number + part + groups * (slot // 2)
                    col, depth = places[6 * k + 3 * frag + 1], places[6 * k + 3 * frag + 2]
                    piece = jnp.where(((lane - depth) & 127) < FRAG, pieces[4 * part + slot], 0.0)
                    cols = pl.ds(32 + col - 32 * along, FRAG)
                    grid[0, row, cols, :] += jnp.where(lane >= depth, piece, 0.0)
                    grid[1, row, cols, :] += jnp.where(lane >= depth, 0.0, piece)
            return carry

        lax.fori_loop(0, groups // 4, add, 0)


def patch_owned(places, first, second, third, out, grid):
    def clear(row, carry):
        for half in range(2):
            grid[half, row] = jnp.zeros((PADDED, 128), F32)
        return carry

    lax.fori_loop(0, ROWS, clear, 0)
    add_windows(places, grid, 0, (first, second, third))
    for half in range(2):
        out[:, :, half * 128 : half * 128 + 128] = grid[half, :, 32 : 32 + COLS]


def patch_beside(places, owned, beside, out, grid):
    fill_grid(grid, owned[...])
    add_windows(places, grid, 1, (beside,))
    for half in range(2):
        out[:, :, half * 128 : half * 128 + 128] = grid[half, :, 32 : 32 + COLS]


def moved(x, down, along):
    pairs = [
        (p * NPY + q, (p + down) * NPY + q + along)
        for p in range(NPX)
        for q in range(NPY)
        if 0 <= p + down < NPX and 0 <= q + along < NPY
    ]
    return lax.ppermute(x, ALL, pairs)


def body(density, external, orbitals, anchors, weights, degrees):
    row_place = lax.axis_index(PX)
    col_place = lax.axis_index("py")
    origin = jnp.stack([row_place * ROWS, col_place * COLS, 0])
    local = (anchors - origin[None, :]).astype(jnp.int32)
    own = jnp.pad(local.reshape(6), (0, 2))
    above = jnp.stack([own, moved(own, 1, 0), moved(own, 2, 0)])
    meta = jnp.concatenate([local[:, 0], weights, degrees, weights]).astype(jnp.int32)

    sine_y = [jnp.asarray(t) for t in SINE_Y]
    sine_z = jnp.asarray(SINE_Z)
    ey = jnp.asarray(EIGEN_Y)
    ez = lax.dynamic_slice(jnp.asarray(EIGEN_Z), (col_place * KZ, 0), (KZ, 1))
    ez, above = lax.optimization_barrier((ez, above))
    places = jnp.stack([above, moved(above, 0, 1)], 1)[:, :, :6].reshape(36)

    planes = call(
        orbitals_in,
        shape(FRAG, 9, 8, 128),
        [pltpu.VMEM((2, 5, NORB * FRAG, 128), F32), pltpu.VMEM((3, 128, 128), F32)],
    )(orbitals.reshape(2, NORB * FRAG, FRAG * FRAG))
    power, weight, ends = call(
        scan_powers,
        (shape(5, KZ, NY), shape(5, KZ, NY), shape(2, KZ, NY)),
        smem=(0,),
        count=3,
    )(row_place.reshape(1).astype(jnp.int32), ey, ez)

    tiles = call(forward_z, shape(NPY, KZ, ROWS * COLS), count=2)(density, sine_z)
    tiles = lax.all_to_all(tiles, "py", split_axis=0, concat_axis=0, tiled=True)
    field, totals = call(
        forward_y,
        (shape(ROWS * KZ, NY), shape(2 * KZ, NY)),
        [pltpu.VMEM((ROWS * KZ, NY), F32)],
        count=5,
    )(tiles, *sine_y, ey, ez)

    right, left = jnp.zeros((KZ, NY), F32), jnp.zeros((KZ, NY), F32)
    for bit, partner in enumerate((1, 2, 4, 8, 24)):
        pairs = [(p * NPY + q, (p ^ partner) * NPY + q) for p in range(NPX) for q in range(NPY)]
        got = lax.ppermute(totals, ALL, pairs)
        upper = (row_place >> bit) % 2 == 1
        high, low = jnp.where(upper, totals, got), jnp.where(upper, got, totals)
        right = right + jnp.where(upper, weight[bit] * got[:KZ], 0.0)
        left = left + jnp.where(upper, 0.0, weight[bit] * got[KZ:])
        totals = jnp.concatenate([high[:KZ] + power[bit] * low[:KZ], low[KZ:] + power[bit] * high[KZ:]])

    tiles = call(back_y, shape(NPY, KZ, ROWS * COLS), [pltpu.VMEM((ROWS * KZ, NY), F32)], count=9)(
        field, totals, right, left, ends, *sine_y, ey, ez
    )
    tiles = lax.all_to_all(tiles, "py", split_axis=0, concat_axis=0, tiled=True)
    groups = (8, 8, 4)
    grid = [pltpu.VMEM((2, ROWS, PADDED, 128), F32)]
    hartree_field, beside = call(
        back_z, [shape(ROWS, COLS, NZ), shape(20, FRAG, 128)], grid, smem=(0,), count=4
    )(places, tiles, external, sine_z)
    owned = call(cut_owned, [shape(n, FRAG, 128) for n in groups], grid, smem=(0,), count=3)(
        places, hartree_field, external
    )
    beside = moved(beside, 0, -1)
    next_rows = moved(owned[1] + beside[8:16], -1, 0)
    last_rows = moved(owned[2] + beside[16:], -2, 0)
    planes, scale, *shares = call(
        filter_fragments,
        [shape(FRAG, 9, 8, 128), shape(8, 128)] + [shape(n, FRAG, 128) for n in groups],
        [
            pltpu.VMEM((2, 40 * FRAG, 128), F32),
            pltpu.VMEM((3, 128, 128), F32),
            pltpu.VMEM((27, 8, 128), F32),
            pltpu.VMEM((FRAG, 9, 8, 128), F32),
            pltpu.VMEM((FRAG, 9, 8, 128), F32),
            pltpu.VMEM((2, 40 * FRAG, 128), F32),
        ],
        smem=(0,),
        count=6,
    )(meta, owned[0], beside, next_rows, last_rows, planes)
    received = [shares[0], moved(shares[1], 1, 0), moved(shares[2], 2, 0)]
    beside = moved(jnp.concatenate(received), 0, 1)
    filtered = call(
        orbitals_out,
        shape(2, NORB * FRAG, FRAG * FRAG),
        [pltpu.VMEM((2, 5, NORB * FRAG, 128), F32), pltpu.VMEM((3, 128, 128), F32)],
        count=2,
    )(planes, scale)
    density_owned = call(patch_owned, shape(ROWS, COLS, NZ), grid, smem=(0,), count=4)(places, *received)
    new_density = call(patch_beside, shape(ROWS, COLS, NZ), grid, smem=(0,), count=3)(
        places, density_owned, beside
    )
    return hartree_field, filtered.reshape(orbitals.shape), new_density


def solution(mesh):
    torus = Mesh(mesh.devices.reshape(8, 2, 2, NPY), ALL)
    grid = P(PX, "py", None)
    return jax.shard_map(
        body,
        mesh=torus,
        in_specs=(grid, grid, P(ALL, None, None, None), P(ALL, None), P(ALL), P(ALL)),
        out_specs=(grid, P(ALL, None, None, None), grid),
        check_vma=False,
    )
```
